128 devices in a mesh: row: 8 (over z, x_lo), col: 16 (over x_hi, y, core).
Axes of the slice: x: 4 (x_hi: 2, x_lo: 2; x = x_hi * 2 + x_lo), y: 4, z: 4, core: 2. Of those that a mesh axis runs over, the one named last changes fastest.
Arguments:
- positions: float32 [3, 16, 16, 16, 128], P(None, 'row', 'col'), may hold values from 0.5 to 7.5
- torques: float32 [3, 16, 16, 16, 128], P(None, 'row', 'col'), may hold values from -6 to 6
- counts: int32 [16, 16, 16], P('row', 'col'), may hold values from 42 to 128
- neighbour_flags: int32 [6, 16, 16, 16], P(None, 'row', 'col'), may hold values 0 or 1
Outputs:
- moved_positions: float32 [3, 16, 16, 16, 128], P(None, 'row', 'col')
- spin: float32 [3, 16, 16, 16, 128], P(None, 'row', 'col')
The draws below stay inside these ranges and needn't reach their ends.
Inputs may be any that keep to these rules, and one draw needn't show every extreme that they name: `counts`: number of occupied slots of each cell block; slots at or past it hold no particle. `neighbour_flags`: entry f of a block is 1 where its neighbour at the f-th face offset (+x, -x, +y, -y, +z, -z) acts on it, else 0.
All inputs are finite; a program needn't handle non-finite values.
Results may differ from the reference program's by a relative error of at most 0.0003.
Values sent between devices are 32-bit elements; how exact they have to be, the bound alone decides.
A program may use at most 64 MiB of HBM per device.

```python
import math
import jax
import jax.numpy as jnp
from jax import lax

GRID = 128
CELL = 8
SLOT = 128
STEPS = 3
NCELL = 16


def touch_ends(values, stream_key, low, largest):
    extent = values.shape
    spot = [jax.random.randint(jax.random.fold_in(stream_key, axis), (), 0, extent[axis]) for axis in range(len(extent))]
    values = values.at[tuple(spot)].set(low)
    longest = extent.index(max(extent))
    spot[longest] = (spot[longest] + 1) % extent[longest]
    return values.at[tuple(spot)].set(largest)


def levels(rng, extent, pieces, least, high):
    def one(axis_at, parts):
        draws = jax.random.uniform(jax.random.fold_in(jax.random.fold_in(rng, 6), axis_at), (parts,), jnp.float32, least / len(pieces), high / len(pieces))
        return jnp.repeat(jnp.exp(draws), extent[axis_at] // parts).reshape((-1,) + (1,) * (len(extent) - axis_at - 1))

    factor_of = one(*pieces[0])
    for cut in pieces[1:]:
        factor_of = factor_of * one(*cut)
    return factor_of


def gaussian(own_key, shape, scale, limit, split=(), kind=jnp.bfloat16):
    level = levels(own_key, shape, split, -0.22, 0.18) if split else 1.0
    values = jax.random.normal(own_key, shape, jnp.float32) * scale * level
    return jnp.minimum(jnp.maximum(values, -limit), limit).astype(kind)


def setup_inputs(seed: int = 0) -> dict:
    keys = jax.random.split(jax.random.key(seed), 5)
    positions = jnp.clip(0.5 + 7.0 * jax.random.uniform(keys[0], (3, NCELL, NCELL, NCELL, SLOT), jnp.float32) ** levels(keys[0], (3, NCELL, NCELL, NCELL, SLOT), ((1, 8), (2, 16)), -0.2, 0.2), 0.5, 7.5)
    torques = gaussian(keys[1], (3, NCELL, NCELL, NCELL, SLOT), 1.0, 6.0, ((1, 8), (2, 16)), jnp.float32)
    counts = touch_ends(jax.random.randint(keys[2], (NCELL, NCELL, NCELL), SLOT // 3, SLOT + 1), jax.random.fold_in(keys[2], 1), SLOT // 3, SLOT).astype(jnp.int32)
    neighbour_flags = touch_ends((jax.random.randint(keys[3], (6, NCELL, NCELL, NCELL), 0, 4) < 3).astype(jnp.int32), jax.random.fold_in(keys[3], 1), 0, 1)
    return {"positions": positions, "torques": torques, "counts": counts, "neighbour_flags": neighbour_flags}


highest = lax.Precision.HIGHEST
step_pace = 0.06
drift_gain = 1.0
couple_gain = 0.5
bin_rate = 1.0
face_moves = ((0, 1.0), (0, -1.0), (1, 1.0), (1, -1.0), (2, 1.0), (2, -1.0))


def cross_product(left_vec, right_vec):
    return jnp.stack([left_vec[1] * right_vec[2] - left_vec[2] * right_vec[1],
                      left_vec[2] * right_vec[0] - left_vec[0] * right_vec[2],
                      left_vec[0] * right_vec[1] - left_vec[1] * right_vec[0]])


def make_loads(places, torque, filled):
    return jnp.concatenate([torque * filled, cross_product(torque, places) * filled, filled[None]], 0)


def pair_totals(near_places, far_places, far_loads, offset_vec):
    separation = near_places[:, :, :, None] - far_places[:, :, None, :] - offset_vec[:, None, None, None]
    weights = jnp.exp(-jnp.sum(separation * separation, axis=0) * (2.0 / (CELL * CELL)))
    return jnp.einsum('nij,qnj->qni', weights, far_loads, precision=highest)


def to_slabs(values):
    return jnp.moveaxis(values, 1, 0).reshape(NCELL, values.shape[0], NCELL * NCELL, SLOT)


def slab_totals(places, far_places, far_loads, offset_vec):
    def one_slab(members):
        return pair_totals(members[0], members[1], members[2], offset_vec)
    result = lax.map(one_slab, (to_slabs(places), to_slabs(far_places), to_slabs(far_loads)))
    return jnp.moveaxis(result.reshape(NCELL, 7, NCELL, NCELL, SLOT), 0, 1)


def near_field(places, torque, filled, face_flags):
    loads = make_loads(places, torque, filled)
    drives = jnp.zeros(places.shape, jnp.float32)
    twists = jnp.zeros(places.shape, jnp.float32)
    weight_total = jnp.zeros(places.shape[1:], jnp.float32)
    for face_id in range(7):
        if face_id == 0:
            far_places, far_loads = places, loads
            offset_vec = jnp.zeros((3,), jnp.float32)
            face_gate = jnp.ones(places.shape[1:4] + (1,), jnp.float32)
        else:
            axis_id, face_sign = face_moves[face_id - 1]
            far_places = jnp.roll(places, -int(face_sign), axis=axis_id + 1)
            far_loads = jnp.roll(loads, -int(face_sign), axis=axis_id + 1)
            offset_vec = jnp.zeros((3,), jnp.float32).at[axis_id].set(face_sign * CELL)
            face_gate = face_flags[face_id - 1].astype(jnp.float32)[..., None]
        totals = slab_totals(places, far_places, far_loads, offset_vec)
        lever = places - offset_vec[:, None, None, None, None]
        drives = drives + face_gate * (cross_product(totals[0:3], lever) - totals[3:6])
        twists = twists + face_gate * totals[0:3]
        weight_total = weight_total + face_gate * totals[6]
    velocity = (drift_gain / SLOT) * drives * filled
    spin_near = (torque + (couple_gain / SLOT) * (twists - weight_total * torque)) * filled
    return velocity, spin_near


def bin_weights(coordinate):
    centres = jnp.arange(CELL, dtype=jnp.float32) + 0.5
    separation = coordinate[..., None] - centres
    return jnp.exp(-separation * separation * bin_rate)


def signed_wave(values):
    return jnp.where(values < GRID // 2, values, values - GRID).astype(jnp.float32)


def stokes(spectrum, wave_x, wave_y, wave_z):
    wave_square = wave_x * wave_x + wave_y * wave_y + wave_z * wave_z
    damping = 0.25 * jnp.exp(-wave_square * (math.pi / GRID) ** 2)
    along = (wave_x * spectrum[0] + wave_y * spectrum[1] + wave_z * spectrum[2]) / jnp.maximum(wave_square, 1.0)
    return jnp.stack([damping * (spectrum[0] - wave_x * along),
                      damping * (spectrum[1] - wave_y * along),
                      damping * (spectrum[2] - wave_z * along)])


def far_field(places, torque, filled):
    place_slabs = to_slabs(places)
    load_slabs = to_slabs(torque * filled)

    def spread_slab(members):
        flat_places, loads = members
        weight_x = bin_weights(flat_places[0])
        weight_y = bin_weights(flat_places[1])
        weight_z = bin_weights(flat_places[2])
        planar = weight_x[:, :, :, None] * weight_y[:, :, None, :]
        lifted = loads[:, :, :, None] * weight_z[None]
        return jnp.einsum('niab,qnic->qnabc', planar, lifted, precision=highest)

    cubes = lax.map(spread_slab, (place_slabs, load_slabs))
    grid_field = cubes.reshape(NCELL, 3, NCELL, NCELL, CELL, CELL, CELL).transpose(1, 0, 4, 2, 5, 3, 6).reshape(3, GRID, GRID, GRID)
    spectrum = jnp.fft.fftn(grid_field, axes=(1, 2, 3))
    waves = signed_wave(jnp.arange(GRID, dtype=jnp.int32))
    spectrum = stokes(spectrum, waves[:, None, None], waves[None, :, None], waves[None, None, :])
    far_grid = jnp.real(jnp.fft.ifftn(spectrum, axes=(1, 2, 3)))
    cubes = far_grid.reshape(3, NCELL, CELL, NCELL, CELL, NCELL, CELL).transpose(1, 0, 3, 5, 2, 4, 6).reshape(NCELL, 3, NCELL * NCELL, CELL, CELL, CELL)

    def gather_slab(members):
        cube_slab, flat_places = members
        weight_x = bin_weights(flat_places[0])
        weight_y = bin_weights(flat_places[1])
        weight_z = bin_weights(flat_places[2])
        planar = weight_x[:, :, :, None] * weight_y[:, :, None, :]
        partial_sum = jnp.einsum('qnabc,niab->qnic', cube_slab, planar, precision=highest)
        return jnp.sum(partial_sum * weight_z[None], axis=3)

    result = lax.map(gather_slab, (cubes, place_slabs))
    return jnp.moveaxis(result.reshape(NCELL, 3, NCELL, NCELL, SLOT), 0, 1)


def reference(positions, torques, counts, neighbour_flags):
    filled = (jnp.arange(SLOT, dtype=jnp.int32) < counts[..., None]).astype(jnp.float32)
    places = positions
    spin_near = jnp.zeros(positions.shape, jnp.float32)
    for step_id in range(STEPS):
        velocity, spin_near = near_field(places, torques, filled, neighbour_flags)
        places = places + (step_pace * CELL) * velocity
    far_spin = far_field(places, torques, filled)
    return places, spin_near + far_spin * filled
```

```python
import math

import jax
import jax.numpy as jnp
import numpy as np
from jax import lax
from jax.experimental import pallas as pl
from jax.experimental.pallas import tpu as pltpu
from jax.sharding import PartitionSpec as P

GRID = 128
CELL = 8
SLOT = 128
STEPS = 3
ROWS = 8
COLS = 16
DEVICES = ROWS * COLS
CELLS = 32
HALF = 16
MESH = pl.DeviceIdType.MESH
F32 = jnp.float32
BF16 = jnp.bfloat16

KAPPA = 2.0 / (CELL * CELL) * math.log2(math.e)
PACE = 0.06 * CELL
DRIFT = 1.0 / SLOT
COUPLE = 0.5 / SLOT
MID = 0.5 * CELL

A_ROWS = 48
B_ROWS = 16
L_ROWS = 16


def narrow(v):
    return v.astype(BF16).astype(F32)


def split3(v):
    h = narrow(v)
    r = v - h
    m = narrow(r)
    return h, m, r - m


def put(ref, lead, start, stride, val):
    ref[lead, pl.ds(start, val.shape[0], stride=stride), :] = val


def put_receiver(afeat, half, px, py, pz):
    base = half * HALF * A_ROWS

    def row(k, v):
        afeat[pl.ds(base + k, HALF, stride=A_ROWS), :] = v

    parts = [split3(v * (2.0 * KAPPA)) for v in (px, py, pz)]
    size = split3(-KAPPA * (px * px + py * py + pz * pz))
    for d in range(3):
        h, m, l = parts[d]
        row(d, h)
        row(8 + d, h)
        row(11 + d, h)
        row(16 + d, m)
        row(24 + d, m)
        row(32 + d, l)
    row(6, size[0])
    row(16 + 6, size[1])
    row(32 + 6, size[2])


def put_source(bfeat, lfeat, slot, half, place, torque, fill, shift, gate):
    place = [place[d] + shift[d] if shift[d] != 0.0 else place[d] for d in range(3)]
    x, y, z = place
    base = half * HALF * B_ROWS
    for d in range(3):
        h, m, l = split3(place[d])
        put(bfeat, slot, base + d, B_ROWS, h)
        put(bfeat, slot, base + 8 + d, B_ROWS, m)
        put(bfeat, slot, base + 11 + d, B_ROWS, l)
    for k, v in enumerate(split3(-KAPPA * (x * x + y * y + z * z))):
        put(bfeat, slot, base + 3 + k, B_ROWS, v)
    if gate is not None:
        torque = [t * gate for t in torque]
        fill = fill * gate
    tx, ty, tz = torque
    loads = (tx, ty, tz, ty * z - tz * y, tz * x - tx * z, tx * y - ty * x)
    base = half * HALF * L_ROWS
    for q, v in enumerate(loads):
        h = narrow(v)
        put(lfeat, slot, base + q, L_ROWS, h)
        put(lfeat, slot, base + 8 + q, L_ROWS, v - h)
    put(lfeat, slot, base + 6, L_ROWS, fill)


def near_kernel(
    pos_in, tor_in, cnt, flg, pos_out, near_out, fill_out,
    state, places, gates, afeat, trans, bfeat, lfeat, totals,
    full_x, full_y, part_x, part_y, send_sem, recv_sem,
):
    row = lax.axis_index("row")
    col = lax.axis_index("col")
    peers = (
        (lax.rem(row + 1, ROWS), col),
        (lax.rem(row + ROWS - 1, ROWS), col),
        (row, lax.rem(col + 1, COLS)),
        (row, lax.rem(col + COLS - 1, COLS)),
    )
    barrier = pltpu.get_barrier_semaphore()
    for peer in peers:
        pl.semaphore_signal(barrier, inc=1, device_id=peer, device_id_type=MESH)

    lane = lax.broadcasted_iota(jnp.int32, (1, SLOT), 1)

    def spread_scalars(z, carry):
        for h in range(2):
            state[6, pl.ds(h * HALF + z, 1), :] = (lane < cnt[h, 0, z]).astype(F32)
            for f in range(6):
                gates[f, pl.ds(h * HALF + z, 1), :] = jnp.full((1, SLOT), flg[f, h, 0, z], jnp.int32).astype(F32)
        return carry

    lax.fori_loop(0, HALF, spread_scalars, 0)
    fill = state[6]
    fill_out[...] = fill
    for d in range(3):
        state[d] = pos_in[d] - MID
        state[3 + d] = tor_in[d] * fill

    pl.semaphore_wait(barrier, 4)

    def halo(step):
        if step == 0:
            own, into_x, into_y = state, full_x, full_y
        else:
            own, into_x, into_y = places.at[step - 1], part_x.at[step - 1], part_y.at[step - 1]
        moves = (
            (own.at[:, pl.ds(HALF, HALF), :], into_x.at[0], 0),
            (own.at[:, pl.ds(0, HALF), :], into_x.at[1], 1),
            (own, into_y.at[0], 2),
            (own, into_y.at[1], 3),
        )
        copies = []
        for src, dst, k in moves:
            copies.append(
                pltpu.make_async_remote_copy(
                    src_ref=src,
                    dst_ref=dst,
                    send_sem=send_sem.at[step, k],
                    recv_sem=recv_sem.at[step, k],
                    device_id=peers[k],
                    device_id_type=MESH,
                )
            )
        return copies

    one = jnp.ones((CELLS, SLOT), F32)
    zero = jnp.zeros((CELLS, SLOT), F32)
    for k in (7, 14, 15, 19, 20, 21, 23, 27, 28, 29, 30, 31, 35, 36, 37, 39, *range(40, 48)):
        afeat[pl.ds(k, CELLS, stride=A_ROWS), :] = zero
    for k in (3, 4, 5):
        afeat[pl.ds(k, CELLS, stride=A_ROWS), :] = one
    for e in range(7):
        put(bfeat, e, 6, B_ROWS, one)
        for k in (7, 14, 15):
            put(bfeat, e, k, B_ROWS, zero)
        for k in (7, 14, 15):
            put(lfeat, e, k, L_ROWS, zero)

    def weighted(at, cell, faces):
        def wide(ref, n):
            blocks = [ref[e, pl.ds(pl.multiple_of(cell * n, n), n), :] for e in faces]
            return (blocks[0] if len(blocks) == 1 else jnp.concatenate(blocks, 1)).astype(BF16)

        b = wide(bfeat, B_ROWS)
        b = jnp.concatenate([b, b, b], 0)
        power = jnp.dot(at, b, preferred_element_type=F32)
        w = jnp.exp2(power).astype(BF16)
        return lax.dot_general(wide(lfeat, L_ROWS), w, (((1,), (1,)), ((), ())), preferred_element_type=F32)

    def inner_faces(z, carry):
        for h in range(2):
            cell = h * HALF + z
            at = afeat[pl.ds(pl.multiple_of(cell * A_ROWS, A_ROWS), A_ROWS), :].T.astype(BF16)
            trans[cell] = at
            acc = weighted(at, cell, (0, 1)) + weighted(at, cell, (2, 3))
            totals[pl.ds(pl.multiple_of(cell * 8, 8), 8), :] = acc[0:8] + acc[8:16]
        return carry

    def outer_faces(z, carry):
        for h in range(2):
            cell = h * HALF + z
            at = trans[cell]
            acc = weighted(at, cell, (4, 5)) + weighted(at, cell, (6,))
            spot = pl.ds(pl.multiple_of(cell * 8, 8), 8)
            totals[spot, :] = totals[spot, :] + (acc[0:8] + acc[8:16])
        return carry

    for step in range(STEPS):
        copies = halo(step)
        for copy in copies:
            copy.start()
        here = state if step == 0 else places.at[step - 1]
        for h in range(2):
            part = slice(h * HALF, (h + 1) * HALF)
            other = slice((1 - h) * HALF, (2 - h) * HALF)
            place = [here[d, part, :] for d in range(3)]
            torque = [state[3 + d, part, :] for d in range(3)]
            fill = state[6, part, :]
            put_receiver(afeat, h, *place)
            put_source(bfeat, lfeat, 0, h, place, torque, fill, (0.0, 0.0, 0.0), None)
            for slot, turn, lift, face in ((1, HALF - 1, CELL, 4), (2, 1, -CELL, 5)):
                def turned(v):
                    return pltpu.roll(v, turn, 0)

                put_source(
                    bfeat, lfeat, slot, h, [turned(v) for v in place], [turned(v) for v in torque], turned(fill),
                    (0.0, 0.0, float(lift)), gates[face, part, :],
                )
            put_source(
                bfeat, lfeat, 3, h,
                [here[d, other, :] for d in range(3)],
                [state[3 + d, other, :] for d in range(3)],
                state[6, other, :],
                (float(CELL) if h == 0 else -float(CELL), 0.0, 0.0),
                gates[0 if h == 0 else 1, part, :],
            )
        lax.fori_loop(0, HALF, inner_faces, 0)
        for copy in copies:
            copy.wait_recv()
        for h in range(2):
            part = slice(h * HALF, (h + 1) * HALF)
            near_x = full_x if step == 0 else part_x.at[step - 1]
            near_y = full_y if step == 0 else part_y.at[step - 1]
            put_source(
                bfeat, lfeat, 4, h,
                [near_x[h, d] for d in range(3)],
                [full_x[h, 3 + d] for d in range(3)],
                full_x[h, 6],
                (-float(CELL) if h == 0 else float(CELL), 0.0, 0.0),
                gates[1 if h == 0 else 0, part, :],
            )
            for slot, side, lift, face in ((5, 1, CELL, 2), (6, 0, -CELL, 3)):
                put_source(
                    bfeat, lfeat, slot, h,
                    [near_y[side, d, part, :] for d in range(3)],
                    [full_y[side, 3 + d, part, :] for d in range(3)],
                    full_y[side, 6, part, :],
                    (0.0, float(lift), 0.0),
                    gates[face, part, :],
                )
        lax.fori_loop(0, HALF, outer_faces, 0)

        tot = [totals[pl.ds(q, CELLS, stride=8), :] for q in range(7)]
        fill = state[6]
        x, y, z = (here[d] for d in range(3))
        speed = (
            tot[1] * z - tot[2] * y - tot[3],
            tot[2] * x - tot[0] * z - tot[4],
            tot[0] * y - tot[1] * x - tot[5],
        )
        for d in range(3):
            moved = here[d] + PACE * (DRIFT * speed[d] * fill)
            if step < STEPS - 1:
                places[step, d] = moved
            else:
                pos_out[d] = moved + MID
                torque = tor_in[d]
                near_out[d] = (torque + COUPLE * (tot[d] - tot[6] * torque)) * fill

    for step in range(STEPS):
        for copy in halo(step):
            copy.wait_send()


def near_field(positions, torques, counts, flags):
    vmem = pl.BlockSpec(memory_space=pltpu.VMEM)
    smem = pl.BlockSpec(memory_space=pltpu.SMEM)
    field = jax.ShapeDtypeStruct((3, CELLS, SLOT), F32)
    return pl.pallas_call(
        near_kernel,
        name="near",
        out_shape=(field, field, jax.ShapeDtypeStruct((CELLS, SLOT), F32)),
        in_specs=[vmem, vmem, smem, smem],
        out_specs=(vmem, vmem, vmem),
        scratch_shapes=[
            pltpu.VMEM((7, CELLS, SLOT), F32),
            pltpu.VMEM((STEPS - 1, 3, CELLS, SLOT), F32),
            pltpu.VMEM((6, CELLS, SLOT), F32),
            pltpu.VMEM((CELLS * A_ROWS, SLOT), F32),
            pltpu.VMEM((CELLS, SLOT, A_ROWS), BF16),
            pltpu.VMEM((7, CELLS * B_ROWS, SLOT), F32),
            pltpu.VMEM((7, CELLS * L_ROWS, SLOT), F32),
            pltpu.VMEM((CELLS * 8, SLOT), F32),
            pltpu.VMEM((2, 7, HALF, SLOT), F32),
            pltpu.VMEM((2, 7, CELLS, SLOT), F32),
            pltpu.VMEM((STEPS - 1, 2, 3, HALF, SLOT), F32),
            pltpu.VMEM((STEPS - 1, 2, 3, CELLS, SLOT), F32),
            pltpu.SemaphoreType.DMA((STEPS, 4)),
            pltpu.SemaphoreType.DMA((STEPS, 4)),
        ],
        compiler_params=pltpu.CompilerParams(collective_id=0, has_side_effects=True),
    )(positions, torques, counts, flags)


def halves(table):
    high = table.astype(np.float32).astype(jnp.bfloat16)
    low = (table - high.astype(np.float64)).astype(np.float32).astype(jnp.bfloat16)
    return high, low


def make_tables():
    n = np.arange(GRID)
    level = np.where(n == 1, 64, n // 2)
    angle = 2.0 * np.pi * (level[:, None] * n[None, :] % GRID) / GRID
    cosine, sine = np.cos(angle), np.sin(angle)
    even = (n % 2 == 0)[:, None]
    whole = (n < 2)[:, None]
    basis_xy = np.where(whole | even, cosine, sine)
    basis_z = np.where(whole | ~even, cosine, sine)
    count = np.where(n < 2, 1.0, 2.0)[:, None]
    back_xy, back_z = (basis_xy * count).T, (basis_z * count).T

    def wave(a, b, period_a, period_b):
        return 2.0 * np.pi * ((a * b[0] % period_a) / period_a + (b[1] % period_b) / period_b)

    r, q = n // 16, n % 16
    turn_l = 2.0 * np.pi * ((r[:, None] * r[None, :] % 8) / 8 + (q[:, None] * q[None, :] % 16) / 16)
    s, t = n // 8, n % 8
    turn_r = 2.0 * np.pi * ((s[:, None] * s[None, :] % 16) / 16 + (t[:, None] * t[None, :] % 8) / 8)
    twist = 2.0 * np.pi * (r[:, None] * s[None, :] + q[:, None] * t[None, :]) / GRID
    cl, sl = np.cos(turn_l), np.sin(turn_l)
    cr, sr = np.cos(turn_r), np.sin(turn_r)
    left = np.concatenate([cl, -sl], 0)
    left_back = np.concatenate([cl, -sl], 1)
    right = np.block([[cr, -sr], [sr, cr]])
    right_back = np.block([[cr, sr], [-sr, cr]])
    out = []
    for table in (basis_xy, basis_z, back_xy, back_z, left, left_back, right, right_back):
        high, low = halves(table)
        out += [high, low]
    out.append(np.stack([np.cos(twist), np.sin(twist)]).astype(np.float32))
    return out


def cut(v):
    h = v.astype(BF16)
    return h, (v - h.astype(F32)).astype(BF16)


def mul(a, b):
    return jnp.dot(a, b, preferred_element_type=F32)


def mul_t(a, b):
    return lax.dot_general(a, b, (((1,), (1,)), ((), ())), preferred_element_type=F32)


def table_left(high, low, v):
    vh, vl = cut(v)
    return mul(high, vh) + (mul(low, vh) + mul(high, vl))


def table_right(v, high, low):
    vh, vl = cut(v)
    return mul(vh, high) + (mul(vl, high) + mul(vh, low))


def far_kernel(
    pos, tor, near, fill, zf_xy_h, zf_xy_l, zf_z_h, zf_z_l, zb_xy_h, zb_xy_l, zb_z_h, zb_z_l,
    lf_h, lf_l, lb_h, lb_l, rf_h, rf_l, rb_h, rb_l, twist,
    spin,
    grid, plan_h, plan_l, depth, out_1, in_1, out_2, in_2, work, far, send_sem, recv_sem, self_sem,
):
    row = lax.axis_index("row")
    col = lax.axis_index("col")
    me = row * COLS + col
    barrier = pltpu.get_barrier_semaphore()

    def peer(k):
        p = lax.rem(me + k, DEVICES)
        return p, (p // COLS, lax.rem(p, COLS))

    def greet(k, carry):
        pl.semaphore_signal(barrier, inc=1, device_id=peer(k)[1], device_id_type=MESH)
        return carry

    lax.fori_loop(1, DEVICES, greet, 0)

    level = lax.broadcasted_iota(jnp.int32, (CELL, SLOT), 0).astype(F32) + 0.5
    low_lane = lax.broadcasted_iota(jnp.int32, (24, SLOT), 1) < 64

    def bins(d, cell):
        apart = pos[d, pl.ds(cell, 1), :] - level
        return jnp.exp(-apart * apart)

    def spread(z, carry):
        planar, lifted, rest = [], [], []
        for h in range(2):
            cell = h * HALF + z
            bx, by, bz = (bins(d, cell) for d in range(3))
            depth[pl.ds(pl.multiple_of(cell * 8, 8), 8), :] = bz
            planar += [bx[a : a + 1, :] * by for a in range(CELL)]
            lift = [tor[c, pl.ds(cell, 1), :] * fill[pl.ds(cell, 1), :] * bz for c in range(3)]
            top = [narrow(v) for v in lift]
            lifted += top
            rest += [v - t for v, t in zip(lift, top)]
        ph, pl_ = cut(jnp.concatenate(planar, 0))
        plan_h[z] = ph
        plan_l[z] = pl_
        both = mul_t(jnp.concatenate(lifted + rest, 0).astype(BF16), ph)
        more = mul_t(jnp.concatenate(lifted, 0).astype(BF16), pl_)
        sums = both[0:48] + both[48:96] + more
        block = jnp.where(low_lane, sums[0:24], sums[24:48])
        for c in range(3):
            grid[c, pl.ds(pl.multiple_of(z * 8, 8), 8), :] = block[c * 8 : c * 8 + 8]
        return carry

    lax.fori_loop(0, HALF, spread, 0)

    for c in range(3):
        high, low = (zf_xy_h, zf_xy_l) if c < 2 else (zf_z_h, zf_z_l)
        out_1[pl.ds(c, DEVICES, stride=8), :] = table_left(high[...], low[...], grid[c])

    pl.semaphore_wait(barrier, DEVICES - 1)

    def exchange(out, into, k):
        def post(i, carry):
            p, where = peer(i)
            pltpu.make_async_remote_copy(
                src_ref=out.at[pl.ds(pl.multiple_of(p * 8, 8), 3), :],
                dst_ref=into.at[pl.ds(pl.multiple_of(me * 8, 8), 3), :],
                send_sem=send_sem.at[k],
                recv_sem=recv_sem.at[k],
                device_id=where,
                device_id_type=MESH,
            ).start()
            return carry

        lax.fori_loop(1, DEVICES, post, 0)
        mine = pl.ds(pl.multiple_of(me * 8, 8), 3)
        keep = pltpu.make_async_copy(out.at[mine, :], into.at[mine, :], self_sem.at[k])
        keep.start()
        keep.wait()
        bulk = out.at[pl.ds(0, 3 * (DEVICES - 1)), :]
        pltpu.make_async_copy(bulk, bulk, recv_sem.at[k]).wait()

    exchange(out_1, in_1, 0)

    cos_t, sin_t = twist[0], twist[1]
    for c in range(3):
        both = table_left(lf_h[...], lf_l[...], in_1[pl.ds(c, DEVICES, stride=8), :])
        re, im = both[0:128], both[128:256]
        work[c, :, 0:128] = re * cos_t + im * sin_t
        work[c, :, 128:256] = im * cos_t - re * sin_t
    for c in range(3):
        work[c] = table_right(work[c], rf_h[...], rf_l[...])

    special = me < 2
    plain = jnp.where(special, 1.0, 0.0).astype(F32)
    turn = jnp.where(special, 0, 2 * lax.rem(me, 2) - 1).astype(F32)
    kz = jnp.where(me == 1, -64, me // 2).astype(F32)
    kz_top = jnp.where(me == 1, -64, 0).astype(F32)
    kz_low = jnp.where(me == 1, 0, me // 2).astype(F32)

    def signed(v):
        return jnp.where(v < GRID // 2, v, v - GRID)

    def stokes(i, carry):
        rows = pl.ds(pl.multiple_of(i * 16, 16), 16)
        f1 = lax.broadcasted_iota(jnp.int32, (16, 128), 0) + i * 16
        f2 = lax.broadcasted_iota(jnp.int32, (16, 128), 1)
        ix = signed(f1 // 16 + 8 * (f2 // 8))
        iy = signed(f1 % 16 + 16 * (f2 % 8))
        kx, ky = ix.astype(F32), iy.astype(F32)
        kx_top = jnp.where(ix == -64, kx, 0.0)
        ky_top = jnp.where(iy == -64, ky, 0.0)
        kx_low, ky_low = kx - kx_top, ky - ky_top
        square = kx * kx + ky * ky + kz * kz
        damping = (0.25 / GRID**3) * jnp.exp(square * (-((math.pi / GRID) ** 2)))
        inverse = 1.0 / jnp.maximum(square, 1.0)
        w_re, w_im = work[2, rows, 0:128], work[2, rows, 128:256]
        sides = (
            (work[0, rows, 0:128], work[1, rows, 0:128], plain * w_re - turn * w_im),
            (work[0, rows, 128:256], work[1, rows, 128:256], plain * w_im + turn * w_re),
        )
        done = []
        for u, v, w in sides:
            low = (kx_low * u + ky_low * v + kz_low * w) * inverse
            top = (kx_top * u + ky_top * v + kz_top * w) * inverse
            done.append(
                (
                    damping * (u - kx_low * low - kx_top * top),
                    damping * (v - ky_low * low - ky_top * top),
                    damping * (w - kz_low * low - kz_top * top),
                )
            )
        for c in range(2):
            work[c, rows, 0:128] = done[0][c]
            work[c, rows, 128:256] = done[1][c]
        work[2, rows, 0:128] = plain * done[0][2] + turn * done[1][2]
        work[2, rows, 128:256] = plain * done[1][2] - turn * done[0][2]
        return carry

    lax.fori_loop(0, 8, stokes, 0)

    for c in range(3):
        both = table_right(work[c], rb_h[...], rb_l[...])
        re, im = both[:, 0:128], both[:, 128:256]
        pair = jnp.concatenate([re * cos_t - im * sin_t, im * cos_t + re * sin_t], 0)
        out_2[pl.ds(c, DEVICES, stride=8), :] = table_left(lb_h[...], lb_l[...], pair)

    exchange(out_2, in_2, 1)

    for c in range(3):
        high, low = (zb_xy_h, zb_xy_l) if c < 2 else (zb_z_h, zb_z_l)
        grid[c] = table_left(high[...], low[...], in_2[pl.ds(c, DEVICES, stride=8), :])

    def gather(z, carry):
        rows = pl.ds(pl.multiple_of(z * 8, 8), 8)
        block = jnp.concatenate([grid[c, rows, :] for c in range(3)], 0)
        near_half = jnp.where(low_lane, block, 0.0)
        far_half = block - near_half
        both = jnp.concatenate([near_half, far_half], 0)
        top = narrow(both)
        first = mul(jnp.concatenate([top, both - top], 0).astype(BF16), plan_h[z])
        second = mul(top.astype(BF16), plan_l[z])
        sums = first[0:48] + first[48:96] + second
        for h in range(2):
            spot = pl.ds(pl.multiple_of((h * HALF + z) * 8, 8), 8)
            bz = depth[spot, :]
            for c in range(3):
                far[c, spot, :] = sums[h * 24 + c * 8 : h * 24 + c * 8 + 8] * bz
        return carry

    lax.fori_loop(0, HALF, gather, 0)

    for c in range(3):
        total = far[c, pl.ds(0, CELLS, stride=8), :]
        for g in range(1, CELL):
            total = total + far[c, pl.ds(g, CELLS, stride=8), :]
        spin[c] = near[c] + total * fill[...]

    for k in range(2):
        bulk = out_1.at[pl.ds(0, 3 * (DEVICES - 1)), :]
        pltpu.make_async_copy(bulk, bulk, send_sem.at[k]).wait()


def far_field(places, torques, near, fill):
    tables = [jnp.asarray(t) for t in make_tables()]
    vmem = pl.BlockSpec(memory_space=pltpu.VMEM)
    buffer = pltpu.VMEM((DEVICES * 8, 128), F32)
    return pl.pallas_call(
        far_kernel,
        name="far",
        out_shape=jax.ShapeDtypeStruct((3, CELLS, SLOT), F32),
        in_specs=[vmem] * (4 + len(tables)),
        out_specs=vmem,
        scratch_shapes=[
            pltpu.VMEM((3, GRID, 128), F32),
            pltpu.VMEM((HALF, 128, SLOT), BF16),
            pltpu.VMEM((HALF, 128, SLOT), BF16),
            pltpu.VMEM((CELLS * 8, SLOT), F32),
            buffer,
            buffer,
            buffer,
            buffer,
            pltpu.VMEM((3, 128, 256), F32),
            pltpu.VMEM((3, CELLS * 8, SLOT), F32),
            pltpu.SemaphoreType.DMA((2,)),
            pltpu.SemaphoreType.DMA((2,)),
            pltpu.SemaphoreType.DMA((2,)),
        ],
        compiler_params=pltpu.CompilerParams(collective_id=1, has_side_effects=True),
    )(places, torques, near, fill, *tables)


def shards(positions, torques, counts, neighbour_flags):
    shape = positions.shape
    flat = (3, CELLS, SLOT)
    torques = torques.reshape(flat)
    places, near, fill = near_field(positions.reshape(flat), torques, counts, neighbour_flags)
    spin = far_field(places, torques, near, fill)
    return places.reshape(shape), spin.reshape(shape)


def solution(mesh):
    in_specs = (
        P(None, "row", "col", None, None),
        P(None, "row", "col", None, None),
        P("row", "col", None),
        P(None, "row", "col", None),
    )
    out_specs = (P(None, "row", "col", None, None), P(None, "row", "col", None, None))
    return jax.shard_map(shards, mesh=mesh, in_specs=in_specs, out_specs=out_specs, check_vma=False)
```

```python
import math

import jax
import jax.numpy as jnp
import numpy as np
from jax import lax
from jax.experimental import pallas as pl
from jax.experimental.pallas import tpu as pltpu
from jax.sharding import PartitionSpec as P

GRID = 128
CELL = 8
SLOT = 128
STEPS = 3
ROWS = 8
COLS = 16
DEVICES = ROWS * COLS
CELLS = 32
HALF = 16
MESH = pl.DeviceIdType.MESH
LOGICAL = pl.DeviceIdType.LOGICAL
F32 = jnp.float32
BF16 = jnp.bfloat16

KAPPA = 2.0 / (CELL * CELL) * math.log2(math.e)
PACE = 0.06 * CELL
DRIFT = 1.0 / SLOT
COUPLE = 0.5 / SLOT
MID = 0.5 * CELL

A_ROWS = 32
GROUP = SLOT // A_ROWS
B_ROWS = 16
L_ROWS = 16
A_PITCH = A_ROWS + 1
B_PITCH = B_ROWS + 1
L_PITCH = L_ROWS + 1
T_PITCH = 9


def narrow(v):
    return v.astype(BF16).astype(F32)


def split3(v):
    h = narrow(v)
    r = v - h
    m = narrow(r)
    return h, m, r - m


def put(ref, lead, start, stride, val):
    ref[lead, pl.ds(start, val.shape[0], stride=stride), :] = val


def put_receiver(afeat, half, px, py, pz):
    base = half * HALF * A_PITCH

    def row(k, v):
        afeat[pl.ds(base + k, HALF, stride=A_PITCH), :] = v

    size = split3(-KAPPA * (px * px + py * py + pz * pz))
    for d, v in enumerate((px, py, pz)):
        h, m, l = split3(v * (2.0 * KAPPA))
        row(d, h)
        row(8 + d, h)
        row(11 + d, h)
        row((7, 14, 15)[d], l)
        row(16 + d, m)
        row(24 + d, m)
    row(6, size[0])
    row(16 + 6, size[1])


def put_source(bfeat, lfeat, slot, half, place, torque, fill, shift, gate):
    place = [place[d] + shift[d] if shift[d] != 0.0 else place[d] for d in range(3)]
    x, y, z = place
    base = half * HALF * B_PITCH
    for d in range(3):
        h, m, l = split3(place[d])
        put(bfeat, slot, base + d, B_PITCH, h)
        put(bfeat, slot, base + 8 + d, B_PITCH, m)
        put(bfeat, slot, base + 11 + d, B_PITCH, l)
        put(bfeat, slot, base + (7, 14, 15)[d], B_PITCH, h)
    for k, v in enumerate(split3(-KAPPA * (x * x + y * y + z * z))):
        put(bfeat, slot, base + 3 + k, B_PITCH, v)
    if gate is not None:
        torque = [t * gate for t in torque]
        fill = fill * gate
    tx, ty, tz = torque
    loads = (tx, ty, tz, ty * z - tz * y, tz * x - tx * z, tx * y - ty * x)
    base = half * HALF * L_PITCH
    for q, v in enumerate(loads):
        h = narrow(v)
        put(lfeat, slot, base + q, L_PITCH, h)
        put(lfeat, slot, base + 8 + q, L_PITCH, v - h)
    put(lfeat, slot, base + 6, L_PITCH, fill)


def near_kernel(
    pos_in, tor_in, cnt, flg, pos_out, near_out, fill_out,
    state, places, gates, afeat, trans, bfeat, lfeat, totals,
    full_x, full_y, part_x, part_y, send_sem, recv_sem,
):
    row = lax.axis_index("row")
    col = lax.axis_index("col")
    peers = (
        (lax.rem(row + 1, ROWS), col),
        (lax.rem(row + ROWS - 1, ROWS), col),
        (row, lax.rem(col + 1, COLS)),
        (row, lax.rem(col + COLS - 1, COLS)),
    )
    barrier = pltpu.get_barrier_semaphore()
    for peer in peers:
        pl.semaphore_signal(barrier, inc=1, device_id=peer, device_id_type=MESH)

    lane = lax.broadcasted_iota(jnp.int32, (1, SLOT), 1)

    def spread_scalars(z, carry):
        for h in range(2):
            state[6, pl.ds(h * HALF + z, 1), :] = (lane < cnt[h, 0, z]).astype(F32)
            for f in range(6):
                gates[f, pl.ds(h * HALF + z, 1), :] = jnp.full((1, SLOT), flg[f, h, 0, z], jnp.int32).astype(F32)
        return carry

    lax.fori_loop(0, HALF, spread_scalars, 0)
    fill = state[6]
    fill_out[...] = fill
    for d in range(3):
        state[d] = pos_in[d] - MID
        state[3 + d] = tor_in[d] * fill

    pl.semaphore_wait(barrier, 4)

    def halo(step):
        if step == 0:
            own, into_x, into_y = state, full_x, full_y
        else:
            own, into_x, into_y = places.at[step - 1], part_x.at[step - 1], part_y.at[step - 1]
        moves = (
            (own.at[:, pl.ds(HALF, HALF), :], into_x.at[0], 0),
            (own.at[:, pl.ds(0, HALF), :], into_x.at[1], 1),
            (own, into_y.at[0], 2),
            (own, into_y.at[1], 3),
        )
        copies = []
        for src, dst, k in moves:
            copies.append(
                pltpu.make_async_remote_copy(
                    src_ref=src,
                    dst_ref=dst,
                    send_sem=send_sem.at[step, k],
                    recv_sem=recv_sem.at[step, k],
                    device_id=peers[k],
                    device_id_type=MESH,
                )
            )
        return copies

    one = jnp.ones((CELLS, SLOT), F32)
    zero = jnp.zeros((CELLS, SLOT), F32)
    for k in (19, 20, 21, 23, 27, 28, 29, 30, 31):
        afeat[pl.ds(k, CELLS, stride=A_PITCH), :] = zero
    for k in (3, 4, 5):
        afeat[pl.ds(k, CELLS, stride=A_PITCH), :] = one
    for e in range(7):
        put(bfeat, e, 6, B_PITCH, one)
        for k in (7, 14, 15):
            put(lfeat, e, k, L_PITCH, zero)

    owner = lax.broadcasted_iota(jnp.int32, (SLOT, SLOT), 1) // A_ROWS

    def wide(ref, n, cell, faces):
        blocks = [ref[e, pl.ds(cell * (n + 1), n), :] for e in faces]
        return (blocks[0] if len(blocks) == 1 else jnp.concatenate(blocks, 1)).astype(BF16)

    def weighted(block, first, pairs):
        ats = [jnp.where(owner == k, block, jnp.zeros_like(block)) for k in range(GROUP)]
        acc = [None] * GROUP
        for faces in pairs:
            b = []
            for k in range(GROUP):
                part = wide(bfeat, B_ROWS, first + k, faces)
                b += [part, part]
            b = jnp.concatenate(b, 0)
            power = jnp.dot(jnp.concatenate(ats, 0), b, preferred_element_type=F32)
            for k in range(GROUP):
                w = jnp.exp2(power[k * SLOT : (k + 1) * SLOT]).astype(BF16)
                load = wide(lfeat, L_ROWS, first + k, faces)
                out = lax.dot_general(load, w, (((1,), (1,)), ((), ())), preferred_element_type=F32)
                acc[k] = out if acc[k] is None else acc[k] + out
        return acc

    def inner_faces(i, carry):
        first = i * GROUP
        rows = [afeat[pl.ds((first + k) * A_PITCH, A_ROWS), :] for k in range(GROUP)]
        block = jnp.concatenate(rows, 0).T.astype(BF16)
        trans[i] = block
        for k, acc in enumerate(weighted(block, first, ((0, 1, 2, 3),))):
            totals[pl.ds((first + k) * T_PITCH, 8), :] = acc[0:8] + acc[8:16]
        return carry

    def outer_faces(i, carry):
        first = i * GROUP
        for k, acc in enumerate(weighted(trans[i], first, ((4, 5, 6),))):
            spot = pl.ds((first + k) * T_PITCH, 8)
            totals[spot, :] = totals[spot, :] + (acc[0:8] + acc[8:16])
        return carry

    for step in range(STEPS):
        copies = halo(step)
        for copy in copies:
            copy.start()
        here = state if step == 0 else places.at[step - 1]
        for h in range(2):
            part = slice(h * HALF, (h + 1) * HALF)
            other = slice((1 - h) * HALF, (2 - h) * HALF)
            place = [here[d, part, :] for d in range(3)]
            torque = [state[3 + d, part, :] for d in range(3)]
            fill = state[6, part, :]
            put_receiver(afeat, h, *place)
            put_source(bfeat, lfeat, 0, h, place, torque, fill, (0.0, 0.0, 0.0), None)
            for slot, turn, lift, face in ((1, HALF - 1, CELL, 4), (2, 1, -CELL, 5)):
                def turned(v):
                    return pltpu.roll(v, turn, 0)

                put_source(
                    bfeat, lfeat, slot, h, [turned(v) for v in place], [turned(v) for v in torque], turned(fill),
                    (0.0, 0.0, float(lift)), gates[face, part, :],
                )
            put_source(
                bfeat, lfeat, 3, h,
                [here[d, other, :] for d in range(3)],
                [state[3 + d, other, :] for d in range(3)],
                state[6, other, :],
                (float(CELL) if h == 0 else -float(CELL), 0.0, 0.0),
                gates[0 if h == 0 else 1, part, :],
            )
        lax.fori_loop(0, CELLS // GROUP, inner_faces, 0)
        for copy in copies:
            copy.wait_recv()
        for h in range(2):
            part = slice(h * HALF, (h + 1) * HALF)
            near_x = full_x if step == 0 else part_x.at[step - 1]
            near_y = full_y if step == 0 else part_y.at[step - 1]
            put_source(
                bfeat, lfeat, 4, h,
                [near_x[h, d] for d in range(3)],
                [full_x[h, 3 + d] for d in range(3)],
                full_x[h, 6],
                (-float(CELL) if h == 0 else float(CELL), 0.0, 0.0),
                gates[1 if h == 0 else 0, part, :],
            )
            for slot, side, lift, face in ((5, 1, CELL, 2), (6, 0, -CELL, 3)):
                put_source(
                    bfeat, lfeat, slot, h,
                    [near_y[side, d, part, :] for d in range(3)],
                    [full_y[side, 3 + d, part, :] for d in range(3)],
                    full_y[side, 6, part, :],
                    (0.0, float(lift), 0.0),
                    gates[face, part, :],
                )
        lax.fori_loop(0, CELLS // GROUP, outer_faces, 0)

        tot = [totals[pl.ds(q, CELLS, stride=T_PITCH), :] for q in range(7)]
        fill = state[6]
        x, y, z = (here[d] for d in range(3))
        speed = (
            tot[1] * z - tot[2] * y - tot[3],
            tot[2] * x - tot[0] * z - tot[4],
            tot[0] * y - tot[1] * x - tot[5],
        )
        for d in range(3):
            moved = here[d] + PACE * (DRIFT * speed[d] * fill)
            if step < STEPS - 1:
                places[step, d] = moved
            else:
                pos_out[d] = moved + MID
                torque = tor_in[d]
                near_out[d] = (torque + COUPLE * (tot[d] - tot[6] * torque)) * fill

    for step in range(STEPS):
        for copy in halo(step):
            copy.wait_send()


def near_field(positions, torques, counts, flags):
    vmem = pl.BlockSpec(memory_space=pltpu.VMEM)
    smem = pl.BlockSpec(memory_space=pltpu.SMEM)
    field = jax.ShapeDtypeStruct((3, CELLS, SLOT), F32)
    return pl.pallas_call(
        near_kernel,
        name="near",
        out_shape=(field, field, jax.ShapeDtypeStruct((CELLS, SLOT), F32)),
        in_specs=[vmem, vmem, smem, smem],
        out_specs=(vmem, vmem, vmem),
        scratch_shapes=[
            pltpu.VMEM((7, CELLS, SLOT), F32),
            pltpu.VMEM((STEPS - 1, 3, CELLS, SLOT), F32),
            pltpu.VMEM((6, CELLS, SLOT), F32),
            pltpu.VMEM((CELLS * A_PITCH, SLOT), F32),
            pltpu.VMEM((CELLS // GROUP, SLOT, SLOT), BF16),
            pltpu.VMEM((7, CELLS * B_PITCH, SLOT), F32),
            pltpu.VMEM((7, CELLS * L_PITCH, SLOT), F32),
            pltpu.VMEM((CELLS * T_PITCH, SLOT), F32),
            pltpu.VMEM((2, 7, HALF, SLOT), F32),
            pltpu.VMEM((2, 7, CELLS, SLOT), F32),
            pltpu.VMEM((STEPS - 1, 2, 3, HALF, SLOT), F32),
            pltpu.VMEM((STEPS - 1, 2, 3, CELLS, SLOT), F32),
            pltpu.SemaphoreType.DMA((STEPS, 4)),
            pltpu.SemaphoreType.DMA((STEPS, 4)),
        ],
        compiler_params=pltpu.CompilerParams(collective_id=0, has_side_effects=True),
    )(positions, torques, counts, flags)


def halves(table):
    high = table.astype(np.float32).astype(jnp.bfloat16)
    low = (table - high.astype(np.float64)).astype(np.float32).astype(jnp.bfloat16)
    return high, low


def make_tables():
    n = np.arange(GRID)
    level = np.where(n == 1, 64, n // 2)
    angle = 2.0 * np.pi * (level[:, None] * n[None, :] % GRID) / GRID
    cosine, sine = np.cos(angle), np.sin(angle)
    even = (n % 2 == 0)[:, None]
    whole = (n < 2)[:, None]
    basis_xy = np.where(whole | even, cosine, sine)
    basis_z = np.where(whole | ~even, cosine, sine)
    count = np.where(n < 2, 1.0, 2.0)[:, None]
    back_xy, back_z = (basis_xy * count).T, (basis_z * count).T

    def wave(a, b, period_a, period_b):
        return 2.0 * np.pi * ((a * b[0] % period_a) / period_a + (b[1] % period_b) / period_b)

    r, q = n // 16, n % 16
    turn_l = 2.0 * np.pi * ((r[:, None] * r[None, :] % 8) / 8 + (q[:, None] * q[None, :] % 16) / 16)
    s, t = n // 8, n % 8
    turn_r = 2.0 * np.pi * ((s[:, None] * s[None, :] % 16) / 16 + (t[:, None] * t[None, :] % 8) / 8)
    twist = 2.0 * np.pi * (r[:, None] * s[None, :] + q[:, None] * t[None, :]) / GRID
    cl, sl = np.cos(turn_l), np.sin(turn_l)
    cr, sr = np.cos(turn_r), np.sin(turn_r)
    left = np.concatenate([cl, -sl], 0)
    left_back = np.concatenate([cl, -sl], 1)
    right = np.block([[cr, -sr], [sr, cr]])
    right_back = np.block([[cr, sr], [-sr, cr]])
    out = []
    for table in (basis_xy, basis_z, back_xy, back_z, left, left_back, right, right_back):
        high, low = halves(table)
        out += [high, low]
    out.append(np.stack([np.cos(twist), np.sin(twist)]).astype(np.float32))
    return out


def cut(v):
    h = v.astype(BF16)
    return h, (v - h.astype(F32)).astype(BF16)


def mul(a, b):
    return jnp.dot(a, b, preferred_element_type=F32)


def mul_t(a, b):
    return lax.dot_general(a, b, (((1,), (1,)), ((), ())), preferred_element_type=F32)


def table_left(high, low, v):
    vh, vl = cut(v)
    return mul(high, vh) + (mul(low, vh) + mul(high, vl))


def table_right(v, high, low):
    vh, vl = cut(v)
    return mul(vh, high) + (mul(vl, high) + mul(vh, low))


def far_kernel(
    pos, tor, near, fill, zf_xy_h, zf_xy_l, zf_z_h, zf_z_l, zb_xy_h, zb_xy_l, zb_z_h, zb_z_l,
    lf_h, lf_l, lb_h, lb_l, rf_h, rf_l, rb_h, rb_l, twist,
    spin,
    grid, plan_h, plan_l, depth, out_1, in_1, out_2, in_2, work, far, send_sem, recv_sem, self_sem,
):
    row = lax.axis_index("row")
    col = lax.axis_index("col")
    me = row * COLS + col
    barrier = pltpu.get_barrier_semaphore()

    def peer(k):
        p = me + k
        return jnp.where(p >= DEVICES, p - DEVICES, p)

    def greet(k, carry):
        pl.semaphore_signal(barrier, inc=1, device_id=peer(k), device_id_type=LOGICAL)
        return carry

    lax.fori_loop(1, DEVICES, greet, 0, unroll=9)

    level = lax.broadcasted_iota(jnp.int32, (CELL, SLOT), 0).astype(F32) + 0.5
    low_lane = lax.broadcasted_iota(jnp.int32, (24, SLOT), 1) < 64

    def bins(d, cell):
        apart = pos[d, pl.ds(cell, 1), :] - level
        return jnp.exp(-apart * apart)

    def spread(z, carry):
        planar, lifted, rest = [], [], []
        for h in range(2):
            cell = h * HALF + z
            bx, by, bz = (bins(d, cell) for d in range(3))
            depth[pl.ds(pl.multiple_of(cell * 8, 8), 8), :] = bz
            planar += [bx[a : a + 1, :] * by for a in range(CELL)]
            lift = [tor[c, pl.ds(cell, 1), :] * fill[pl.ds(cell, 1), :] * bz for c in range(3)]
            top = [narrow(v) for v in lift]
            lifted += top
            rest += [v - t for v, t in zip(lift, top)]
        ph, pl_ = cut(jnp.concatenate(planar, 0))
        plan_h[z] = ph
        plan_l[z] = pl_
        both = mul_t(jnp.concatenate(lifted + rest, 0).astype(BF16), ph)
        more = mul_t(jnp.concatenate(lifted, 0).astype(BF16), pl_)
        sums = both[0:48] + both[48:96] + more
        block = jnp.where(low_lane, sums[0:24], sums[24:48])
        for c in range(3):
            grid[c, pl.ds(pl.multiple_of(z * 8, 8), 8), :] = block[c * 8 : c * 8 + 8]
        return carry

    lax.fori_loop(0, HALF, spread, 0)

    for c in range(3):
        high, low = (zf_xy_h, zf_xy_l) if c < 2 else (zf_z_h, zf_z_l)
        out_1[pl.ds(c, DEVICES, stride=8), :] = table_left(high[...], low[...], grid[c])

    pl.semaphore_wait(barrier, DEVICES - 1)

    def exchange(out, into, k):
        def post(i, carry):
            p = peer(i)
            pltpu.make_async_remote_copy(
                src_ref=out.at[pl.ds(pl.multiple_of(p * 8, 8), 3), :],
                dst_ref=into.at[pl.ds(pl.multiple_of(me * 8, 8), 3), :],
                send_sem=send_sem.at[k],
                recv_sem=recv_sem.at[k],
                device_id=p,
                device_id_type=LOGICAL,
            ).start()
            return carry

        lax.fori_loop(1, DEVICES, post, 0, unroll=9)
        mine = pl.ds(pl.multiple_of(me * 8, 8), 3)
        keep = pltpu.make_async_copy(out.at[mine, :], into.at[mine, :], self_sem.at[k])
        keep.start()
        keep.wait()
        bulk = out.at[pl.ds(0, 3 * (DEVICES - 1)), :]
        pltpu.make_async_copy(bulk, bulk, recv_sem.at[k]).wait()

    exchange(out_1, in_1, 0)

    cos_t, sin_t = twist[0], twist[1]
    for c in range(3):
        both = table_left(lf_h[...], lf_l[...], in_1[pl.ds(c, DEVICES, stride=8), :])
        re, im = both[0:128], both[128:256]
        work[c, :, 0:128] = re * cos_t + im * sin_t
        work[c, :, 128:256] = im * cos_t - re * sin_t
    for c in range(3):
        work[c] = table_right(work[c], rf_h[...], rf_l[...])

    special = me < 2
    plain = jnp.where(special, 1.0, 0.0).astype(F32)
    turn = jnp.where(special, 0, 2 * lax.rem(me, 2) - 1).astype(F32)
    kz = jnp.where(me == 1, -64, me // 2).astype(F32)
    kz_top = jnp.where(me == 1, -64, 0).astype(F32)
    kz_low = jnp.where(me == 1, 0, me // 2).astype(F32)

    def signed(v):
        return jnp.where(v < GRID // 2, v, v - GRID)

    def stokes(i, carry):
        rows = pl.ds(pl.multiple_of(i * 16, 16), 16)
        f1 = lax.broadcasted_iota(jnp.int32, (16, 128), 0) + i * 16
        f2 = lax.broadcasted_iota(jnp.int32, (16, 128), 1)
        ix = signed(f1 // 16 + 8 * (f2 // 8))
        iy = signed(f1 % 16 + 16 * (f2 % 8))
        kx, ky = ix.astype(F32), iy.astype(F32)
        kx_top = jnp.where(ix == -64, kx, 0.0)
        ky_top = jnp.where(iy == -64, ky, 0.0)
        kx_low, ky_low = kx - kx_top, ky - ky_top
        square = kx * kx + ky * ky + kz * kz
        damping = (0.25 / GRID**3) * jnp.exp(square * (-((math.pi / GRID) ** 2)))
        inverse = 1.0 / jnp.maximum(square, 1.0)
        w_re, w_im = work[2, rows, 0:128], work[2, rows, 128:256]
        sides = (
            (work[0, rows, 0:128], work[1, rows, 0:128], plain * w_re - turn * w_im),
            (work[0, rows, 128:256], work[1, rows, 128:256], plain * w_im + turn * w_re),
        )
        done = []
        for u, v, w in sides:
            low = (kx_low * u + ky_low * v + kz_low * w) * inverse
            top = (kx_top * u + ky_top * v + kz_top * w) * inverse
            done.append(
                (
                    damping * (u - kx_low * low - kx_top * top),
                    damping * (v - ky_low * low - ky_top * top),
                    damping * (w - kz_low * low - kz_top * top),
                )
            )
        for c in range(2):
            work[c, rows, 0:128] = done[0][c]
            work[c, rows, 128:256] = done[1][c]
        work[2, rows, 0:128] = plain * done[0][2] + turn * done[1][2]
        work[2, rows, 128:256] = plain * done[1][2] - turn * done[0][2]
        return carry

    lax.fori_loop(0, 8, stokes, 0)

    for c in range(3):
        both = table_right(work[c], rb_h[...], rb_l[...])
        re, im = both[:, 0:128], both[:, 128:256]
        pair = jnp.concatenate([re * cos_t - im * sin_t, im * cos_t + re * sin_t], 0)
        out_2[pl.ds(c, DEVICES, stride=8), :] = table_left(lb_h[...], lb_l[...], pair)

    exchange(out_2, in_2, 1)

    for c in range(3):
        high, low = (zb_xy_h, zb_xy_l) if c < 2 else (zb_z_h, zb_z_l)
        grid[c] = table_left(high[...], low[...], in_2[pl.ds(c, DEVICES, stride=8), :])

    def gather(z, carry):
        rows = pl.ds(pl.multiple_of(z * 8, 8), 8)
        block = jnp.concatenate([grid[c, rows, :] for c in range(3)], 0)
        near_half = jnp.where(low_lane, block, 0.0)
        far_half = block - near_half
        both = jnp.concatenate([near_half, far_half], 0)
        top = narrow(both)
        first = mul(jnp.concatenate([top, both - top], 0).astype(BF16), plan_h[z])
        second = mul(top.astype(BF16), plan_l[z])
        sums = first[0:48] + first[48:96] + second
        for h in range(2):
            spot = pl.ds(pl.multiple_of((h * HALF + z) * 8, 8), 8)
            bz = depth[spot, :]
            for c in range(3):
                far[c, spot, :] = sums[h * 24 + c * 8 : h * 24 + c * 8 + 8] * bz
        return carry

    lax.fori_loop(0, HALF, gather, 0)

    for c in range(3):
        total = far[c, pl.ds(0, CELLS, stride=8), :]
        for g in range(1, CELL):
            total = total + far[c, pl.ds(g, CELLS, stride=8), :]
        spin[c] = near[c] + total * fill[...]

    for k in range(2):
        bulk = out_1.at[pl.ds(0, 3 * (DEVICES - 1)), :]
        pltpu.make_async_copy(bulk, bulk, send_sem.at[k]).wait()


def far_field(places, torques, near, fill):
    tables = [jnp.asarray(t) for t in make_tables()]
    vmem = pl.BlockSpec(memory_space=pltpu.VMEM)
    buffer = pltpu.VMEM((DEVICES * 8, 128), F32)
    return pl.pallas_call(
        far_kernel,
        name="far",
        out_shape=jax.ShapeDtypeStruct((3, CELLS, SLOT), F32),
        in_specs=[vmem] * (4 + len(tables)),
        out_specs=vmem,
        scratch_shapes=[
            pltpu.VMEM((3, GRID, 128), F32),
            pltpu.VMEM((HALF, 128, SLOT), BF16),
            pltpu.VMEM((HALF, 128, SLOT), BF16),
            pltpu.VMEM((CELLS * 8, SLOT), F32),
            buffer,
            buffer,
            buffer,
            buffer,
            pltpu.VMEM((3, 128, 256), F32),
            pltpu.VMEM((3, CELLS * 8, SLOT), F32),
            pltpu.SemaphoreType.DMA((2,)),
            pltpu.SemaphoreType.DMA((2,)),
            pltpu.SemaphoreType.DMA((2,)),
        ],
        compiler_params=pltpu.CompilerParams(collective_id=1, has_side_effects=True),
    )(places, torques, near, fill, *tables)


def shards(positions, torques, counts, neighbour_flags):
    shape = positions.shape
    flat = (3, CELLS, SLOT)
    torques = torques.reshape(flat)
    places, near, fill = near_field(positions.reshape(flat), torques, counts, neighbour_flags)
    spin = far_field(places, torques, near, fill)
    return places.reshape(shape), spin.reshape(shape)


def solution(mesh):
    in_specs = (
        P(None, "row", "col", None, None),
        P(None, "row", "col", None, None),
        P("row", "col", None),
        P(None, "row", "col", None),
    )
    out_specs = (P(None, "row", "col", None, None), P(None, "row", "col", None, None))
    return jax.shard_map(shards, mesh=mesh, in_specs=in_specs, out_specs=out_specs, check_vma=False)
```

```python
import math

import jax
import jax.numpy as jnp
import numpy as np
from jax import lax
from jax.experimental import pallas as pl
from jax.experimental.pallas import tpu as pltpu
from jax.sharding import PartitionSpec as P

GRID = 128
CELL = 8
SLOT = 128
STEPS = 3
ROWS = 8
COLS = 16
DEVICES = ROWS * COLS
CELLS = 32
HALF = 16
MESH = pl.DeviceIdType.MESH
LOGICAL = pl.DeviceIdType.LOGICAL
F32 = jnp.float32
BF16 = jnp.bfloat16

KAPPA = 2.0 / (CELL * CELL) * math.log2(math.e)
PACE = 0.06 * CELL
DRIFT = 1.0 / SLOT
COUPLE = 0.5 / SLOT
MID = 0.5 * CELL

A_ROWS = 32
GROUP = SLOT // A_ROWS
B_ROWS = 16
L_ROWS = 16
A_PITCH = A_ROWS + 1
B_PITCH = B_ROWS + 1
L_PITCH = L_ROWS + 1
T_PITCH = 9


def halves(table):
    high = table.astype(np.float32).astype(jnp.bfloat16)
    low = (table - high.astype(np.float64)).astype(np.float32).astype(jnp.bfloat16)
    return high, low


def make_tables():
    n = np.arange(GRID)
    level = np.where(n == 1, 64, n // 2)
    angle = 2.0 * np.pi * (level[:, None] * n[None, :] % GRID) / GRID
    cosine, sine = np.cos(angle), np.sin(angle)
    even = (n % 2 == 0)[:, None]
    whole = (n < 2)[:, None]
    basis_xy = np.where(whole | even, cosine, sine)
    basis_z = np.where(whole | ~even, cosine, sine)
    count = np.where(n < 2, 1.0, 2.0)[:, None]
    back_xy, back_z = (basis_xy * count).T, (basis_z * count).T

    def wave(a, b, period_a, period_b):
        return 2.0 * np.pi * ((a * b[0] % period_a) / period_a + (b[1] % period_b) / period_b)

    r, q = n // 16, n % 16
    turn_l = 2.0 * np.pi * ((r[:, None] * r[None, :] % 8) / 8 + (q[:, None] * q[None, :] % 16) / 16)
    s, t = n // 8, n % 8
    turn_r = 2.0 * np.pi * ((s[:, None] * s[None, :] % 16) / 16 + (t[:, None] * t[None, :] % 8) / 8)
    twist = 2.0 * np.pi * (r[:, None] * s[None, :] + q[:, None] * t[None, :]) / GRID
    cl, sl = np.cos(turn_l), np.sin(turn_l)
    cr, sr = np.cos(turn_r), np.sin(turn_r)
    left = np.concatenate([cl, -sl], 0)
    left_back = np.concatenate([cl, -sl], 1)
    right = np.block([[cr, -sr], [sr, cr]])
    right_back = np.block([[cr, sr], [-sr, cr]])
    along_z = [half for table in (basis_xy, basis_z, back_xy, back_z) for half in halves(table)]
    out = [np.stack(along_z)] + [np.stack(halves(table)) for table in (left, left_back, right, right_back)]
    return out + [np.stack([np.cos(twist), np.sin(twist)]).astype(np.float32)]


def cut(v):
    h = v.astype(BF16)
    return h, (v - h.astype(F32)).astype(BF16)


def mul(a, b):
    return jnp.dot(a, b, preferred_element_type=F32)


def mul_t(a, b):
    return lax.dot_general(a, b, (((1,), (1,)), ((), ())), preferred_element_type=F32)


def table_left(high, low, v):
    vh, vl = cut(v)
    return mul(high, vh) + (mul(low, vh) + mul(high, vl))


def table_right(v, high, low):
    vh, vl = cut(v)
    return mul(vh, high) + (mul(vl, high) + mul(vh, low))


def narrow(v):
    return v.astype(BF16).astype(F32)


def split3(v):
    h = narrow(v)
    r = v - h
    m = narrow(r)
    return h, m, r - m


def put(ref, lead, start, stride, val):
    ref[lead, pl.ds(start, val.shape[0], stride=stride), :] = val


def put_receiver(afeat, half, px, py, pz):
    base = half * HALF * A_PITCH

    def row(k, v):
        afeat[pl.ds(base + k, HALF, stride=A_PITCH), :] = v

    size = split3(-KAPPA * (px * px + py * py + pz * pz))
    for d, v in enumerate((px, py, pz)):
        h, m, l = split3(v * (2.0 * KAPPA))
        row(d, h)
        row(8 + d, h)
        row(11 + d, h)
        row((7, 14, 15)[d], l)
        row(16 + d, m)
        row(24 + d, m)
    row(6, size[0])
    row(16 + 6, size[1])


def put_source(bfeat, lfeat, slot, half, place, torque, fill, shift, gate):
    place = [place[d] + shift[d] if shift[d] != 0.0 else place[d] for d in range(3)]
    x, y, z = place
    base = half * HALF * B_PITCH
    for d in range(3):
        h, m, l = split3(place[d])
        put(bfeat, slot, base + d, B_PITCH, h)
        put(bfeat, slot, base + 8 + d, B_PITCH, m)
        put(bfeat, slot, base + 11 + d, B_PITCH, l)
        put(bfeat, slot, base + (7, 14, 15)[d], B_PITCH, h)
    for k, v in enumerate(split3(-KAPPA * (x * x + y * y + z * z))):
        put(bfeat, slot, base + 3 + k, B_PITCH, v)
    if gate is not None:
        torque = [t * gate for t in torque]
        fill = fill * gate
    tx, ty, tz = torque
    loads = (tx, ty, tz, ty * z - tz * y, tz * x - tx * z, tx * y - ty * x)
    base = half * HALF * L_PITCH
    for q, v in enumerate(loads):
        h = narrow(v)
        put(lfeat, slot, base + q, L_PITCH, h)
        put(lfeat, slot, base + 8 + q, L_PITCH, v - h)
    put(lfeat, slot, base + 6, L_PITCH, fill)


def kernel(
    pos_in, tor_in, cnt, flg, z_far, lf_far, lb_far, rf_far, rb_far, twist_far, pos_out, spin,
    near_out, state, places, gates, afeat, trans, bfeat, lfeat, totals,
    full_x, full_y, part_x, part_y, send_sem, recv_sem, tell,
    z_tab, lf, lb, rf, rb, twist, table_sem,
    grid, plan_h, plan_l, depth, out_1, in_1, out_2, in_2, work, far, all_send, all_recv, self_sem,
):
    row = lax.axis_index("row")
    col = lax.axis_index("col")
    peers = (
        (lax.rem(row + 1, ROWS), col),
        (lax.rem(row + ROWS - 1, ROWS), col),
        (row, lax.rem(col + 1, COLS)),
        (row, lax.rem(col + COLS - 1, COLS)),
    )
    barrier = pltpu.get_barrier_semaphore()
    for peer in peers:
        pl.semaphore_signal(barrier, inc=1, device_id=peer, device_id_type=MESH)

    tables = [
        pltpu.make_async_copy(src, dst, table_sem.at[k])
        for k, (src, dst) in enumerate(
            ((z_far, z_tab), (lf_far, lf), (lb_far, lb), (rf_far, rf), (rb_far, rb), (twist_far, twist))
        )
    ]
    for table in tables:
        table.start()

    def inform(k, steps):
        for down, right in steps:
            where = (lax.rem(row + down + ROWS, ROWS), lax.rem(col + right + COLS, COLS))
            pl.semaphore_signal(tell.at[k], inc=1, device_id=where, device_id_type=MESH)

    def learn(step):
        if step == 0:
            inform(0, ((2, 0), (-2, 0), (0, 2), (0, -2)))
        elif step == 1:
            pl.semaphore_wait(tell.at[0], 4)
            inform(1, ((0, 4), (0, -4)))
        else:
            pl.semaphore_wait(tell.at[1], 2)
            inform(2, [(k, 0) for k in range(1, ROWS)])

    lane = lax.broadcasted_iota(jnp.int32, (1, SLOT), 1)

    def spread_scalars(z, carry):
        for h in range(2):
            state[6, pl.ds(h * HALF + z, 1), :] = (lane < cnt[h, 0, z]).astype(F32)
            for f in range(6):
                gates[f, pl.ds(h * HALF + z, 1), :] = jnp.full((1, SLOT), flg[f, h, 0, z], jnp.int32).astype(F32)
        return carry

    lax.fori_loop(0, HALF, spread_scalars, 0)
    fill = state[6]
    for d in range(3):
        state[d] = pos_in[d] - MID
        state[3 + d] = tor_in[d] * fill

    pl.semaphore_wait(barrier, 4)

    def halo(step):
        if step == 0:
            own, into_x, into_y = state, full_x, full_y
        else:
            own, into_x, into_y = places.at[step - 1], part_x.at[step - 1], part_y.at[step - 1]
        moves = (
            (own.at[:, pl.ds(HALF, HALF), :], into_x.at[0], 0),
            (own.at[:, pl.ds(0, HALF), :], into_x.at[1], 1),
            (own, into_y.at[0], 2),
            (own, into_y.at[1], 3),
        )
        copies = []
        for src, dst, k in moves:
            copies.append(
                pltpu.make_async_remote_copy(
                    src_ref=src,
                    dst_ref=dst,
                    send_sem=send_sem.at[step, k],
                    recv_sem=recv_sem.at[step, k],
                    device_id=peers[k],
                    device_id_type=MESH,
                )
            )
        return copies

    one = jnp.ones((CELLS, SLOT), F32)
    zero = jnp.zeros((CELLS, SLOT), F32)
    for k in (19, 20, 21, 23, 27, 28, 29, 30, 31):
        afeat[pl.ds(k, CELLS, stride=A_PITCH), :] = zero
    for k in (3, 4, 5):
        afeat[pl.ds(k, CELLS, stride=A_PITCH), :] = one
    for e in range(7):
        put(bfeat, e, 6, B_PITCH, one)
        for k in (7, 14, 15):
            put(lfeat, e, k, L_PITCH, zero)

    owner = lax.broadcasted_iota(jnp.int32, (SLOT, SLOT), 1) // A_ROWS

    def wide(ref, n, cell, faces):
        blocks = [ref[e, pl.ds(cell * (n + 1), n), :] for e in faces]
        return (blocks[0] if len(blocks) == 1 else jnp.concatenate(blocks, 1)).astype(BF16)

    def weighted(block, first, pairs):
        ats = [jnp.where(owner == k, block, jnp.zeros_like(block)) for k in range(GROUP)]
        acc = [None] * GROUP
        for faces in pairs:
            b = []
            for k in range(GROUP):
                part = wide(bfeat, B_ROWS, first + k, faces)
                b += [part, part]
            b = jnp.concatenate(b, 0)
            power = jnp.dot(jnp.concatenate(ats, 0), b, preferred_element_type=F32)
            for k in range(GROUP):
                w = jnp.exp2(power[k * SLOT : (k + 1) * SLOT]).astype(BF16)
                load = wide(lfeat, L_ROWS, first + k, faces)
                out = lax.dot_general(load, w, (((1,), (1,)), ((), ())), preferred_element_type=F32)
                acc[k] = out if acc[k] is None else acc[k] + out
        return acc

    def inner_faces(i, carry):
        first = i * GROUP
        rows = [afeat[pl.ds((first + k) * A_PITCH, A_ROWS), :] for k in range(GROUP)]
        block = jnp.concatenate(rows, 0).T.astype(BF16)
        trans[i] = block
        for k, acc in enumerate(weighted(block, first, ((0, 1, 2, 3),))):
            totals[pl.ds((first + k) * T_PITCH, 8), :] = acc[0:8] + acc[8:16]
        return carry

    def outer_faces(i, carry):
        first = i * GROUP
        for k, acc in enumerate(weighted(trans[i], first, ((4, 5, 6),))):
            spot = pl.ds((first + k) * T_PITCH, 8)
            totals[spot, :] = totals[spot, :] + (acc[0:8] + acc[8:16])
        return carry

    for step in range(STEPS):
        copies = halo(step)
        for copy in copies:
            copy.start()
        here = state if step == 0 else places.at[step - 1]
        for h in range(2):
            part = slice(h * HALF, (h + 1) * HALF)
            other = slice((1 - h) * HALF, (2 - h) * HALF)
            place = [here[d, part, :] for d in range(3)]
            torque = [state[3 + d, part, :] for d in range(3)]
            fill = state[6, part, :]
            put_receiver(afeat, h, *place)
            put_source(bfeat, lfeat, 0, h, place, torque, fill, (0.0, 0.0, 0.0), None)
            for slot, turn, lift, face in ((1, HALF - 1, CELL, 4), (2, 1, -CELL, 5)):
                def turned(v):
                    return pltpu.roll(v, turn, 0)

                put_source(
                    bfeat, lfeat, slot, h, [turned(v) for v in place], [turned(v) for v in torque], turned(fill),
                    (0.0, 0.0, float(lift)), gates[face, part, :],
                )
            put_source(
                bfeat, lfeat, 3, h,
                [here[d, other, :] for d in range(3)],
                [state[3 + d, other, :] for d in range(3)],
                state[6, other, :],
                (float(CELL) if h == 0 else -float(CELL), 0.0, 0.0),
                gates[0 if h == 0 else 1, part, :],
            )
        lax.fori_loop(0, CELLS // GROUP, inner_faces, 0)
        for copy in copies:
            copy.wait_recv()
        learn(step)
        for h in range(2):
            part = slice(h * HALF, (h + 1) * HALF)
            near_x = full_x if step == 0 else part_x.at[step - 1]
            near_y = full_y if step == 0 else part_y.at[step - 1]
            put_source(
                bfeat, lfeat, 4, h,
                [near_x[h, d] for d in range(3)],
                [full_x[h, 3 + d] for d in range(3)],
                full_x[h, 6],
                (-float(CELL) if h == 0 else float(CELL), 0.0, 0.0),
                gates[1 if h == 0 else 0, part, :],
            )
            for slot, side, lift, face in ((5, 1, CELL, 2), (6, 0, -CELL, 3)):
                put_source(
                    bfeat, lfeat, slot, h,
                    [near_y[side, d, part, :] for d in range(3)],
                    [full_y[side, 3 + d, part, :] for d in range(3)],
                    full_y[side, 6, part, :],
                    (0.0, float(lift), 0.0),
                    gates[face, part, :],
                )
        lax.fori_loop(0, CELLS // GROUP, outer_faces, 0)

        tot = [totals[pl.ds(q, CELLS, stride=T_PITCH), :] for q in range(7)]
        fill = state[6]
        x, y, z = (here[d] for d in range(3))
        speed = (
            tot[1] * z - tot[2] * y - tot[3],
            tot[2] * x - tot[0] * z - tot[4],
            tot[0] * y - tot[1] * x - tot[5],
        )
        for d in range(3):
            moved = here[d] + PACE * (DRIFT * speed[d] * fill)
            if step < STEPS - 1:
                places[step, d] = moved
            else:
                pos_out[d] = moved + MID
                torque = tor_in[d]
                near_out[d] = (torque + COUPLE * (tot[d] - tot[6] * torque)) * fill

    me = row * COLS + col

    def peer(k):
        p = me + k
        return jnp.where(p >= DEVICES, p - DEVICES, p)

    level = lax.broadcasted_iota(jnp.int32, (CELL, SLOT), 0).astype(F32) + 0.5
    low_lane = lax.broadcasted_iota(jnp.int32, (24, SLOT), 1) < 64

    for table in tables:
        table.wait()

    def bins(d, cell):
        apart = pos_out[d, pl.ds(cell, 1), :] - level
        return jnp.exp(-apart * apart)

    def spread(z, carry):
        planar, lifted, rest = [], [], []
        for h in range(2):
            cell = h * HALF + z
            bx, by, bz = (bins(d, cell) for d in range(3))
            depth[pl.ds(pl.multiple_of(cell * 8, 8), 8), :] = bz
            planar += [bx[a : a + 1, :] * by for a in range(CELL)]
            lift = [state[3 + c, pl.ds(cell, 1), :] * bz for c in range(3)]
            top = [narrow(v) for v in lift]
            lifted += top
            rest += [v - t for v, t in zip(lift, top)]
        ph, pl_ = cut(jnp.concatenate(planar, 0))
        plan_h[z] = ph
        plan_l[z] = pl_
        both = mul_t(jnp.concatenate(lifted + rest, 0).astype(BF16), ph)
        more = mul_t(jnp.concatenate(lifted, 0).astype(BF16), pl_)
        sums = both[0:48] + both[48:96] + more
        block = jnp.where(low_lane, sums[0:24], sums[24:48])
        for c in range(3):
            grid[c, pl.ds(pl.multiple_of(z * 8, 8), 8), :] = block[c * 8 : c * 8 + 8]
        return carry

    lax.fori_loop(0, HALF, spread, 0)

    for c in range(3):
        n = 0 if c < 2 else 2
        out_1[pl.ds(c, DEVICES, stride=8), :] = table_left(z_tab[n], z_tab[n + 1], grid[c])

    pl.semaphore_wait(tell.at[2], ROWS - 1)

    def exchange(out, into, k):
        def post(i, carry):
            p = peer(i)
            pltpu.make_async_remote_copy(
                src_ref=out.at[pl.ds(pl.multiple_of(p * 8, 8), 3), :],
                dst_ref=into.at[pl.ds(pl.multiple_of(me * 8, 8), 3), :],
                send_sem=all_send.at[k],
                recv_sem=all_recv.at[k],
                device_id=p,
                device_id_type=LOGICAL,
            ).start()
            return carry

        lax.fori_loop(1, DEVICES, post, 0, unroll=9)
        mine = pl.ds(pl.multiple_of(me * 8, 8), 3)
        keep = pltpu.make_async_copy(out.at[mine, :], into.at[mine, :], self_sem.at[k])
        keep.start()
        keep.wait()
        bulk = out.at[pl.ds(0, 3 * (DEVICES - 1)), :]
        pltpu.make_async_copy(bulk, bulk, all_recv.at[k]).wait()

    exchange(out_1, in_1, 0)

    cos_t, sin_t = twist[0], twist[1]
    for c in range(3):
        both = table_left(lf[0], lf[1], in_1[pl.ds(c, DEVICES, stride=8), :])
        re, im = both[0:128], both[128:256]
        work[c, :, 0:128] = re * cos_t + im * sin_t
        work[c, :, 128:256] = im * cos_t - re * sin_t
    for c in range(3):
        work[c] = table_right(work[c], rf[0], rf[1])

    special = me < 2
    plain = jnp.where(special, 1.0, 0.0).astype(F32)
    turn = jnp.where(special, 0, 2 * lax.rem(me, 2) - 1).astype(F32)
    kz = jnp.where(me == 1, -64, me // 2).astype(F32)
    kz_top = jnp.where(me == 1, -64, 0).astype(F32)
    kz_low = jnp.where(me == 1, 0, me // 2).astype(F32)

    def signed(v):
        return jnp.where(v < GRID // 2, v, v - GRID)

    def stokes(i, carry):
        rows = pl.ds(pl.multiple_of(i * 16, 16), 16)
        f1 = lax.broadcasted_iota(jnp.int32, (16, 128), 0) + i * 16
        f2 = lax.broadcasted_iota(jnp.int32, (16, 128), 1)
        ix = signed(f1 // 16 + 8 * (f2 // 8))
        iy = signed(f1 % 16 + 16 * (f2 % 8))
        kx, ky = ix.astype(F32), iy.astype(F32)
        kx_top = jnp.where(ix == -64, kx, 0.0)
        ky_top = jnp.where(iy == -64, ky, 0.0)
        kx_low, ky_low = kx - kx_top, ky - ky_top
        square = kx * kx + ky * ky + kz * kz
        damping = (0.25 / GRID**3) * jnp.exp(square * (-((math.pi / GRID) ** 2)))
        inverse = 1.0 / jnp.maximum(square, 1.0)
        w_re, w_im = work[2, rows, 0:128], work[2, rows, 128:256]
        sides = (
            (work[0, rows, 0:128], work[1, rows, 0:128], plain * w_re - turn * w_im),
            (work[0, rows, 128:256], work[1, rows, 128:256], plain * w_im + turn * w_re),
        )
        done = []
        for u, v, w in sides:
            low = (kx_low * u + ky_low * v + kz_low * w) * inverse
            top = (kx_top * u + ky_top * v + kz_top * w) * inverse
            done.append(
                (
                    damping * (u - kx_low * low - kx_top * top),
                    damping * (v - ky_low * low - ky_top * top),
                    damping * (w - kz_low * low - kz_top * top),
                )
            )
        for c in range(2):
            work[c, rows, 0:128] = done[0][c]
            work[c, rows, 128:256] = done[1][c]
        work[2, rows, 0:128] = plain * done[0][2] + turn * done[1][2]
        work[2, rows, 128:256] = plain * done[1][2] - turn * done[0][2]
        return carry

    lax.fori_loop(0, 8, stokes, 0)

    for c in range(3):
        both = table_right(work[c], rb[0], rb[1])
        re, im = both[:, 0:128], both[:, 128:256]
        pair = jnp.concatenate([re * cos_t - im * sin_t, im * cos_t + re * sin_t], 0)
        out_2[pl.ds(c, DEVICES, stride=8), :] = table_left(lb[0], lb[1], pair)

    exchange(out_2, in_2, 1)

    for c in range(3):
        n = 4 if c < 2 else 6
        grid[c] = table_left(z_tab[n], z_tab[n + 1], in_2[pl.ds(c, DEVICES, stride=8), :])

    def gather(z, carry):
        rows = pl.ds(pl.multiple_of(z * 8, 8), 8)
        block = jnp.concatenate([grid[c, rows, :] for c in range(3)], 0)
        near_half = jnp.where(low_lane, block, 0.0)
        far_half = block - near_half
        both = jnp.concatenate([near_half, far_half], 0)
        top = narrow(both)
        first = mul(jnp.concatenate([top, both - top], 0).astype(BF16), plan_h[z])
        second = mul(top.astype(BF16), plan_l[z])
        sums = first[0:48] + first[48:96] + second
        for h in range(2):
            spot = pl.ds(pl.multiple_of((h * HALF + z) * 8, 8), 8)
            bz = depth[spot, :]
            for c in range(3):
                far[c, spot, :] = sums[h * 24 + c * 8 : h * 24 + c * 8 + 8] * bz
        return carry

    lax.fori_loop(0, HALF, gather, 0)

    for c in range(3):
        total = far[c, pl.ds(0, CELLS, stride=8), :]
        for g in range(1, CELL):
            total = total + far[c, pl.ds(g, CELLS, stride=8), :]
        spin[c] = near_out[c] + total * state[6]

    for k in range(2):
        bulk = out_1.at[pl.ds(0, 3 * (DEVICES - 1)), :]
        pltpu.make_async_copy(bulk, bulk, all_send.at[k]).wait()
    for step in range(STEPS):
        for copy in halo(step):
            copy.wait_send()
def shards(positions, torques, counts, neighbour_flags):
    shape = positions.shape
    flat = (3, CELLS, SLOT)
    tables = [jnp.asarray(t) for t in make_tables()]
    vmem = pl.BlockSpec(memory_space=pltpu.VMEM)
    smem = pl.BlockSpec(memory_space=pltpu.SMEM)
    field = jax.ShapeDtypeStruct(flat, F32)
    buffer = pltpu.VMEM((DEVICES * 8, 128), F32)
    places, spin = pl.pallas_call(
        kernel,
        name="spinners",
        out_shape=(field, field),
        in_specs=[vmem, vmem, smem, smem] + [pl.BlockSpec(memory_space=pl.ANY)] * len(tables),
        out_specs=(vmem, vmem),
        scratch_shapes=[
            pltpu.VMEM(flat, F32),
            pltpu.VMEM((7, CELLS, SLOT), F32),
            pltpu.VMEM((STEPS - 1, 3, CELLS, SLOT), F32),
            pltpu.VMEM((6, CELLS, SLOT), F32),
            pltpu.VMEM((CELLS * A_PITCH, SLOT), F32),
            pltpu.VMEM((CELLS // GROUP, SLOT, SLOT), BF16),
            pltpu.VMEM((7, CELLS * B_PITCH, SLOT), F32),
            pltpu.VMEM((7, CELLS * L_PITCH, SLOT), F32),
            pltpu.VMEM((CELLS * T_PITCH, SLOT), F32),
            pltpu.VMEM((2, 7, HALF, SLOT), F32),
            pltpu.VMEM((2, 7, CELLS, SLOT), F32),
            pltpu.VMEM((STEPS - 1, 2, 3, HALF, SLOT), F32),
            pltpu.VMEM((STEPS - 1, 2, 3, CELLS, SLOT), F32),
            pltpu.SemaphoreType.DMA((STEPS, 4)),
            pltpu.SemaphoreType.DMA((STEPS, 4)),
            pltpu.SemaphoreType.REGULAR((3,)),
        ]
        + [pltpu.VMEM(t.shape, t.dtype) for t in tables]
        + [
            pltpu.SemaphoreType.DMA((len(tables),)),
            pltpu.VMEM((3, GRID, 128), F32),
            pltpu.VMEM((HALF, 128, SLOT), BF16),
            pltpu.VMEM((HALF, 128, SLOT), BF16),
            pltpu.VMEM((CELLS * 8, SLOT), F32),
            buffer,
            buffer,
            buffer,
            buffer,
            pltpu.VMEM((3, 128, 256), F32),
            pltpu.VMEM((3, CELLS * 8, SLOT), F32),
            pltpu.SemaphoreType.DMA((2,)),
            pltpu.SemaphoreType.DMA((2,)),
            pltpu.SemaphoreType.DMA((2,)),
        ],
        compiler_params=pltpu.CompilerParams(collective_id=0, has_side_effects=True),
    )(positions.reshape(flat), torques.reshape(flat), counts, neighbour_flags, *tables)
    return places.reshape(shape), spin.reshape(shape)


def solution(mesh):
    in_specs = (
        P(None, "row", "col", None, None),
        P(None, "row", "col", None, None),
        P("row", "col", None),
        P(None, "row", "col", None),
    )
    out_specs = (P(None, "row", "col", None, None), P(None, "row", "col", None, None))
    return jax.shard_map(shards, mesh=mesh, in_specs=in_specs, out_specs=out_specs, check_vma=False)
```

```python
import math

import jax
import jax.numpy as jnp
import numpy as np
from jax import lax
from jax.experimental import pallas as pl
from jax.experimental.pallas import tpu as pltpu
from jax.sharding import PartitionSpec as P

GRID = 128
CELL = 8
SLOT = 128
STEPS = 3
ROWS = 8
COLS = 16
DEVICES = ROWS * COLS
CELLS = 32
HALF = 16
MESH = pl.DeviceIdType.MESH
LOGICAL = pl.DeviceIdType.LOGICAL
F32 = jnp.float32
BF16 = jnp.bfloat16

KAPPA = 2.0 / (CELL * CELL) * math.log2(math.e)
PACE = 0.06 * CELL
DRIFT = 1.0 / SLOT
COUPLE = 0.5 / SLOT
MID = 0.5 * CELL

A_ROWS = 32
GROUP = SLOT // A_ROWS
GROUPS = CELLS // GROUP
B_ROWS = 16
L_ROWS = 16
A_PITCH = A_ROWS + 1
B_PITCH = B_ROWS + 1
L_PITCH = L_ROWS + 1
T_PITCH = 9


def halves(table):
    high = table.astype(np.float32).astype(jnp.bfloat16)
    low = (table - high.astype(np.float64)).astype(np.float32).astype(jnp.bfloat16)
    return high, low


def make_tables():
    n = np.arange(GRID)
    level = np.where(n == 1, 64, n // 2)
    angle = 2.0 * np.pi * (level[:, None] * n[None, :] % GRID) / GRID
    cosine, sine = np.cos(angle), np.sin(angle)
    even = (n % 2 == 0)[:, None]
    whole = (n < 2)[:, None]
    basis_xy = np.where(whole | even, cosine, sine)
    basis_z = np.where(whole | ~even, cosine, sine)
    count = np.where(n < 2, 1.0, 2.0)[:, None]
    back_xy, back_z = (basis_xy * count).T, (basis_z * count).T

    def wave(a, b, period_a, period_b):
        return 2.0 * np.pi * ((a * b[0] % period_a) / period_a + (b[1] % period_b) / period_b)

    r, q = n // 16, n % 16
    turn_l = 2.0 * np.pi * ((r[:, None] * r[None, :] % 8) / 8 + (q[:, None] * q[None, :] % 16) / 16)
    s, t = n // 8, n % 8
    turn_r = 2.0 * np.pi * ((s[:, None] * s[None, :] % 16) / 16 + (t[:, None] * t[None, :] % 8) / 8)
    twist = 2.0 * np.pi * (r[:, None] * s[None, :] + q[:, None] * t[None, :]) / GRID
    cl, sl = np.cos(turn_l), np.sin(turn_l)
    cr, sr = np.cos(turn_r), np.sin(turn_r)
    left = np.concatenate([cl, -sl], 0)
    left_back = np.concatenate([cl, -sl], 1)
    right = np.block([[cr, -sr], [sr, cr]])
    right_back = np.block([[cr, sr], [-sr, cr]])
    along_z = [half for table in (basis_xy, basis_z, back_xy, back_z) for half in halves(table)]
    out = [np.stack(along_z)] + [np.stack(halves(table)) for table in (left, left_back, right, right_back)]
    return out + [np.stack([np.cos(twist), np.sin(twist)]).astype(np.float32)]


def cut(v):
    h = v.astype(BF16)
    return h, (v - h.astype(F32)).astype(BF16)


def mul(a, b):
    return jnp.dot(a, b, preferred_element_type=F32)


def mul_t(a, b):
    return lax.dot_general(a, b, (((1,), (1,)), ((), ())), preferred_element_type=F32)


def table_left(high, low, v):
    vh, vl = cut(v)
    return mul(high, vh) + (mul(low, vh) + mul(high, vl))


def table_right(v, high, low):
    vh, vl = cut(v)
    return mul(vh, high) + (mul(vl, high) + mul(vh, low))


def narrow(v):
    return v.astype(BF16).astype(F32)


def split3(v):
    h = narrow(v)
    r = v - h
    m = narrow(r)
    return h, m, r - m


def put(ref, lead, start, stride, val):
    ref[lead, pl.ds(start, val.shape[0], stride=stride), :] = val


def put_receiver(afeat, half, px, py, pz):
    base = half * HALF * A_PITCH

    def row(k, v):
        afeat[pl.ds(base + k, HALF, stride=A_PITCH), :] = v

    size = split3(-KAPPA * (px * px + py * py + pz * pz))
    for d, v in enumerate((px, py, pz)):
        h, m, l = split3(v * (2.0 * KAPPA))
        row(d, h)
        row(8 + d, h)
        row(11 + d, h)
        row((7, 14, 15)[d], l)
        row(16 + d, m)
        row(24 + d, m)
    row(6, size[0])
    row(16 + 6, size[1])


def put_source(bfeat, lfeat, slot, half, place, torque, fill, shift, gate):
    place = [place[d] + shift[d] if shift[d] != 0.0 else place[d] for d in range(3)]
    x, y, z = place
    base = half * HALF * B_PITCH
    for d in range(3):
        h, m, l = split3(place[d])
        put(bfeat, slot, base + d, B_PITCH, h)
        put(bfeat, slot, base + 8 + d, B_PITCH, m)
        put(bfeat, slot, base + 11 + d, B_PITCH, l)
        put(bfeat, slot, base + (7, 14, 15)[d], B_PITCH, h)
    for k, v in enumerate(split3(-KAPPA * (x * x + y * y + z * z))):
        put(bfeat, slot, base + 3 + k, B_PITCH, v)
    if gate is not None:
        torque = [t * gate for t in torque]
        fill = fill * gate
    tx, ty, tz = torque
    loads = (tx, ty, tz, ty * z - tz * y, tz * x - tx * z, tx * y - ty * x)
    base = half * HALF * L_PITCH
    for q, v in enumerate(loads):
        h = narrow(v)
        put(lfeat, slot, base + q, L_PITCH, h)
        put(lfeat, slot, base + 8 + q, L_PITCH, v - h)
    put(lfeat, slot, base + 6, L_PITCH, fill)


def kernel(
    pos_in, tor_in, cnt, flg, z_far, lf_far, lb_far, rf_far, rb_far, twist_far, pos_out, spin,
    near_out, state, places, gates, afeat, trans, bfeat, lfeat, totals, totals_z, totals_x,
    full_x, full_y, part_x, part_y, send_sem, recv_sem, tell,
    z_tab, lf, lb, rf, rb, twist, table_sem,
    grid, plan_h, plan_l, depth, out_1, in_1, out_2, in_2, work, far, all_send, all_recv, self_sem,
):
    row = lax.axis_index("row")
    col = lax.axis_index("col")
    peers = (
        (lax.rem(row + 1, ROWS), col),
        (lax.rem(row + ROWS - 1, ROWS), col),
        (row, lax.rem(col + 1, COLS)),
        (row, lax.rem(col + COLS - 1, COLS)),
    )
    barrier = pltpu.get_barrier_semaphore()
    for peer in peers:
        pl.semaphore_signal(barrier, inc=1, device_id=peer, device_id_type=MESH)

    tables = [
        pltpu.make_async_copy(src, dst, table_sem.at[k])
        for k, (src, dst) in enumerate(
            ((z_far, z_tab), (lf_far, lf), (lb_far, lb), (rf_far, rf), (rb_far, rb), (twist_far, twist))
        )
    ]
    for table in tables:
        table.start()

    def inform(k, steps):
        for down, right in steps:
            where = (lax.rem(row + down + ROWS, ROWS), lax.rem(col + right + COLS, COLS))
            pl.semaphore_signal(tell.at[k], inc=1, device_id=where, device_id_type=MESH)

    def learn(step):
        if step == 0:
            inform(0, ((2, 0), (-2, 0), (0, 2), (0, -2)))
        elif step == 1:
            pl.semaphore_wait(tell.at[0], 4)
            inform(1, ((0, 4), (0, -4)))
        else:
            pl.semaphore_wait(tell.at[1], 2)
            inform(2, [(k, 0) for k in range(1, ROWS)])

    lane = lax.broadcasted_iota(jnp.int32, (1, SLOT), 1)

    def spread_scalars(z, carry):
        for h in range(2):
            state[6, pl.ds(h * HALF + z, 1), :] = (lane < cnt[h, 0, z]).astype(F32)
            for f in range(6):
                gates[f, pl.ds(h * HALF + z, 1), :] = jnp.full((1, SLOT), flg[f, h, 0, z], jnp.int32).astype(F32)
        return carry

    lax.fori_loop(0, HALF, spread_scalars, 0)
    fill = state[6]
    for d in range(3):
        state[d] = pos_in[d] - MID
        state[3 + d] = tor_in[d] * fill

    pl.semaphore_wait(barrier, 4)

    def halo(step):
        if step == 0:
            own, into_x, into_y = state, full_x, full_y
        else:
            own, into_x, into_y = places.at[step - 1], part_x.at[step - 1], part_y.at[step - 1]
        moves = (
            (own.at[:, pl.ds(HALF, HALF), :], into_x.at[0], 0),
            (own.at[:, pl.ds(0, HALF), :], into_x.at[1], 1),
            (own, into_y.at[0], 2),
            (own, into_y.at[1], 3),
        )
        copies = []
        for src, dst, k in moves:
            copies.append(
                pltpu.make_async_remote_copy(
                    src_ref=src,
                    dst_ref=dst,
                    send_sem=send_sem.at[step, k],
                    recv_sem=recv_sem.at[step, k],
                    device_id=peers[k],
                    device_id_type=MESH,
                )
            )
        return copies

    one = jnp.ones((CELLS, SLOT), F32)
    zero = jnp.zeros((CELLS, SLOT), F32)
    for k in (19, 20, 21, 23, 27, 28, 29, 30, 31):
        afeat[pl.ds(k, CELLS, stride=A_PITCH), :] = zero
    for k in (3, 4, 5):
        afeat[pl.ds(k, CELLS, stride=A_PITCH), :] = one
    totals_x[pl.ds(0, HALF * T_PITCH), :] = jnp.zeros((HALF * T_PITCH, SLOT), F32)
    for e in range(7):
        put(bfeat, e, 6, B_PITCH, one)
        for k in (7, 14, 15):
            put(lfeat, e, k, L_PITCH, zero)

    owner = lax.broadcasted_iota(jnp.int32, (SLOT, SLOT), 1) // A_ROWS

    def wide(ref, n, cell, faces):
        blocks = [ref[e, pl.ds(cell * (n + 1), n), :] for e in faces]
        return (blocks[0] if len(blocks) == 1 else jnp.concatenate(blocks, 1)).astype(BF16)

    def powers(group, faces):
        block = trans[group]
        ats = [jnp.where(owner == k, block, jnp.zeros_like(block)) for k in range(GROUP)]
        b = []
        for k in range(GROUP):
            part = wide(bfeat, B_ROWS, group * GROUP + k, faces)
            b += [part, part]
        return jnp.dot(jnp.concatenate(ats, 0), jnp.concatenate(b, 0), preferred_element_type=F32)

    def add_up(load, w, side):
        acc = lax.dot_general(load, w, (((1,), (side,)), ((), ())), preferred_element_type=F32)
        return acc[0:8] + acc[8:16]

    def inner_group(group, faces, into, power):
        for k in range(GROUP):
            cell = group * GROUP + k
            w = jnp.exp2(power[k * SLOT : (k + 1) * SLOT]).astype(BF16)
            into[pl.ds(cell * T_PITCH, 8), :] = add_up(wide(lfeat, L_ROWS, cell, faces), w, 1)
            for n, e in enumerate(faces):
                if e == 1:
                    upper = (cell // HALF) * HALF + (cell + 1) % HALF
                    load = wide(lfeat, L_ROWS, upper, (2,))
                    totals_z[pl.ds(upper * T_PITCH, 8), :] = add_up(load, w[:, n * SLOT : (n + 1) * SLOT], 0)
                if e == 3:
                    load = wide(lfeat, L_ROWS, cell + HALF, (3,))
                    totals_x[pl.ds((cell + HALF) * T_PITCH, 8), :] = add_up(load, w[:, n * SLOT : (n + 1) * SLOT], 0)

    def inner_faces(i, carry):
        low, high = powers(i, (0, 1, 3)), powers(i + GROUPS // 2, (0, 1))
        inner_group(i, (0, 1, 3), totals, low)
        inner_group(i + GROUPS // 2, (0, 1), totals, high)
        for g in (i, i + GROUPS // 2):
            turn_receivers(jnp.minimum(g + 1, GROUPS - 1))
        return carry

    def turn_receivers(group):
        rows = [afeat[pl.ds((group * GROUP + k) * A_PITCH, A_ROWS), :] for k in range(GROUP)]
        trans[group] = jnp.concatenate(rows, 0).T.astype(BF16)

    def outer_faces(i, carry):
        both = [powers(i + g * (GROUPS // 2), (4, 5, 6)) for g in range(2)]
        for cell, power, k in [((i + g * (GROUPS // 2)) * GROUP + k, both[g], k) for g in range(2) for k in range(GROUP)]:
            w = jnp.exp2(power[k * SLOT : (k + 1) * SLOT]).astype(BF16)
            spot = pl.ds(cell * T_PITCH, 8)
            totals[spot, :] = totals[spot, :] + add_up(wide(lfeat, L_ROWS, cell, (4, 5, 6)), w, 1)
        return carry

    for step in range(STEPS):
        copies = halo(step)
        for copy in copies:
            copy.start()
        here = state if step == 0 else places.at[step - 1]
        for h in range(2):
            part = slice(h * HALF, (h + 1) * HALF)
            other = slice((1 - h) * HALF, (2 - h) * HALF)
            place = [here[d, part, :] for d in range(3)]
            torque = [state[3 + d, part, :] for d in range(3)]
            fill = state[6, part, :]
            put_receiver(afeat, h, *place)
            put_source(bfeat, lfeat, 0, h, place, torque, fill, (0.0, 0.0, 0.0), None)
            for slot, turn, lift, face in ((1, HALF - 1, CELL, 4), (2, 1, -CELL, 5)):
                def turned(v):
                    return pltpu.roll(v, turn, 0)

                put_source(
                    bfeat, lfeat, slot, h, [turned(v) for v in place], [turned(v) for v in torque], turned(fill),
                    (0.0, 0.0, float(lift)), gates[face, part, :],
                )
            put_source(
                bfeat, lfeat, 3, h,
                [here[d, other, :] for d in range(3)],
                [state[3 + d, other, :] for d in range(3)],
                state[6, other, :],
                (float(CELL) if h == 0 else -float(CELL), 0.0, 0.0),
                gates[0 if h == 0 else 1, part, :],
            )
        turn_receivers(0)
        turn_receivers(GROUPS // 2)
        lax.fori_loop(0, GROUPS // 2, inner_faces, 0)
        for copy in copies:
            copy.wait_recv()
        learn(step)
        for h in range(2):
            part = slice(h * HALF, (h + 1) * HALF)
            near_x = full_x if step == 0 else part_x.at[step - 1]
            near_y = full_y if step == 0 else part_y.at[step - 1]
            put_source(
                bfeat, lfeat, 4, h,
                [near_x[h, d] for d in range(3)],
                [full_x[h, 3 + d] for d in range(3)],
                full_x[h, 6],
                (-float(CELL) if h == 0 else float(CELL), 0.0, 0.0),
                gates[1 if h == 0 else 0, part, :],
            )
            for slot, side, lift, face in ((5, 1, CELL, 2), (6, 0, -CELL, 3)):
                put_source(
                    bfeat, lfeat, slot, h,
                    [near_y[side, d, part, :] for d in range(3)],
                    [full_y[side, 3 + d, part, :] for d in range(3)],
                    full_y[side, 6, part, :],
                    (0.0, float(lift), 0.0),
                    gates[face, part, :],
                )
        lax.fori_loop(0, GROUPS // 2, outer_faces, 0)

        tot = []
        for q in range(7):
            rows = pl.ds(q, CELLS, stride=T_PITCH)
            tot.append(totals[rows, :] + totals_z[rows, :] + totals_x[rows, :])
        fill = state[6]
        x, y, z = (here[d] for d in range(3))
        speed = (
            tot[1] * z - tot[2] * y - tot[3],
            tot[2] * x - tot[0] * z - tot[4],
            tot[0] * y - tot[1] * x - tot[5],
        )
        for d in range(3):
            moved = here[d] + PACE * (DRIFT * speed[d] * fill)
            if step < STEPS - 1:
                places[step, d] = moved
            else:
                pos_out[d] = moved + MID
                torque = tor_in[d]
                near_out[d] = (torque + COUPLE * (tot[d] - tot[6] * torque)) * fill

    me = row * COLS + col

    def peer(k):
        p = me + k
        return jnp.where(p >= DEVICES, p - DEVICES, p)

    level = lax.broadcasted_iota(jnp.int32, (CELL, SLOT), 0).astype(F32) + 0.5
    low_lane = lax.broadcasted_iota(jnp.int32, (24, SLOT), 1) < 64

    for table in tables:
        table.wait()

    def bins(d, cell):
        apart = pos_out[d, pl.ds(cell, 1), :] - level
        return jnp.exp(-apart * apart)

    def spread(z, carry):
        planar, lifted, rest = [], [], []
        for h in range(2):
            cell = h * HALF + z
            bx, by, bz = (bins(d, cell) for d in range(3))
            depth[pl.ds(pl.multiple_of(cell * 8, 8), 8), :] = bz
            planar += [bx[a : a + 1, :] * by for a in range(CELL)]
            lift = [state[3 + c, pl.ds(cell, 1), :] * bz for c in range(3)]
            top = [narrow(v) for v in lift]
            lifted += top
            rest += [v - t for v, t in zip(lift, top)]
        ph, pl_ = cut(jnp.concatenate(planar, 0))
        plan_h[z] = ph
        plan_l[z] = pl_
        both = mul_t(jnp.concatenate(lifted + rest, 0).astype(BF16), ph)
        more = mul_t(jnp.concatenate(lifted, 0).astype(BF16), pl_)
        sums = both[0:48] + both[48:96] + more
        block = jnp.where(low_lane, sums[0:24], sums[24:48])
        for c in range(3):
            grid[c, pl.ds(pl.multiple_of(z * 8, 8), 8), :] = block[c * 8 : c * 8 + 8]
        return carry

    lax.fori_loop(0, HALF, spread, 0)

    for c in range(3):
        n = 0 if c < 2 else 2
        out_1[pl.ds(c, DEVICES, stride=8), :] = table_left(z_tab[n], z_tab[n + 1], grid[c])

    pl.semaphore_wait(tell.at[2], ROWS - 1)

    def exchange(out, into, k):
        def post(i, carry):
            p = peer(i)
            pltpu.make_async_remote_copy(
                src_ref=out.at[pl.ds(pl.multiple_of(p * 8, 8), 3), :],
                dst_ref=into.at[pl.ds(pl.multiple_of(me * 8, 8), 3), :],
                send_sem=all_send.at[k],
                recv_sem=all_recv.at[k],
                device_id=p,
                device_id_type=LOGICAL,
            ).start()
            return carry

        lax.fori_loop(1, DEVICES, post, 0, unroll=9)
        mine = pl.ds(pl.multiple_of(me * 8, 8), 3)
        keep = pltpu.make_async_copy(out.at[mine, :], into.at[mine, :], self_sem.at[k])
        keep.start()
        keep.wait()
        bulk = out.at[pl.ds(0, 3 * (DEVICES - 1)), :]
        pltpu.make_async_copy(bulk, bulk, all_recv.at[k]).wait()

    exchange(out_1, in_1, 0)

    cos_t, sin_t = twist[0], twist[1]
    for c in range(3):
        both = table_left(lf[0], lf[1], in_1[pl.ds(c, DEVICES, stride=8), :])
        re, im = both[0:128], both[128:256]
        work[c, :, 0:128] = re * cos_t + im * sin_t
        work[c, :, 128:256] = im * cos_t - re * sin_t
    for c in range(3):
        work[c] = table_right(work[c], rf[0], rf[1])

    special = me < 2
    plain = jnp.where(special, 1.0, 0.0).astype(F32)
    turn = jnp.where(special, 0, 2 * lax.rem(me, 2) - 1).astype(F32)
    kz = jnp.where(me == 1, -64, me // 2).astype(F32)
    kz_top = jnp.where(me == 1, -64, 0).astype(F32)
    kz_low = jnp.where(me == 1, 0, me // 2).astype(F32)

    def signed(v):
        return jnp.where(v < GRID // 2, v, v - GRID)

    def stokes(i, carry):
        rows = pl.ds(pl.multiple_of(i * 16, 16), 16)
        f1 = lax.broadcasted_iota(jnp.int32, (16, 128), 0) + i * 16
        f2 = lax.broadcasted_iota(jnp.int32, (16, 128), 1)
        ix = signed(f1 // 16 + 8 * (f2 // 8))
        iy = signed(f1 % 16 + 16 * (f2 % 8))
        kx, ky = ix.astype(F32), iy.astype(F32)
        kx_top = jnp.where(ix == -64, kx, 0.0)
        ky_top = jnp.where(iy == -64, ky, 0.0)
        kx_low, ky_low = kx - kx_top, ky - ky_top
        square = kx * kx + ky * ky + kz * kz
        damping = (0.25 / GRID**3) * jnp.exp(square * (-((math.pi / GRID) ** 2)))
        inverse = 1.0 / jnp.maximum(square, 1.0)
        w_re, w_im = work[2, rows, 0:128], work[2, rows, 128:256]
        sides = (
            (work[0, rows, 0:128], work[1, rows, 0:128], plain * w_re - turn * w_im),
            (work[0, rows, 128:256], work[1, rows, 128:256], plain * w_im + turn * w_re),
        )
        done = []
        for u, v, w in sides:
            low = (kx_low * u + ky_low * v + kz_low * w) * inverse
            top = (kx_top * u + ky_top * v + kz_top * w) * inverse
            done.append(
                (
                    damping * (u - kx_low * low - kx_top * top),
                    damping * (v - ky_low * low - ky_top * top),
                    damping * (w - kz_low * low - kz_top * top),
                )
            )
        for c in range(2):
            work[c, rows, 0:128] = done[0][c]
            work[c, rows, 128:256] = done[1][c]
        work[2, rows, 0:128] = plain * done[0][2] + turn * done[1][2]
        work[2, rows, 128:256] = plain * done[1][2] - turn * done[0][2]
        return carry

    lax.fori_loop(0, 8, stokes, 0)

    for c in range(3):
        both = table_right(work[c], rb[0], rb[1])
        re, im = both[:, 0:128], both[:, 128:256]
        pair = jnp.concatenate([re * cos_t - im * sin_t, im * cos_t + re * sin_t], 0)
        out_2[pl.ds(c, DEVICES, stride=8), :] = table_left(lb[0], lb[1], pair)

    exchange(out_2, in_2, 1)

    for c in range(3):
        n = 4 if c < 2 else 6
        grid[c] = table_left(z_tab[n], z_tab[n + 1], in_2[pl.ds(c, DEVICES, stride=8), :])

    def gather(z, carry):
        rows = pl.ds(pl.multiple_of(z * 8, 8), 8)
        block = jnp.concatenate([grid[c, rows, :] for c in range(3)], 0)
        near_half = jnp.where(low_lane, block, 0.0)
        far_half = block - near_half
        both = jnp.concatenate([near_half, far_half], 0)
        top = narrow(both)
        first = mul(jnp.concatenate([top, both - top], 0).astype(BF16), plan_h[z])
        second = mul(top.astype(BF16), plan_l[z])
        sums = first[0:48] + first[48:96] + second
        for h in range(2):
            spot = pl.ds(pl.multiple_of((h * HALF + z) * 8, 8), 8)
            bz = depth[spot, :]
            for c in range(3):
                far[c, spot, :] = sums[h * 24 + c * 8 : h * 24 + c * 8 + 8] * bz
        return carry

    lax.fori_loop(0, HALF, gather, 0)

    for c in range(3):
        total = far[c, pl.ds(0, CELLS, stride=8), :]
        for g in range(1, CELL):
            total = total + far[c, pl.ds(g, CELLS, stride=8), :]
        spin[c] = near_out[c] + total * state[6]

    for k in range(2):
        bulk = out_1.at[pl.ds(0, 3 * (DEVICES - 1)), :]
        pltpu.make_async_copy(bulk, bulk, all_send.at[k]).wait()
    for step in range(STEPS):
        for copy in halo(step):
            copy.wait_send()
def shards(positions, torques, counts, neighbour_flags):
    shape = positions.shape
    flat = (3, CELLS, SLOT)
    tables = [jnp.asarray(t) for t in make_tables()]
    vmem = pl.BlockSpec(memory_space=pltpu.VMEM)
    smem = pl.BlockSpec(memory_space=pltpu.SMEM)
    field = jax.ShapeDtypeStruct(flat, F32)
    buffer = pltpu.VMEM((DEVICES * 8, 128), F32)
    places, spin = pl.pallas_call(
        kernel,
        name="spinners",
        out_shape=(field, field),
        in_specs=[vmem, vmem, smem, smem] + [pl.BlockSpec(memory_space=pl.ANY)] * len(tables),
        out_specs=(vmem, vmem),
        scratch_shapes=[
            pltpu.VMEM(flat, F32),
            pltpu.VMEM((7, CELLS, SLOT), F32),
            pltpu.VMEM((STEPS - 1, 3, CELLS, SLOT), F32),
            pltpu.VMEM((6, CELLS, SLOT), F32),
            pltpu.VMEM((CELLS * A_PITCH, SLOT), F32),
            pltpu.VMEM((CELLS // GROUP, SLOT, SLOT), BF16),
            pltpu.VMEM((7, CELLS * B_PITCH, SLOT), F32),
            pltpu.VMEM((7, CELLS * L_PITCH, SLOT), F32),
            pltpu.VMEM((CELLS * T_PITCH, SLOT), F32),
            pltpu.VMEM((CELLS * T_PITCH, SLOT), F32),
            pltpu.VMEM((CELLS * T_PITCH, SLOT), F32),
            pltpu.VMEM((2, 7, HALF, SLOT), F32),
            pltpu.VMEM((2, 7, CELLS, SLOT), F32),
            pltpu.VMEM((STEPS - 1, 2, 3, HALF, SLOT), F32),
            pltpu.VMEM((STEPS - 1, 2, 3, CELLS, SLOT), F32),
            pltpu.SemaphoreType.DMA((STEPS, 4)),
            pltpu.SemaphoreType.DMA((STEPS, 4)),
            pltpu.SemaphoreType.REGULAR((3,)),
        ]
        + [pltpu.VMEM(t.shape, t.dtype) for t in tables]
        + [
            pltpu.SemaphoreType.DMA((len(tables),)),
            pltpu.VMEM((3, GRID, 128), F32),
            pltpu.VMEM((HALF, 128, SLOT), BF16),
            pltpu.VMEM((HALF, 128, SLOT), BF16),
            pltpu.VMEM((CELLS * 8, SLOT), F32),
            buffer,
            buffer,
            buffer,
            buffer,
            pltpu.VMEM((3, 128, 256), F32),
            pltpu.VMEM((3, CELLS * 8, SLOT), F32),
            pltpu.SemaphoreType.DMA((2,)),
            pltpu.SemaphoreType.DMA((2,)),
            pltpu.SemaphoreType.DMA((2,)),
        ],
        compiler_params=pltpu.CompilerParams(collective_id=0, has_side_effects=True),
    )(positions.reshape(flat), torques.reshape(flat), counts, neighbour_flags, *tables)
    return places.reshape(shape), spin.reshape(shape)


def solution(mesh):
    in_specs = (
        P(None, "row", "col", None, None),
        P(None, "row", "col", None, None),
        P("row", "col", None),
        P(None, "row", "col", None),
    )
    out_specs = (P(None, "row", "col", None, None), P(None, "row", "col", None, None))
    return jax.shard_map(shards, mesh=mesh, in_specs=in_specs, out_specs=out_specs, check_vma=False)
```

```python
import math

import jax
import jax.numpy as jnp
import numpy as np
from jax import lax
from jax.experimental import pallas as pl
from jax.experimental.pallas import tpu as pltpu
from jax.sharding import PartitionSpec as P

GRID = 128
CELL = 8
SLOT = 128
STEPS = 3
ROWS = 8
COLS = 16
DEVICES = ROWS * COLS
BUNCH = 8
CELLS = 32
HALF = 16
MESH = pl.DeviceIdType.MESH
LOGICAL = pl.DeviceIdType.LOGICAL
F32 = jnp.float32
BF16 = jnp.bfloat16

KAPPA = 2.0 / (CELL * CELL) * math.log2(math.e)
PACE = 0.06 * CELL
DRIFT = 1.0 / SLOT
COUPLE = 0.5 / SLOT
MID = 0.5 * CELL

A_ROWS = 32
GROUP = SLOT // A_ROWS
GROUPS = CELLS // GROUP
B_ROWS = 16
L_ROWS = 16
A_PITCH = A_ROWS + 1
B_PITCH = B_ROWS + 1
L_PITCH = L_ROWS + 1
T_PITCH = 9


def halves(table):
    high = table.astype(np.float32).astype(jnp.bfloat16)
    low = (table - high.astype(np.float64)).astype(np.float32).astype(jnp.bfloat16)
    return high, low


def make_tables():
    n = np.arange(GRID)
    level = np.where(n == 1, 64, n // 2)
    angle = 2.0 * np.pi * (level[:, None] * n[None, :] % GRID) / GRID
    cosine, sine = np.cos(angle), np.sin(angle)
    even = (n % 2 == 0)[:, None]
    whole = (n < 2)[:, None]
    basis_xy = np.where(whole | even, cosine, sine)
    basis_z = np.where(whole | ~even, cosine, sine)
    count = np.where(n < 2, 1.0, 2.0)[:, None]
    back_xy, back_z = (basis_xy * count).T, (basis_z * count).T

    def wave(a, b, period_a, period_b):
        return 2.0 * np.pi * ((a * b[0] % period_a) / period_a + (b[1] % period_b) / period_b)

    r, q = n // 16, n % 16
    turn_l = 2.0 * np.pi * ((r[:, None] * r[None, :] % 8) / 8 + (q[:, None] * q[None, :] % 16) / 16)
    s, t = n // 8, n % 8
    turn_r = 2.0 * np.pi * ((s[:, None] * s[None, :] % 16) / 16 + (t[:, None] * t[None, :] % 8) / 8)
    twist = 2.0 * np.pi * (r[:, None] * s[None, :] + q[:, None] * t[None, :]) / GRID
    cl, sl = np.cos(turn_l), np.sin(turn_l)
    cr, sr = np.cos(turn_r), np.sin(turn_r)
    left = np.concatenate([cl, -sl], 0)
    left_back = np.concatenate([cl, -sl], 1)
    right = np.block([[cr, -sr], [sr, cr]])
    right_back = np.block([[cr, sr], [-sr, cr]])
    along_z = [half for table in (basis_xy, basis_z, back_xy, back_z) for half in halves(table)]
    out = [np.stack(along_z)] + [np.stack(halves(table)) for table in (left, left_back, right, right_back)]
    return out + [np.stack([np.cos(twist), np.sin(twist)]).astype(np.float32)]


def cut(v):
    h = v.astype(BF16)
    return h, (v - h.astype(F32)).astype(BF16)


def mul(a, b):
    return jnp.dot(a, b, preferred_element_type=F32)


def mul_t(a, b):
    return lax.dot_general(a, b, (((1,), (1,)), ((), ())), preferred_element_type=F32)


def table_left(high, low, v):
    vh, vl = cut(v)
    return mul(high, vh) + (mul(low, vh) + mul(high, vl))


def table_right(v, high, low):
    vh, vl = cut(v)
    return mul(vh, high) + (mul(vl, high) + mul(vh, low))


def narrow(v):
    return v.astype(BF16).astype(F32)


def split3(v):
    h = narrow(v)
    r = v - h
    m = narrow(r)
    return h, m, r - m


def put(ref, lead, start, stride, val):
    ref[lead, pl.ds(start, val.shape[0], stride=stride), :] = val


def put_receiver(afeat, half, px, py, pz):
    base = half * HALF * A_PITCH

    def row(k, v):
        afeat[pl.ds(base + k, HALF, stride=A_PITCH), :] = v

    size = split3(-KAPPA * (px * px + py * py + pz * pz))
    for d, v in enumerate((px, py, pz)):
        h, m, l = split3(v * (2.0 * KAPPA))
        row(d, h)
        row(8 + d, h)
        row(11 + d, h)
        row((7, 14, 15)[d], l)
        row(16 + d, m)
        row(24 + d, m)
    row(6, size[0])
    row(16 + 6, size[1])


def put_source(bfeat, lfeat, slot, half, place, torque, fill, shift, gate):
    place = [place[d] + shift[d] if shift[d] != 0.0 else place[d] for d in range(3)]
    x, y, z = place
    base = half * HALF * B_PITCH
    for d in range(3):
        h, m, l = split3(place[d])
        put(bfeat, slot, base + d, B_PITCH, h)
        put(bfeat, slot, base + 8 + d, B_PITCH, m)
        put(bfeat, slot, base + 11 + d, B_PITCH, l)
        put(bfeat, slot, base + (7, 14, 15)[d], B_PITCH, h)
    for k, v in enumerate(split3(-KAPPA * (x * x + y * y + z * z))):
        put(bfeat, slot, base + 3 + k, B_PITCH, v)
    if gate is not None:
        torque = [t * gate for t in torque]
        fill = fill * gate
    tx, ty, tz = torque
    loads = (tx, ty, tz, ty * z - tz * y, tz * x - tx * z, tx * y - ty * x)
    base = half * HALF * L_PITCH
    for q, v in enumerate(loads):
        h = narrow(v)
        put(lfeat, slot, base + q, L_PITCH, h)
        put(lfeat, slot, base + 8 + q, L_PITCH, v - h)
    put(lfeat, slot, base + 6, L_PITCH, fill)


def kernel(
    pos_in, tor_in, cnt, flg, z_far, lf_far, lb_far, rf_far, rb_far, twist_far, pos_out, spin,
    near_out, state, places, gates, afeat, trans, bfeat, lfeat, totals, totals_z, totals_x,
    full_x, full_y, part_x, part_y, send_sem, recv_sem, tell,
    z_tab, lf, lb, rf, rb, twist, table_sem,
    grid, plan_h, plan_l, depth, out_1, in_1, out_2, in_2, work, far, all_send, all_recv, self_sem,
):
    row = lax.axis_index("row")
    col = lax.axis_index("col")
    peers = (
        (lax.rem(row + 1, ROWS), col),
        (lax.rem(row + ROWS - 1, ROWS), col),
        (row, lax.rem(col + 1, COLS)),
        (row, lax.rem(col + COLS - 1, COLS)),
    )
    barrier = pltpu.get_barrier_semaphore()
    for peer in peers:
        pl.semaphore_signal(barrier, inc=1, device_id=peer, device_id_type=MESH)

    tables = [
        pltpu.make_async_copy(src, dst, table_sem.at[k])
        for k, (src, dst) in enumerate(
            ((z_far, z_tab), (lf_far, lf), (lb_far, lb), (rf_far, rf), (rb_far, rb), (twist_far, twist))
        )
    ]
    for table in tables:
        table.start()

    def inform(k, steps):
        for down, right in steps:
            where = (lax.rem(row + down + ROWS, ROWS), lax.rem(col + right + COLS, COLS))
            pl.semaphore_signal(tell.at[k], inc=1, device_id=where, device_id_type=MESH)

    def learn(step):
        if step == 0:
            inform(0, ((2, 0), (-2, 0), (0, 2), (0, -2)))
        elif step == 1:
            pl.semaphore_wait(tell.at[0], 4)
            inform(1, ((0, 4), (0, -4)))
        else:
            pl.semaphore_wait(tell.at[1], 2)
            inform(2, [(k, 0) for k in range(1, ROWS)])

    lane = lax.broadcasted_iota(jnp.int32, (1, SLOT), 1)

    def spread_scalars(z, carry):
        for h in range(2):
            state[6, pl.ds(h * HALF + z, 1), :] = (lane < cnt[h, 0, z]).astype(F32)
            for f in range(6):
                gates[f, pl.ds(h * HALF + z, 1), :] = jnp.full((1, SLOT), flg[f, h, 0, z], jnp.int32).astype(F32)
        return carry

    lax.fori_loop(0, HALF, spread_scalars, 0)
    fill = state[6]
    for d in range(3):
        state[d] = pos_in[d] - MID
        state[3 + d] = tor_in[d] * fill

    pl.semaphore_wait(barrier, 4)

    def halo(step):
        if step == 0:
            own, into_x, into_y = state, full_x, full_y
        else:
            own, into_x, into_y = places.at[step - 1], part_x.at[step - 1], part_y.at[step - 1]
        moves = (
            (own.at[:, pl.ds(HALF, HALF), :], into_x.at[0], 0),
            (own.at[:, pl.ds(0, HALF), :], into_x.at[1], 1),
            (own, into_y.at[0], 2),
            (own, into_y.at[1], 3),
        )
        copies = []
        for src, dst, k in moves:
            copies.append(
                pltpu.make_async_remote_copy(
                    src_ref=src,
                    dst_ref=dst,
                    send_sem=send_sem.at[step, k],
                    recv_sem=recv_sem.at[step, k],
                    device_id=peers[k],
                    device_id_type=MESH,
                )
            )
        return copies

    one = jnp.ones((CELLS, SLOT), F32)
    zero = jnp.zeros((CELLS, SLOT), F32)
    for k in (19, 20, 21, 23, 27, 28, 29, 30, 31):
        afeat[pl.ds(k, CELLS, stride=A_PITCH), :] = zero
    for k in (3, 4, 5):
        afeat[pl.ds(k, CELLS, stride=A_PITCH), :] = one
    totals_x[pl.ds(0, HALF * T_PITCH), :] = jnp.zeros((HALF * T_PITCH, SLOT), F32)
    for e in range(7):
        put(bfeat, e, 6, B_PITCH, one)
        for k in (7, 14, 15):
            put(lfeat, e, k, L_PITCH, zero)

    owner = lax.broadcasted_iota(jnp.int32, (SLOT, SLOT), 1) // A_ROWS

    def wide(ref, n, cell, faces):
        blocks = [ref[e, pl.ds(cell * (n + 1), n), :] for e in faces]
        return (blocks[0] if len(blocks) == 1 else jnp.concatenate(blocks, 1)).astype(BF16)

    def powers(group, faces):
        block = trans[group]
        ats = [jnp.where(owner == k, block, jnp.zeros_like(block)) for k in range(GROUP)]
        b = []
        for k in range(GROUP):
            part = wide(bfeat, B_ROWS, group * GROUP + k, faces)
            b += [part, part]
        return jnp.dot(jnp.concatenate(ats, 0), jnp.concatenate(b, 0), preferred_element_type=F32)

    def add_up(load, w, side):
        acc = lax.dot_general(load, w, (((1,), (side,)), ((), ())), preferred_element_type=F32)
        return acc[0:8] + acc[8:16]

    def inner_cell(group, k, faces, power):
        cell = group * GROUP + k
        w = jnp.exp2(power[k * SLOT : (k + 1) * SLOT]).astype(BF16)
        totals[pl.ds(cell * T_PITCH, 8), :] = add_up(wide(lfeat, L_ROWS, cell, faces), w, 1)
        upper = (cell // HALF) * HALF + (cell + 1) % HALF
        load = wide(lfeat, L_ROWS, upper, (2,))
        if len(faces) == 2:
            totals_z[pl.ds(upper * T_PITCH, 8), :] = add_up(load, w[:, SLOT:], 0)
        else:
            load = jnp.concatenate([load, wide(lfeat, L_ROWS, cell + HALF, (3,))], 0)
            acc = lax.dot_general(load, w[:, SLOT:], (((1,), (0,)), ((), ())), preferred_element_type=F32)
            totals_z[pl.ds(upper * T_PITCH, 8), :] = acc[0:8, 0:SLOT] + acc[8:16, 0:SLOT]
            totals_x[pl.ds((cell + HALF) * T_PITCH, 8), :] = acc[16:24, SLOT:] + acc[24:32, SLOT:]

    def inner_faces(i, carry):
        sides = ((i, (0, 1, 3)), (i + GROUPS // 2, (0, 1)))
        both = [powers(g, faces) for g, faces in sides]
        for k, n in [(k, n) for k in range(GROUP) for n in range(2)]:
            inner_cell(sides[n][0], k, sides[n][1], both[n])

        return carry

    def turn_receivers(group):
        rows = [afeat[pl.ds((group * GROUP + k) * A_PITCH, A_ROWS), :] for k in range(GROUP)]
        trans[group] = jnp.concatenate(rows, 0).T.astype(BF16)

    def outer_faces(i, carry):
        both = [powers(i + g * (GROUPS // 2), (4, 5, 6)) for g in range(2)]
        for cell, power, k in [((i + g * (GROUPS // 2)) * GROUP + k, both[g], k) for g in range(2) for k in range(GROUP)]:
            w = jnp.exp2(power[k * SLOT : (k + 1) * SLOT]).astype(BF16)
            spot = pl.ds(cell * T_PITCH, 8)
            totals[spot, :] = totals[spot, :] + add_up(wide(lfeat, L_ROWS, cell, (4, 5, 6)), w, 1)
        return carry

    for step in range(STEPS):
        copies = halo(step)
        for copy in copies:
            copy.start()
        here = state if step == 0 else places.at[step - 1]
        for h in range(2):
            part = slice(h * HALF, (h + 1) * HALF)
            other = slice((1 - h) * HALF, (2 - h) * HALF)
            place = [here[d, part, :] for d in range(3)]
            torque = [state[3 + d, part, :] for d in range(3)]
            fill = state[6, part, :]
            put_receiver(afeat, h, *place)
            put_source(bfeat, lfeat, 0, h, place, torque, fill, (0.0, 0.0, 0.0), None)
            for slot, turn, lift, face in ((1, HALF - 1, CELL, 4), (2, 1, -CELL, 5)):
                def turned(v):
                    return pltpu.roll(v, turn, 0)

                put_source(
                    bfeat, lfeat, slot, h, [turned(v) for v in place], [turned(v) for v in torque], turned(fill),
                    (0.0, 0.0, float(lift)), gates[face, part, :],
                )
            put_source(
                bfeat, lfeat, 3, h,
                [here[d, other, :] for d in range(3)],
                [state[3 + d, other, :] for d in range(3)],
                state[6, other, :],
                (float(CELL) if h == 0 else -float(CELL), 0.0, 0.0),
                gates[0 if h == 0 else 1, part, :],
            )
        for g in range(GROUPS):
            turn_receivers(g)
        lax.fori_loop(0, GROUPS // 2, inner_faces, 0)
        for copy in copies:
            copy.wait_recv()
        learn(step)
        for h in range(2):
            part = slice(h * HALF, (h + 1) * HALF)
            near_x = full_x if step == 0 else part_x.at[step - 1]
            near_y = full_y if step == 0 else part_y.at[step - 1]
            put_source(
                bfeat, lfeat, 4, h,
                [near_x[h, d] for d in range(3)],
                [full_x[h, 3 + d] for d in range(3)],
                full_x[h, 6],
                (-float(CELL) if h == 0 else float(CELL), 0.0, 0.0),
                gates[1 if h == 0 else 0, part, :],
            )
            for slot, side, lift, face in ((5, 1, CELL, 2), (6, 0, -CELL, 3)):
                put_source(
                    bfeat, lfeat, slot, h,
                    [near_y[side, d, part, :] for d in range(3)],
                    [full_y[side, 3 + d, part, :] for d in range(3)],
                    full_y[side, 6, part, :],
                    (0.0, float(lift), 0.0),
                    gates[face, part, :],
                )
        lax.fori_loop(0, GROUPS // 2, outer_faces, 0)

        tot = []
        for q in range(7):
            rows = pl.ds(q, CELLS, stride=T_PITCH)
            tot.append(totals[rows, :] + totals_z[rows, :] + totals_x[rows, :])
        fill = state[6]
        x, y, z = (here[d] for d in range(3))
        speed = (
            tot[1] * z - tot[2] * y - tot[3],
            tot[2] * x - tot[0] * z - tot[4],
            tot[0] * y - tot[1] * x - tot[5],
        )
        for d in range(3):
            moved = here[d] + PACE * (DRIFT * speed[d] * fill)
            if step < STEPS - 1:
                places[step, d] = moved
            else:
                pos_out[d] = moved + MID
                torque = tor_in[d]
                near_out[d] = (torque + COUPLE * (tot[d] - tot[6] * torque)) * fill

    me = row * COLS + col

    level = lax.broadcasted_iota(jnp.int32, (CELL, SLOT), 0).astype(F32) + 0.5
    low_lane = lax.broadcasted_iota(jnp.int32, (24, SLOT), 1) < 64

    for table in tables:
        table.wait()

    def bins(d, cell):
        apart = pos_out[d, pl.ds(cell, 1), :] - level
        return jnp.exp(-apart * apart)

    def spread(z, carry):
        planar, lifted, rest = [], [], []
        for h in range(2):
            cell = h * HALF + z
            bx, by, bz = (bins(d, cell) for d in range(3))
            depth[pl.ds(pl.multiple_of(cell * 8, 8), 8), :] = bz
            planar += [bx[a : a + 1, :] * by for a in range(CELL)]
            lift = [state[3 + c, pl.ds(cell, 1), :] * bz for c in range(3)]
            top = [narrow(v) for v in lift]
            lifted += top
            rest += [v - t for v, t in zip(lift, top)]
        ph, pl_ = cut(jnp.concatenate(planar, 0))
        plan_h[z] = ph
        plan_l[z] = pl_
        both = mul_t(jnp.concatenate(lifted + rest, 0).astype(BF16), ph)
        more = mul_t(jnp.concatenate(lifted, 0).astype(BF16), pl_)
        sums = both[0:48] + both[48:96] + more
        block = jnp.where(low_lane, sums[0:24], sums[24:48])
        for c in range(3):
            grid[c, pl.ds(pl.multiple_of(z * 8, 8), 8), :] = block[c * 8 : c * 8 + 8]
        return carry

    lax.fori_loop(0, HALF, spread, 0, unroll=4)

    for c in range(3):
        n = 0 if c < 2 else 2
        out_1[pl.ds(c, DEVICES, stride=8), :] = table_left(z_tab[n], z_tab[n + 1], grid[c])

    pl.semaphore_wait(tell.at[2], ROWS - 1)

    def exchange(out, into, k):
        def post(p):
            pltpu.make_async_remote_copy(
                src_ref=out.at[pl.ds(pl.multiple_of(p * 8, 8), 3), :],
                dst_ref=into.at[pl.ds(pl.multiple_of(me * 8, 8), 3), :],
                send_sem=all_send.at[k],
                recv_sem=all_recv.at[k],
                device_id=p,
                device_id_type=LOGICAL,
            ).start()

        def post_bunch(i, carry):
            bunch = me // BUNCH + i
            first = jnp.where(bunch >= DEVICES // BUNCH, bunch - DEVICES // BUNCH, bunch) * BUNCH
            for n in range(BUNCH):
                post(first + n)
            return carry

        lax.fori_loop(1, DEVICES // BUNCH, post_bunch, 0)
        for n in range(1, BUNCH):
            post(me // BUNCH * BUNCH + lax.rem(me + n, BUNCH))
        mine = pl.ds(pl.multiple_of(me * 8, 8), 3)
        keep = pltpu.make_async_copy(out.at[mine, :], into.at[mine, :], self_sem.at[k])
        keep.start()
        keep.wait()
        bulk = out.at[pl.ds(0, 3 * (DEVICES - 1)), :]
        pltpu.make_async_copy(bulk, bulk, all_recv.at[k]).wait()

    exchange(out_1, in_1, 0)

    cos_t, sin_t = twist[0], twist[1]
    for c in range(3):
        both = table_left(lf[0], lf[1], in_1[pl.ds(c, DEVICES, stride=8), :])
        re, im = both[0:128], both[128:256]
        work[c, :, 0:128] = re * cos_t + im * sin_t
        work[c, :, 128:256] = im * cos_t - re * sin_t
    for c in range(3):
        work[c] = table_right(work[c], rf[0], rf[1])

    special = me < 2
    plain = jnp.where(special, 1.0, 0.0).astype(F32)
    turn = jnp.where(special, 0, 2 * lax.rem(me, 2) - 1).astype(F32)
    kz = jnp.where(me == 1, -64, me // 2).astype(F32)
    kz_top = jnp.where(me == 1, -64, 0).astype(F32)
    kz_low = jnp.where(me == 1, 0, me // 2).astype(F32)

    def signed(v):
        return jnp.where(v < GRID // 2, v, v - GRID)

    def stokes(i, carry):
        rows = pl.ds(pl.multiple_of(i * 16, 16), 16)
        f1 = lax.broadcasted_iota(jnp.int32, (16, 128), 0) + i * 16
        f2 = lax.broadcasted_iota(jnp.int32, (16, 128), 1)
        ix = signed(f1 // 16 + 8 * (f2 // 8))
        iy = signed(f1 % 16 + 16 * (f2 % 8))
        kx, ky = ix.astype(F32), iy.astype(F32)
        kx_top = jnp.where(ix == -64, kx, 0.0)
        ky_top = jnp.where(iy == -64, ky, 0.0)
        kx_low, ky_low = kx - kx_top, ky - ky_top
        square = kx * kx + ky * ky + kz * kz
        damping = (0.25 / GRID**3) * jnp.exp(square * (-((math.pi / GRID) ** 2)))
        inverse = 1.0 / jnp.maximum(square, 1.0)
        w_re, w_im = work[2, rows, 0:128], work[2, rows, 128:256]
        sides = (
            (work[0, rows, 0:128], work[1, rows, 0:128], plain * w_re - turn * w_im),
            (work[0, rows, 128:256], work[1, rows, 128:256], plain * w_im + turn * w_re),
        )
        done = []
        for u, v, w in sides:
            low = (kx_low * u + ky_low * v + kz_low * w) * inverse
            top = (kx_top * u + ky_top * v + kz_top * w) * inverse
            done.append(
                (
                    damping * (u - kx_low * low - kx_top * top),
                    damping * (v - ky_low * low - ky_top * top),
                    damping * (w - kz_low * low - kz_top * top),
                )
            )
        for c in range(2):
            work[c, rows, 0:128] = done[0][c]
            work[c, rows, 128:256] = done[1][c]
        work[2, rows, 0:128] = plain * done[0][2] + turn * done[1][2]
        work[2, rows, 128:256] = plain * done[1][2] - turn * done[0][2]
        return carry

    lax.fori_loop(0, 8, stokes, 0)

    for c in range(3):
        both = table_right(work[c], rb[0], rb[1])
        re, im = both[:, 0:128], both[:, 128:256]
        pair = jnp.concatenate([re * cos_t - im * sin_t, im * cos_t + re * sin_t], 0)
        out_2[pl.ds(c, DEVICES, stride=8), :] = table_left(lb[0], lb[1], pair)

    exchange(out_2, in_2, 1)

    for c in range(3):
        n = 4 if c < 2 else 6
        grid[c] = table_left(z_tab[n], z_tab[n + 1], in_2[pl.ds(c, DEVICES, stride=8), :])

    def gather(z, carry):
        rows = pl.ds(pl.multiple_of(z * 8, 8), 8)
        block = jnp.concatenate([grid[c, rows, :] for c in range(3)], 0)
        near_half = jnp.where(low_lane, block, 0.0)
        far_half = block - near_half
        both = jnp.concatenate([near_half, far_half], 0)
        top = narrow(both)
        first = mul(jnp.concatenate([top, both - top], 0).astype(BF16), plan_h[z])
        second = mul(top.astype(BF16), plan_l[z])
        sums = first[0:48] + first[48:96] + second
        for h in range(2):
            spot = pl.ds(pl.multiple_of((h * HALF + z) * 8, 8), 8)
            bz = depth[spot, :]
            for c in range(3):
                far[c, spot, :] = sums[h * 24 + c * 8 : h * 24 + c * 8 + 8] * bz
        return carry

    lax.fori_loop(0, HALF, gather, 0)

    for c in range(3):
        total = far[c, pl.ds(0, CELLS, stride=8), :]
        for g in range(1, CELL):
            total = total + far[c, pl.ds(g, CELLS, stride=8), :]
        spin[c] = near_out[c] + total * state[6]

    for k in range(2):
        bulk = out_1.at[pl.ds(0, 3 * (DEVICES - 1)), :]
        pltpu.make_async_copy(bulk, bulk, all_send.at[k]).wait()
    for step in range(STEPS):
        for copy in halo(step):
            copy.wait_send()
def shards(positions, torques, counts, neighbour_flags):
    shape = positions.shape
    flat = (3, CELLS, SLOT)
    tables = [jnp.asarray(t) for t in make_tables()]
    vmem = pl.BlockSpec(memory_space=pltpu.VMEM)
    smem = pl.BlockSpec(memory_space=pltpu.SMEM)
    field = jax.ShapeDtypeStruct(flat, F32)
    buffer = pltpu.VMEM((DEVICES * 8, 128), F32)
    places, spin = pl.pallas_call(
        kernel,
        name="spinners",
        out_shape=(field, field),
        in_specs=[vmem, vmem, smem, smem] + [pl.BlockSpec(memory_space=pl.ANY)] * len(tables),
        out_specs=(vmem, vmem),
        scratch_shapes=[
            pltpu.VMEM(flat, F32),
            pltpu.VMEM((7, CELLS, SLOT), F32),
            pltpu.VMEM((STEPS - 1, 3, CELLS, SLOT), F32),
            pltpu.VMEM((6, CELLS, SLOT), F32),
            pltpu.VMEM((CELLS * A_PITCH, SLOT), F32),
            pltpu.VMEM((CELLS // GROUP, SLOT, SLOT), BF16),
            pltpu.VMEM((7, CELLS * B_PITCH, SLOT), F32),
            pltpu.VMEM((7, CELLS * L_PITCH, SLOT), F32),
            pltpu.VMEM((CELLS * T_PITCH, SLOT), F32),
            pltpu.VMEM((CELLS * T_PITCH, SLOT), F32),
            pltpu.VMEM((CELLS * T_PITCH, SLOT), F32),
            pltpu.VMEM((2, 7, HALF, SLOT), F32),
            pltpu.VMEM((2, 7, CELLS, SLOT), F32),
            pltpu.VMEM((STEPS - 1, 2, 3, HALF, SLOT), F32),
            pltpu.VMEM((STEPS - 1, 2, 3, CELLS, SLOT), F32),
            pltpu.SemaphoreType.DMA((STEPS, 4)),
            pltpu.SemaphoreType.DMA((STEPS, 4)),
            pltpu.SemaphoreType.REGULAR((3,)),
        ]
        + [pltpu.VMEM(t.shape, t.dtype) for t in tables]
        + [
            pltpu.SemaphoreType.DMA((len(tables),)),
            pltpu.VMEM((3, GRID, 128), F32),
            pltpu.VMEM((HALF, 128, SLOT), BF16),
            pltpu.VMEM((HALF, 128, SLOT), BF16),
            pltpu.VMEM((CELLS * 8, SLOT), F32),
            buffer,
            buffer,
            buffer,
            buffer,
            pltpu.VMEM((3, 128, 256), F32),
            pltpu.VMEM((3, CELLS * 8, SLOT), F32),
            pltpu.SemaphoreType.DMA((2,)),
            pltpu.SemaphoreType.DMA((2,)),
            pltpu.SemaphoreType.DMA((2,)),
        ],
        compiler_params=pltpu.CompilerParams(collective_id=0, has_side_effects=True),
    )(positions.reshape(flat), torques.reshape(flat), counts, neighbour_flags, *tables)
    return places.reshape(shape), spin.reshape(shape)


def solution(mesh):
    in_specs = (
        P(None, "row", "col", None, None),
        P(None, "row", "col", None, None),
        P("row", "col", None),
        P(None, "row", "col", None),
    )
    out_specs = (P(None, "row", "col", None, None), P(None, "row", "col", None, None))
    return jax.shard_map(shards, mesh=mesh, in_specs=in_specs, out_specs=out_specs, check_vma=False)
```

```python
import math

import jax
import jax.numpy as jnp
import numpy as np
from jax import lax
from jax.experimental import pallas as pl
from jax.experimental.pallas import tpu as pltpu
from jax.sharding import PartitionSpec as P

GRID = 128
CELL = 8
SLOT = 128
STEPS = 3
ROWS = 8
COLS = 16
DEVICES = ROWS * COLS
BUNCH = 8
CELLS = 32
HALF = 16
MESH = pl.DeviceIdType.MESH
LOGICAL = pl.DeviceIdType.LOGICAL
F32 = jnp.float32
BF16 = jnp.bfloat16

KAPPA = 2.0 / (CELL * CELL) * math.log2(math.e)
PACE = 0.06 * CELL
DRIFT = 1.0 / SLOT
COUPLE = 0.5 / SLOT
MID = 0.5 * CELL

A_ROWS = 32
GROUP = SLOT // A_ROWS
GROUPS = CELLS // GROUP
B_ROWS = 16
L_ROWS = 16
A_PITCH = A_ROWS + 1
B_PITCH = B_ROWS + 1
L_PITCH = L_ROWS + 1
T_PITCH = 9


def halves(table):
    high = table.astype(np.float32).astype(jnp.bfloat16)
    low = (table - high.astype(np.float64)).astype(np.float32).astype(jnp.bfloat16)
    return high, low


def make_tables():
    n = np.arange(GRID)
    level = np.where(n == 1, 64, n // 2)
    angle = 2.0 * np.pi * (level[:, None] * n[None, :] % GRID) / GRID
    cosine, sine = np.cos(angle), np.sin(angle)
    even = (n % 2 == 0)[:, None]
    whole = (n < 2)[:, None]
    basis_xy = np.where(whole | even, cosine, sine)
    basis_z = np.where(whole | ~even, cosine, sine)
    count = np.where(n < 2, 1.0, 2.0)[:, None]
    back_xy, back_z = (basis_xy * count).T, (basis_z * count).T

    def wave(a, b, period_a, period_b):
        return 2.0 * np.pi * ((a * b[0] % period_a) / period_a + (b[1] % period_b) / period_b)

    r, q = n // 16, n % 16
    turn_l = 2.0 * np.pi * ((r[:, None] * r[None, :] % 8) / 8 + (q[:, None] * q[None, :] % 16) / 16)
    s, t = n // 8, n % 8
    turn_r = 2.0 * np.pi * ((s[:, None] * s[None, :] % 16) / 16 + (t[:, None] * t[None, :] % 8) / 8)
    twist = 2.0 * np.pi * (r[:, None] * s[None, :] + q[:, None] * t[None, :]) / GRID
    cl, sl = np.cos(turn_l), np.sin(turn_l)
    cr, sr = np.cos(turn_r), np.sin(turn_r)
    left = np.concatenate([cl, -sl], 0)
    left_back = np.concatenate([cl, -sl], 1)
    right = np.block([[cr, -sr], [sr, cr]])
    right_back = np.block([[cr, sr], [-sr, cr]])
    along_z = [half for table in (basis_xy, basis_z, back_xy, back_z) for half in halves(table)]
    out = [np.stack(along_z)] + [np.stack(halves(table)) for table in (left, left_back, right, right_back)]
    return out + [np.stack([np.cos(twist), np.sin(twist)]).astype(np.float32)]


def cut(v):
    h = v.astype(BF16)
    return h, (v - h.astype(F32)).astype(BF16)


def mul(a, b):
    return jnp.dot(a, b, preferred_element_type=F32)


def mul_t(a, b):
    return lax.dot_general(a, b, (((1,), (1,)), ((), ())), preferred_element_type=F32)


def table_left(table, v):
    vh, vl = cut(v)
    rows = table.shape[1]
    both = mul(table.reshape(2 * rows, table.shape[2]), vh)
    return both[:rows] + (both[rows:] + mul(table[0], vl))


def table_right(parts, table):
    cuts = [cut(v) for v in parts]
    high = jnp.concatenate([h for h, _ in cuts], 0)
    both = mul(jnp.concatenate([high] + [l for _, l in cuts], 0), table[0])
    rows = high.shape[0]
    total = both[:rows] + (both[rows:] + mul(high, table[1]))
    size = parts[0].shape[0]
    return [total[n * size : (n + 1) * size] for n in range(len(parts))]


def narrow(v):
    return v.astype(BF16).astype(F32)


def split3(v):
    h = narrow(v)
    r = v - h
    m = narrow(r)
    return h, m, r - m


def put(ref, lead, start, stride, val):
    ref[lead, pl.ds(start, val.shape[0], stride=stride), :] = val


def put_receiver(afeat, half, px, py, pz):
    base = half * HALF * A_PITCH

    def row(k, v):
        afeat[pl.ds(base + k, HALF, stride=A_PITCH), :] = v

    size = split3(-KAPPA * (px * px + py * py + pz * pz))
    for d, v in enumerate((px, py, pz)):
        h, m, l = split3(v * (2.0 * KAPPA))
        row(d, h)
        row(8 + d, h)
        row(11 + d, h)
        row((7, 14, 15)[d], l)
        row(16 + d, m)
        row(24 + d, m)
    row(6, size[0])
    row(16 + 6, size[1])


def put_source(bfeat, lfeat, slot, half, place, torque, fill, shift, gate, loads_only=False):
    place = [place[d] + shift[d] if shift[d] != 0.0 else place[d] for d in range(3)]
    x, y, z = place
    if not loads_only:
        base = half * HALF * B_PITCH
        for d in range(3):
            h, m, l = split3(place[d])
            put(bfeat, slot, base + d, B_PITCH, h)
            put(bfeat, slot, base + 8 + d, B_PITCH, m)
            put(bfeat, slot, base + 11 + d, B_PITCH, l)
            put(bfeat, slot, base + (7, 14, 15)[d], B_PITCH, h)
        for k, v in enumerate(split3(-KAPPA * (x * x + y * y + z * z))):
            put(bfeat, slot, base + 3 + k, B_PITCH, v)
    if gate is not None:
        torque = [t * gate for t in torque]
        fill = fill * gate
    tx, ty, tz = torque
    loads = (tx, ty, tz, ty * z - tz * y, tz * x - tx * z, tx * y - ty * x)
    base = half * HALF * L_PITCH
    for q, v in enumerate(loads):
        h = narrow(v)
        put(lfeat, slot, base + q, L_PITCH, h)
        put(lfeat, slot, base + 8 + q, L_PITCH, v - h)
    put(lfeat, slot, base + 6, L_PITCH, fill)


def kernel(
    pos_far, tor_far, cnt_far, flg_far, z_far, lf_far, lb_far, rf_far, rb_far, twist_far, moved_far, spin,
    pos_in, tor_in, pos_out, cnt, flg, field_sem, near_out, state, places, gates, afeat, trans, bfeat, lfeat, totals, totals_z, totals_x,
    full_x, full_y, part_x, part_y, send_sem, recv_sem, tell,
    z_tab, lf, lb, rf, rb, twist, table_sem,
    grid, plan_h, plan_l, depth, out_1, in_1, out_2, in_2, work, far, all_send, all_recv, self_sem,
):
    row = lax.axis_index("row")
    col = lax.axis_index("col")
    peers = (
        (lax.rem(row + 1, ROWS), col),
        (lax.rem(row + ROWS - 1, ROWS), col),
        (row, lax.rem(col + 1, COLS)),
        (row, lax.rem(col + COLS - 1, COLS)),
    )
    barrier = pltpu.get_barrier_semaphore()
    for peer in peers:
        pl.semaphore_signal(barrier, inc=1, device_id=peer, device_id_type=MESH)

    fields = [
        pltpu.make_async_copy(src, dst, field_sem.at[k])
        for k, (src, dst) in enumerate(((pos_far, pos_in), (tor_far, tor_in), (cnt_far, cnt), (flg_far, flg)))
    ]
    for field in fields:
        field.start()
    tables = [
        pltpu.make_async_copy(src, dst, table_sem.at[k])
        for k, (src, dst) in enumerate(
            ((z_far, z_tab), (lf_far, lf), (lb_far, lb), (rf_far, rf), (rb_far, rb), (twist_far, twist))
        )
    ]
    for table in tables:
        table.start()

    def inform(k, steps):
        for down, right in steps:
            where = (lax.rem(row + down + ROWS, ROWS), lax.rem(col + right + COLS, COLS))
            pl.semaphore_signal(tell.at[k], inc=1, device_id=where, device_id_type=MESH)

    def learn(step):
        if step == 0:
            inform(0, ((2, 0), (-2, 0), (0, 2), (0, -2)))
        elif step == 1:
            pl.semaphore_wait(tell.at[0], 4)
            inform(1, ((0, 4), (0, -4)))
        else:
            pl.semaphore_wait(tell.at[1], 2)
            inform(2, [(k, 0) for k in range(1, ROWS)])

    lane = lax.broadcasted_iota(jnp.int32, (1, SLOT), 1)

    def spread_scalars(z, carry):
        for h in range(2):
            state[6, pl.ds(h * HALF + z, 1), :] = (lane < cnt[h, 0, z]).astype(F32)
            for f in range(6):
                gates[f, pl.ds(h * HALF + z, 1), :] = jnp.full((1, SLOT), flg[f, h, 0, z], jnp.int32).astype(F32)
        return carry

    for field in fields:
        field.wait()
    lax.fori_loop(0, HALF, spread_scalars, 0)
    fill = state[6]
    for d in range(3):
        state[d] = pos_in[d] - MID
        state[3 + d] = tor_in[d] * fill

    pl.semaphore_wait(barrier, 4)

    def halo(step):
        if step == 0:
            own, into_x, into_y = state, full_x, full_y
        else:
            own, into_x, into_y = places.at[step - 1], part_x.at[step - 1], part_y.at[step - 1]
        moves = (
            (own.at[:, pl.ds(HALF, HALF), :], into_x.at[0], 0),
            (own.at[:, pl.ds(0, HALF), :], into_x.at[1], 1),
            (own, into_y.at[0], 2),
            (own, into_y.at[1], 3),
        )
        copies = []
        for src, dst, k in moves:
            copies.append(
                pltpu.make_async_remote_copy(
                    src_ref=src,
                    dst_ref=dst,
                    send_sem=send_sem.at[step, k],
                    recv_sem=recv_sem.at[step, k],
                    device_id=peers[k],
                    device_id_type=MESH,
                )
            )
        return copies

    one = jnp.ones((CELLS, SLOT), F32)
    zero = jnp.zeros((CELLS, SLOT), F32)
    for k in (19, 20, 21, 23, 27, 28, 29, 30, 31):
        afeat[pl.ds(k, CELLS, stride=A_PITCH), :] = zero
    for k in (3, 4, 5):
        afeat[pl.ds(k, CELLS, stride=A_PITCH), :] = one
    totals_x[pl.ds(0, HALF * T_PITCH), :] = jnp.zeros((HALF * T_PITCH, SLOT), F32)
    for e in range(7):
        put(bfeat, e, 6, B_PITCH, one)
        for k in (7, 14, 15):
            put(lfeat, e, k, L_PITCH, zero)

    owner = lax.broadcasted_iota(jnp.int32, (SLOT, SLOT), 1) // A_ROWS

    def wide(ref, n, cell, faces):
        blocks = [ref[e, pl.ds(cell * (n + 1), n), :] for e in faces]
        return (blocks[0] if len(blocks) == 1 else jnp.concatenate(blocks, 1)).astype(BF16)

    def powers(group, faces):
        block = trans[group]
        ats = [jnp.where(owner == k, block, jnp.zeros_like(block)) for k in range(GROUP)]
        b = []
        for k in range(GROUP):
            part = wide(bfeat, B_ROWS, group * GROUP + k, faces)
            b += [part, part]
        return jnp.dot(jnp.concatenate(ats, 0), jnp.concatenate(b, 0), preferred_element_type=F32)

    def add_up(load, w, side):
        acc = lax.dot_general(load, w, (((1,), (side,)), ((), ())), preferred_element_type=F32)
        return acc[0:8] + acc[8:16]

    def inner_cell(group, k, faces, power):
        cell = group * GROUP + k
        w = jnp.exp2(power[k * SLOT : (k + 1) * SLOT]).astype(BF16)
        totals[pl.ds(cell * T_PITCH, 8), :] = add_up(wide(lfeat, L_ROWS, cell, faces), w, 1)
        upper = (cell // HALF) * HALF + (cell + 1) % HALF
        load = wide(lfeat, L_ROWS, upper, (2,))
        if len(faces) == 2:
            totals_z[pl.ds(upper * T_PITCH, 8), :] = add_up(load, w[:, SLOT:], 0)
        else:
            load = jnp.concatenate([load, wide(lfeat, L_ROWS, cell + HALF, (3,))], 0)
            acc = lax.dot_general(load, w[:, SLOT:], (((1,), (0,)), ((), ())), preferred_element_type=F32)
            totals_z[pl.ds(upper * T_PITCH, 8), :] = acc[0:8, 0:SLOT] + acc[8:16, 0:SLOT]
            totals_x[pl.ds((cell + HALF) * T_PITCH, 8), :] = acc[16:24, SLOT:] + acc[24:32, SLOT:]

    def inner_faces(i, carry):
        sides = ((i, (0, 1, 3)), (i + GROUPS // 2, (0, 1)))
        both = [powers(g, faces) for g, faces in sides]
        for k, n in [(k, n) for k in range(GROUP) for n in range(2)]:
            inner_cell(sides[n][0], k, sides[n][1], both[n])

        return carry

    def turn_receivers(group):
        rows = [afeat[pl.ds((group * GROUP + k) * A_PITCH, A_ROWS), :] for k in range(GROUP)]
        trans[group] = jnp.concatenate(rows, 0).T.astype(BF16)

    def outer_faces(i, carry):
        both = [powers(i + g * (GROUPS // 2), (4, 5, 6)) for g in range(2)]
        for cell, power, k in [((i + g * (GROUPS // 2)) * GROUP + k, both[g], k) for g in range(2) for k in range(GROUP)]:
            w = jnp.exp2(power[k * SLOT : (k + 1) * SLOT]).astype(BF16)
            spot = pl.ds(cell * T_PITCH, 8)
            totals[spot, :] = totals[spot, :] + add_up(wide(lfeat, L_ROWS, cell, (4, 5, 6)), w, 1)
        return carry

    for step in range(STEPS):
        copies = halo(step)
        for copy in copies:
            copy.start()
        here = state if step == 0 else places.at[step - 1]
        for h in range(2):
            part = slice(h * HALF, (h + 1) * HALF)
            other = slice((1 - h) * HALF, (2 - h) * HALF)
            place = [here[d, part, :] for d in range(3)]
            torque = [state[3 + d, part, :] for d in range(3)]
            fill = state[6, part, :]
            put_receiver(afeat, h, *place)
            put_source(bfeat, lfeat, 0, h, place, torque, fill, (0.0, 0.0, 0.0), None)
            for slot, turn, lift, face in ((1, HALF - 1, CELL, 4), (2, 1, -CELL, 5)):
                def turned(v):
                    return pltpu.roll(v, turn, 0)

                put_source(
                    bfeat, lfeat, slot, h, [turned(v) for v in place], [turned(v) for v in torque], turned(fill),
                    (0.0, 0.0, float(lift)), gates[face, part, :], loads_only=slot == 2,
                )
            put_source(
                bfeat, lfeat, 3, h,
                [here[d, other, :] for d in range(3)],
                [state[3 + d, other, :] for d in range(3)],
                state[6, other, :],
                (float(CELL) if h == 0 else -float(CELL), 0.0, 0.0),
                gates[0 if h == 0 else 1, part, :],
                loads_only=h == 1,
            )
        for g in range(GROUPS):
            turn_receivers(g)
        lax.fori_loop(0, GROUPS // 2, inner_faces, 0)
        for copy in copies:
            copy.wait_recv()
        learn(step)
        for h in range(2):
            part = slice(h * HALF, (h + 1) * HALF)
            near_x = full_x if step == 0 else part_x.at[step - 1]
            near_y = full_y if step == 0 else part_y.at[step - 1]
            put_source(
                bfeat, lfeat, 4, h,
                [near_x[h, d] for d in range(3)],
                [full_x[h, 3 + d] for d in range(3)],
                full_x[h, 6],
                (-float(CELL) if h == 0 else float(CELL), 0.0, 0.0),
                gates[1 if h == 0 else 0, part, :],
            )
            for slot, side, lift, face in ((5, 1, CELL, 2), (6, 0, -CELL, 3)):
                put_source(
                    bfeat, lfeat, slot, h,
                    [near_y[side, d, part, :] for d in range(3)],
                    [full_y[side, 3 + d, part, :] for d in range(3)],
                    full_y[side, 6, part, :],
                    (0.0, float(lift), 0.0),
                    gates[face, part, :],
                )
        lax.fori_loop(0, GROUPS // 2, outer_faces, 0)

        tot = []
        for q in range(7):
            rows = pl.ds(q, CELLS, stride=T_PITCH)
            tot.append(totals[rows, :] + totals_z[rows, :] + totals_x[rows, :])
        fill = state[6]
        x, y, z = (here[d] for d in range(3))
        speed = (
            tot[1] * z - tot[2] * y - tot[3],
            tot[2] * x - tot[0] * z - tot[4],
            tot[0] * y - tot[1] * x - tot[5],
        )
        for d in range(3):
            moved = here[d] + PACE * (DRIFT * speed[d] * fill)
            if step < STEPS - 1:
                places[step, d] = moved
            else:
                pos_out[d] = moved + MID
                torque = tor_in[d]
                near_out[d] = (torque + COUPLE * (tot[d] - tot[6] * torque)) * fill

    me = row * COLS + col

    level = lax.broadcasted_iota(jnp.int32, (CELL, SLOT), 0).astype(F32) + 0.5
    low_lane = lax.broadcasted_iota(jnp.int32, (24, SLOT), 1) < 64

    give = pltpu.make_async_copy(pos_out, moved_far, field_sem.at[4])
    give.start()
    for table in tables:
        table.wait()

    def bins(d, cell):
        apart = pos_out[d, pl.ds(cell, 1), :] - level
        return jnp.exp(-apart * apart)

    def spread(z, carry):
        planar, lifted, rest = [], [], []
        for h in range(2):
            cell = h * HALF + z
            bx, by, bz = (bins(d, cell) for d in range(3))
            depth[pl.ds(pl.multiple_of(cell * 8, 8), 8), :] = bz
            planar += [bx[a : a + 1, :] * by for a in range(CELL)]
            lift = [state[3 + c, pl.ds(cell, 1), :] * bz for c in range(3)]
            top = [narrow(v) for v in lift]
            lifted += top
            rest += [v - t for v, t in zip(lift, top)]
        ph, pl_ = cut(jnp.concatenate(planar, 0))
        plan_h[z] = ph
        plan_l[z] = pl_
        both = mul_t(jnp.concatenate(lifted + rest, 0).astype(BF16), ph)
        more = mul_t(jnp.concatenate(lifted, 0).astype(BF16), pl_)
        sums = both[0:48] + both[48:96] + more
        block = jnp.where(low_lane, sums[0:24], sums[24:48])
        for c in range(3):
            grid[c, pl.ds(pl.multiple_of(z * 8, 8), 8), :] = block[c * 8 : c * 8 + 8]
        return carry

    lax.fori_loop(0, HALF, spread, 0, unroll=4)

    def along_z(first, v):
        pair = table_left(z_tab[first : first + 2], jnp.concatenate(v[0:2], 1))
        return pair[:, 0:128], pair[:, 128:256], table_left(z_tab[first + 2 : first + 4], v[2])

    for c, v in enumerate(along_z(0, [grid[c] for c in range(3)])):
        out_1[pl.ds(c, DEVICES, stride=8), :] = v

    pl.semaphore_wait(tell.at[2], ROWS - 1)

    def exchange(out, into, k):
        def post(p):
            pltpu.make_async_remote_copy(
                src_ref=out.at[pl.ds(pl.multiple_of(p * 8, 8), 3), :],
                dst_ref=into.at[pl.ds(pl.multiple_of(me * 8, 8), 3), :],
                send_sem=all_send.at[k],
                recv_sem=all_recv.at[k],
                device_id=p,
                device_id_type=LOGICAL,
            ).start()

        def post_bunch(i, carry):
            bunch = me // BUNCH + i
            first = jnp.where(bunch >= DEVICES // BUNCH, bunch - DEVICES // BUNCH, bunch) * BUNCH
            for n in range(BUNCH):
                post(first + n)
            return carry

        lax.fori_loop(1, DEVICES // BUNCH, post_bunch, 0)
        for n in range(1, BUNCH):
            post(me // BUNCH * BUNCH + lax.rem(me + n, BUNCH))
        mine = pl.ds(pl.multiple_of(me * 8, 8), 3)
        keep = pltpu.make_async_copy(out.at[mine, :], into.at[mine, :], self_sem.at[k])
        keep.start()
        keep.wait()
        bulk = out.at[pl.ds(0, 3 * (DEVICES - 1)), :]
        pltpu.make_async_copy(bulk, bulk, all_recv.at[k]).wait()

    exchange(out_1, in_1, 0)

    cos_t, sin_t = twist[0], twist[1]
    planes = jnp.concatenate([in_1[pl.ds(c, DEVICES, stride=8), :] for c in range(3)], 1)
    both = table_left(lf[...], planes)
    turned = []
    for c in range(3):
        re, im = both[0:128, c * 128 : c * 128 + 128], both[128:256, c * 128 : c * 128 + 128]
        turned.append(jnp.concatenate([re * cos_t + im * sin_t, im * cos_t - re * sin_t], 1))
    for c, v in enumerate(table_right(turned, rf)):
        work[c] = v

    special = me < 2
    plain = jnp.where(special, 1.0, 0.0).astype(F32)
    turn = jnp.where(special, 0, 2 * lax.rem(me, 2) - 1).astype(F32)
    kz = jnp.where(me == 1, -64, me // 2).astype(F32)
    kz_top = jnp.where(me == 1, -64, 0).astype(F32)
    kz_low = jnp.where(me == 1, 0, me // 2).astype(F32)

    def signed(v):
        return jnp.where(v < GRID // 2, v, v - GRID)

    def stokes(i, carry):
        rows = pl.ds(pl.multiple_of(i * 16, 16), 16)
        f1 = lax.broadcasted_iota(jnp.int32, (16, 128), 0) + i * 16
        f2 = lax.broadcasted_iota(jnp.int32, (16, 128), 1)
        ix = signed(f1 // 16 + 8 * (f2 // 8))
        iy = signed(f1 % 16 + 16 * (f2 % 8))
        kx, ky = ix.astype(F32), iy.astype(F32)
        kx_top = jnp.where(ix == -64, kx, 0.0)
        ky_top = jnp.where(iy == -64, ky, 0.0)
        kx_low, ky_low = kx - kx_top, ky - ky_top
        square = kx * kx + ky * ky + kz * kz
        damping = (0.25 / GRID**3) * jnp.exp(square * (-((math.pi / GRID) ** 2)))
        inverse = 1.0 / jnp.maximum(square, 1.0)
        w_re, w_im = work[2, rows, 0:128], work[2, rows, 128:256]
        sides = (
            (work[0, rows, 0:128], work[1, rows, 0:128], plain * w_re - turn * w_im),
            (work[0, rows, 128:256], work[1, rows, 128:256], plain * w_im + turn * w_re),
        )
        done = []
        for u, v, w in sides:
            low = (kx_low * u + ky_low * v + kz_low * w) * inverse
            top = (kx_top * u + ky_top * v + kz_top * w) * inverse
            done.append(
                (
                    damping * (u - kx_low * low - kx_top * top),
                    damping * (v - ky_low * low - ky_top * top),
                    damping * (w - kz_low * low - kz_top * top),
                )
            )
        for c in range(2):
            work[c, rows, 0:128] = done[0][c]
            work[c, rows, 128:256] = done[1][c]
        work[2, rows, 0:128] = plain * done[0][2] + turn * done[1][2]
        work[2, rows, 128:256] = plain * done[1][2] - turn * done[0][2]
        return carry

    lax.fori_loop(0, 8, stokes, 0)

    pairs = []
    for both in table_right([work[c] for c in range(3)], rb):
        re, im = both[:, 0:128], both[:, 128:256]
        pairs.append(jnp.concatenate([re * cos_t - im * sin_t, im * cos_t + re * sin_t], 0))
    planes = table_left(lb[...], jnp.concatenate(pairs, 1))
    for c in range(3):
        out_2[pl.ds(c, DEVICES, stride=8), :] = planes[:, c * 128 : c * 128 + 128]

    exchange(out_2, in_2, 1)

    for c, v in enumerate(along_z(4, [in_2[pl.ds(c, DEVICES, stride=8), :] for c in range(3)])):
        grid[c] = v

    def gather(z, carry):
        rows = pl.ds(pl.multiple_of(z * 8, 8), 8)
        block = jnp.concatenate([grid[c, rows, :] for c in range(3)], 0)
        near_half = jnp.where(low_lane, block, 0.0)
        far_half = block - near_half
        both = jnp.concatenate([near_half, far_half], 0)
        top = narrow(both)
        first = mul(jnp.concatenate([top, both - top], 0).astype(BF16), plan_h[z])
        second = mul(top.astype(BF16), plan_l[z])
        sums = first[0:48] + first[48:96] + second
        for h in range(2):
            spot = pl.ds(pl.multiple_of((h * HALF + z) * 8, 8), 8)
            bz = depth[spot, :]
            for c in range(3):
                far[c, spot, :] = sums[h * 24 + c * 8 : h * 24 + c * 8 + 8] * bz
        return carry

    lax.fori_loop(0, HALF, gather, 0)

    for c in range(3):
        total = far[c, pl.ds(0, CELLS, stride=8), :]
        for g in range(1, CELL):
            total = total + far[c, pl.ds(g, CELLS, stride=8), :]
        spin[c] = near_out[c] + total * state[6]

    for k in range(2):
        bulk = out_1.at[pl.ds(0, 3 * (DEVICES - 1)), :]
        pltpu.make_async_copy(bulk, bulk, all_send.at[k]).wait()
    give.wait()
    for step in range(STEPS):
        for copy in halo(step):
            copy.wait_send()
def shards(positions, torques, counts, neighbour_flags):
    shape = positions.shape
    flat = (3, CELLS, SLOT)
    tables = [jnp.asarray(t) for t in make_tables()]
    vmem = pl.BlockSpec(memory_space=pltpu.VMEM)
    there = pl.BlockSpec(memory_space=pl.ANY)
    field = jax.ShapeDtypeStruct(flat, F32)
    buffer = pltpu.VMEM((DEVICES * 8, 128), F32)
    places, spin = pl.pallas_call(
        kernel,
        name="spinners",
        out_shape=(field, field),
        in_specs=[there] * (4 + len(tables)),
        out_specs=(there, vmem),
        scratch_shapes=[
            pltpu.VMEM(flat, F32),
            pltpu.VMEM(flat, F32),
            pltpu.VMEM(flat, F32),
            pltpu.SMEM(counts.shape, jnp.int32),
            pltpu.SMEM(neighbour_flags.shape, jnp.int32),
            pltpu.SemaphoreType.DMA((5,)),
            pltpu.VMEM(flat, F32),
            pltpu.VMEM((7, CELLS, SLOT), F32),
            pltpu.VMEM((STEPS - 1, 3, CELLS, SLOT), F32),
            pltpu.VMEM((6, CELLS, SLOT), F32),
            pltpu.VMEM((CELLS * A_PITCH, SLOT), F32),
            pltpu.VMEM((CELLS // GROUP, SLOT, SLOT), BF16),
            pltpu.VMEM((7, CELLS * B_PITCH, SLOT), F32),
            pltpu.VMEM((7, CELLS * L_PITCH, SLOT), F32),
            pltpu.VMEM((CELLS * T_PITCH, SLOT), F32),
            pltpu.VMEM((CELLS * T_PITCH, SLOT), F32),
            pltpu.VMEM((CELLS * T_PITCH, SLOT), F32),
            pltpu.VMEM((2, 7, HALF, SLOT), F32),
            pltpu.VMEM((2, 7, CELLS, SLOT), F32),
            pltpu.VMEM((STEPS - 1, 2, 3, HALF, SLOT), F32),
            pltpu.VMEM((STEPS - 1, 2, 3, CELLS, SLOT), F32),
            pltpu.SemaphoreType.DMA((STEPS, 4)),
            pltpu.SemaphoreType.DMA((STEPS, 4)),
            pltpu.SemaphoreType.REGULAR((3,)),
        ]
        + [pltpu.VMEM(t.shape, t.dtype) for t in tables]
        + [
            pltpu.SemaphoreType.DMA((len(tables),)),
            pltpu.VMEM((3, GRID, 128), F32),
            pltpu.VMEM((HALF, 128, SLOT), BF16),
            pltpu.VMEM((HALF, 128, SLOT), BF16),
            pltpu.VMEM((CELLS * 8, SLOT), F32),
            buffer,
            buffer,
            buffer,
            buffer,
            pltpu.VMEM((3, 128, 256), F32),
            pltpu.VMEM((3, CELLS * 8, SLOT), F32),
            pltpu.SemaphoreType.DMA((2,)),
            pltpu.SemaphoreType.DMA((2,)),
            pltpu.SemaphoreType.DMA((2,)),
        ],
        compiler_params=pltpu.CompilerParams(collective_id=0, has_side_effects=True),
    )(positions.reshape(flat), torques.reshape(flat), counts, neighbour_flags, *tables)
    return places.reshape(shape), spin.reshape(shape)


def solution(mesh):
    in_specs = (
        P(None, "row", "col", None, None),
        P(None, "row", "col", None, None),
        P("row", "col", None),
        P(None, "row", "col", None),
    )
    out_specs = (P(None, "row", "col", None, None), P(None, "row", "col", None, None))
    return jax.shard_map(shards, mesh=mesh, in_specs=in_specs, out_specs=out_specs, check_vma=False)
```

```python
import math

import jax
import jax.numpy as jnp
import numpy as np
from jax import lax
from jax.experimental import pallas as pl
from jax.experimental.pallas import tpu as pltpu
from jax.sharding import PartitionSpec as P

GRID = 128
CELL = 8
SLOT = 128
STEPS = 3
ROWS = 8
COLS = 16
DEVICES = ROWS * COLS
BUNCH = 8
CELLS = 32
HALF = 16
MESH = pl.DeviceIdType.MESH
LOGICAL = pl.DeviceIdType.LOGICAL
F32 = jnp.float32
BF16 = jnp.bfloat16

KAPPA = 2.0 / (CELL * CELL) * math.log2(math.e)
PACE = 0.06 * CELL
DRIFT = 1.0 / SLOT
COUPLE = 0.5 / SLOT
MID = 0.5 * CELL

A_ROWS = 32
GROUP = SLOT // A_ROWS
GROUPS = CELLS // GROUP
B_ROWS = 16
L_ROWS = 16
A_PITCH = A_ROWS + 1
B_PITCH = B_ROWS + 1
L_PITCH = L_ROWS + 1
T_PITCH = 9


def halves(table):
    high = table.astype(np.float32).astype(jnp.bfloat16)
    low = (table - high.astype(np.float64)).astype(np.float32).astype(jnp.bfloat16)
    return high, low


def make_tables():
    n = np.arange(GRID)
    level = np.where(n == 1, 64, n // 2)
    angle = 2.0 * np.pi * (level[:, None] * n[None, :] % GRID) / GRID
    cosine, sine = np.cos(angle), np.sin(angle)
    even = (n % 2 == 0)[:, None]
    whole = (n < 2)[:, None]
    basis_xy = np.where(whole | even, cosine, sine)
    basis_z = np.where(whole | ~even, cosine, sine)
    count = np.where(n < 2, 1.0, 2.0)[:, None]
    back_xy, back_z = (basis_xy * count).T, (basis_z * count).T

    def wave(a, b, period_a, period_b):
        return 2.0 * np.pi * ((a * b[0] % period_a) / period_a + (b[1] % period_b) / period_b)

    r, q = n // 16, n % 16
    turn_l = 2.0 * np.pi * ((r[:, None] * r[None, :] % 8) / 8 + (q[:, None] * q[None, :] % 16) / 16)
    s, t = n // 8, n % 8
    turn_r = 2.0 * np.pi * ((s[:, None] * s[None, :] % 16) / 16 + (t[:, None] * t[None, :] % 8) / 8)
    twist = 2.0 * np.pi * (r[:, None] * s[None, :] + q[:, None] * t[None, :]) / GRID
    cl, sl = np.cos(turn_l), np.sin(turn_l)
    cr, sr = np.cos(turn_r), np.sin(turn_r)
    left = np.concatenate([cl, -sl], 0)
    left_back = np.concatenate([cl, -sl], 1)
    right = np.block([[cr, -sr], [sr, cr]])
    right_back = np.block([[cr, sr], [-sr, cr]])
    along_z = [half for table in (basis_xy, basis_z, back_xy, back_z) for half in halves(table)]
    out = [np.stack(along_z)] + [np.stack(halves(table)) for table in (left, left_back, right, right_back)]
    return out + [np.stack([np.cos(twist), np.sin(twist)]).astype(np.float32)]


def cut(v):
    h = v.astype(BF16)
    return h, (v - h.astype(F32)).astype(BF16)


def mul(a, b):
    return jnp.dot(a, b, preferred_element_type=F32)


def mul_t(a, b):
    return lax.dot_general(a, b, (((1,), (1,)), ((), ())), preferred_element_type=F32)


def table_left(table, v):
    vh, vl = cut(v)
    rows = table.shape[1]
    both = mul(table.reshape(2 * rows, table.shape[2]), vh)
    return both[:rows] + (both[rows:] + mul(table[0], vl))


def table_right(parts, table):
    cuts = [cut(v) for v in parts]
    high = jnp.concatenate([h for h, _ in cuts], 0)
    both = mul(jnp.concatenate([high] + [l for _, l in cuts], 0), table[0])
    rows = high.shape[0]
    total = both[:rows] + (both[rows:] + mul(high, table[1]))
    size = parts[0].shape[0]
    return [total[n * size : (n + 1) * size] for n in range(len(parts))]


def narrow(v):
    return v.astype(BF16).astype(F32)


def split3(v):
    h = narrow(v)
    r = v - h
    m = narrow(r)
    return h, m, r - m


def put(ref, lead, start, stride, val):
    ref[lead, pl.ds(start, val.shape[0], stride=stride), :] = val


def put_receiver(afeat, half, px, py, pz):
    base = half * HALF * A_PITCH

    def row(k, v):
        afeat[pl.ds(base + k, HALF, stride=A_PITCH), :] = v

    size = split3(-KAPPA * (px * px + py * py + pz * pz))
    for d, v in enumerate((px, py, pz)):
        h, m, l = split3(v * (2.0 * KAPPA))
        row(d, h)
        row(8 + d, h)
        row(11 + d, h)
        row((7, 14, 15)[d], l)
        row(16 + d, m)
        row(24 + d, m)
    row(6, size[0])
    row(16 + 6, size[1])


def put_source(bfeat, lfeat, slot, half, place, torque, fill, shift, gate, loads_only=False):
    place = [place[d] + shift[d] if shift[d] != 0.0 else place[d] for d in range(3)]
    x, y, z = place
    if not loads_only:
        base = half * HALF * B_PITCH
        for d in range(3):
            h, m, l = split3(place[d])
            put(bfeat, slot, base + d, B_PITCH, h)
            put(bfeat, slot, base + 8 + d, B_PITCH, m)
            put(bfeat, slot, base + 11 + d, B_PITCH, l)
            put(bfeat, slot, base + (7, 14, 15)[d], B_PITCH, h)
        for k, v in enumerate(split3(-KAPPA * (x * x + y * y + z * z))):
            put(bfeat, slot, base + 3 + k, B_PITCH, v)
    if gate is not None:
        torque = [t * gate for t in torque]
        fill = fill * gate
    tx, ty, tz = torque
    loads = (tx, ty, tz, ty * z - tz * y, tz * x - tx * z, tx * y - ty * x)
    base = half * HALF * L_PITCH
    for q, v in enumerate(loads):
        h = narrow(v)
        put(lfeat, slot, base + q, L_PITCH, h)
        put(lfeat, slot, base + 8 + q, L_PITCH, v - h)
    put(lfeat, slot, base + 6, L_PITCH, fill)


def kernel(
    pos_far, tor_far, cnt_far, flg_far, z_far, lf_far, lb_far, rf_far, rb_far, twist_far, out_far,
    pos_in, tor_in, pos_out, spin, cnt, flg, field_sem, near_out, state, places, gates, afeat, trans, bfeat, lfeat, totals, totals_z, totals_x,
    full_x, full_y, part_x, part_y, send_sem, recv_sem, tell,
    z_tab, lf, lb, rf, rb, twist, table_sem,
    grid, plan_h, plan_l, depth, out_1, in_1, out_2, in_2, work, far, all_send, all_recv, self_sem,
):
    row = lax.axis_index("row")
    col = lax.axis_index("col")
    peers = (
        (lax.rem(row + 1, ROWS), col),
        (lax.rem(row + ROWS - 1, ROWS), col),
        (row, lax.rem(col + 1, COLS)),
        (row, lax.rem(col + COLS - 1, COLS)),
    )
    barrier = pltpu.get_barrier_semaphore()
    for peer in peers:
        pl.semaphore_signal(barrier, inc=1, device_id=peer, device_id_type=MESH)

    fields = [
        pltpu.make_async_copy(src, dst, field_sem.at[k])
        for k, (src, dst) in enumerate(((pos_far, pos_in), (tor_far, tor_in), (cnt_far, cnt), (flg_far, flg)))
    ]
    for field in fields:
        field.start()
    tables = [
        pltpu.make_async_copy(src, dst, table_sem.at[k])
        for k, (src, dst) in enumerate(
            ((z_far, z_tab), (lf_far, lf), (lb_far, lb), (rf_far, rf), (rb_far, rb), (twist_far, twist))
        )
    ]
    for table in tables:
        table.start()

    def inform(k, steps):
        for down, right in steps:
            where = (lax.rem(row + down + ROWS, ROWS), lax.rem(col + right + COLS, COLS))
            pl.semaphore_signal(tell.at[k], inc=1, device_id=where, device_id_type=MESH)

    def learn(step):
        if step == 0:
            inform(0, ((2, 0), (-2, 0), (0, 2), (0, -2)))
        elif step == 1:
            pl.semaphore_wait(tell.at[0], 4)
            inform(1, ((0, 4), (0, -4)))
        else:
            pl.semaphore_wait(tell.at[1], 2)
            inform(2, [(k, 0) for k in range(1, ROWS)])

    lane = lax.broadcasted_iota(jnp.int32, (1, SLOT), 1)

    def spread_scalars(z, carry):
        for h in range(2):
            state[6, pl.ds(h * HALF + z, 1), :] = (lane < cnt[h, 0, z]).astype(F32)
            for f in range(6):
                gates[f, pl.ds(h * HALF + z, 1), :] = jnp.full((1, SLOT), flg[f, h, 0, z], jnp.int32).astype(F32)
        return carry

    for field in fields:
        field.wait()
    lax.fori_loop(0, HALF, spread_scalars, 0)
    fill = state[6]
    for d in range(3):
        state[d] = pos_in[d] - MID
        state[3 + d] = tor_in[d] * fill

    pl.semaphore_wait(barrier, 4)

    def halo(step):
        if step == 0:
            own, into_x, into_y = state, full_x, full_y
        else:
            own, into_x, into_y = places.at[step - 1], part_x.at[step - 1], part_y.at[step - 1]
        moves = (
            (own.at[:, pl.ds(HALF, HALF), :], into_x.at[0], 0),
            (own.at[:, pl.ds(0, HALF), :], into_x.at[1], 1),
            (own, into_y.at[0], 2),
            (own, into_y.at[1], 3),
        )
        copies = []
        for src, dst, k in moves:
            copies.append(
                pltpu.make_async_remote_copy(
                    src_ref=src,
                    dst_ref=dst,
                    send_sem=send_sem.at[step, k],
                    recv_sem=recv_sem.at[step, k],
                    device_id=peers[k],
                    device_id_type=MESH,
                )
            )
        return copies

    one = jnp.ones((CELLS, SLOT), F32)
    zero = jnp.zeros((CELLS, SLOT), F32)
    for k in (19, 20, 21, 23, 27, 28, 29, 30, 31):
        afeat[pl.ds(k, CELLS, stride=A_PITCH), :] = zero
    for k in (3, 4, 5):
        afeat[pl.ds(k, CELLS, stride=A_PITCH), :] = one
    totals_x[pl.ds(0, HALF * T_PITCH), :] = jnp.zeros((HALF * T_PITCH, SLOT), F32)
    for e in range(7):
        put(bfeat, e, 6, B_PITCH, one)
        for k in (7, 14, 15):
            put(lfeat, e, k, L_PITCH, zero)

    owner = lax.broadcasted_iota(jnp.int32, (SLOT, SLOT), 1) // A_ROWS

    def wide(ref, n, cell, faces):
        blocks = [ref[e, pl.ds(cell * (n + 1), n), :] for e in faces]
        return (blocks[0] if len(blocks) == 1 else jnp.concatenate(blocks, 1)).astype(BF16)

    def powers(group, faces):
        block = trans[group]
        ats = [jnp.where(owner == k, block, jnp.zeros_like(block)) for k in range(GROUP)]
        b = []
        for k in range(GROUP):
            part = wide(bfeat, B_ROWS, group * GROUP + k, faces)
            b += [part, part]
        return jnp.dot(jnp.concatenate(ats, 0), jnp.concatenate(b, 0), preferred_element_type=F32)

    def add_up(load, w, side):
        acc = lax.dot_general(load, w, (((1,), (side,)), ((), ())), preferred_element_type=F32)
        return acc[0:8] + acc[8:16]

    def inner_cell(group, k, faces, power):
        cell = group * GROUP + k
        w = jnp.exp2(power[k * SLOT : (k + 1) * SLOT]).astype(BF16)
        totals[pl.ds(cell * T_PITCH, 8), :] = add_up(wide(lfeat, L_ROWS, cell, faces), w, 1)
        upper = (cell // HALF) * HALF + (cell + 1) % HALF
        load = wide(lfeat, L_ROWS, upper, (2,))
        if len(faces) == 2:
            totals_z[pl.ds(upper * T_PITCH, 8), :] = add_up(load, w[:, SLOT:], 0)
        else:
            load = jnp.concatenate([load, wide(lfeat, L_ROWS, cell + HALF, (3,))], 0)
            acc = lax.dot_general(load, w[:, SLOT:], (((1,), (0,)), ((), ())), preferred_element_type=F32)
            totals_z[pl.ds(upper * T_PITCH, 8), :] = acc[0:8, 0:SLOT] + acc[8:16, 0:SLOT]
            totals_x[pl.ds((cell + HALF) * T_PITCH, 8), :] = acc[16:24, SLOT:] + acc[24:32, SLOT:]

    def inner_faces(i, carry):
        sides = ((i, (0, 1, 3)), (i + GROUPS // 2, (0, 1)))
        both = [powers(g, faces) for g, faces in sides]
        for k, n in [(k, n) for k in range(GROUP) for n in range(2)]:
            inner_cell(sides[n][0], k, sides[n][1], both[n])

        return carry

    def turn_receivers(group):
        rows = [afeat[pl.ds((group * GROUP + k) * A_PITCH, A_ROWS), :] for k in range(GROUP)]
        trans[group] = jnp.concatenate(rows, 0).T.astype(BF16)

    def outer_faces(i, carry):
        both = [powers(i + g * (GROUPS // 2), (4, 5, 6)) for g in range(2)]
        for cell, power, k in [((i + g * (GROUPS // 2)) * GROUP + k, both[g], k) for g in range(2) for k in range(GROUP)]:
            w = jnp.exp2(power[k * SLOT : (k + 1) * SLOT]).astype(BF16)
            spot = pl.ds(cell * T_PITCH, 8)
            totals[spot, :] = totals[spot, :] + add_up(wide(lfeat, L_ROWS, cell, (4, 5, 6)), w, 1)
        return carry

    for step in range(STEPS):
        copies = halo(step)
        for copy in copies:
            copy.start()
        here = state if step == 0 else places.at[step - 1]
        for h in range(2):
            part = slice(h * HALF, (h + 1) * HALF)
            other = slice((1 - h) * HALF, (2 - h) * HALF)
            place = [here[d, part, :] for d in range(3)]
            torque = [state[3 + d, part, :] for d in range(3)]
            fill = state[6, part, :]
            put_receiver(afeat, h, *place)
            put_source(bfeat, lfeat, 0, h, place, torque, fill, (0.0, 0.0, 0.0), None)
            for slot, turn, lift, face in ((1, HALF - 1, CELL, 4), (2, 1, -CELL, 5)):
                def turned(v):
                    return pltpu.roll(v, turn, 0)

                put_source(
                    bfeat, lfeat, slot, h, [turned(v) for v in place], [turned(v) for v in torque], turned(fill),
                    (0.0, 0.0, float(lift)), gates[face, part, :], loads_only=slot == 2,
                )
            put_source(
                bfeat, lfeat, 3, h,
                [here[d, other, :] for d in range(3)],
                [state[3 + d, other, :] for d in range(3)],
                state[6, other, :],
                (float(CELL) if h == 0 else -float(CELL), 0.0, 0.0),
                gates[0 if h == 0 else 1, part, :],
                loads_only=h == 1,
            )
        for g in range(GROUPS):
            turn_receivers(g)
        lax.fori_loop(0, GROUPS // 2, inner_faces, 0)
        for copy in copies:
            copy.wait_recv()
        learn(step)
        for h in range(2):
            part = slice(h * HALF, (h + 1) * HALF)
            near_x = full_x if step == 0 else part_x.at[step - 1]
            near_y = full_y if step == 0 else part_y.at[step - 1]
            put_source(
                bfeat, lfeat, 4, h,
                [near_x[h, d] for d in range(3)],
                [full_x[h, 3 + d] for d in range(3)],
                full_x[h, 6],
                (-float(CELL) if h == 0 else float(CELL), 0.0, 0.0),
                gates[1 if h == 0 else 0, part, :],
            )
            for slot, side, lift, face in ((5, 1, CELL, 2), (6, 0, -CELL, 3)):
                put_source(
                    bfeat, lfeat, slot, h,
                    [near_y[side, d, part, :] for d in range(3)],
                    [full_y[side, 3 + d, part, :] for d in range(3)],
                    full_y[side, 6, part, :],
                    (0.0, float(lift), 0.0),
                    gates[face, part, :],
                )
        lax.fori_loop(0, GROUPS // 2, outer_faces, 0)

        tot = []
        for q in range(7):
            rows = pl.ds(q, CELLS, stride=T_PITCH)
            tot.append(totals[rows, :] + totals_z[rows, :] + totals_x[rows, :])
        fill = state[6]
        x, y, z = (here[d] for d in range(3))
        speed = (
            tot[1] * z - tot[2] * y - tot[3],
            tot[2] * x - tot[0] * z - tot[4],
            tot[0] * y - tot[1] * x - tot[5],
        )
        for d in range(3):
            moved = here[d] + PACE * (DRIFT * speed[d] * fill)
            if step < STEPS - 1:
                places[step, d] = moved
            else:
                pos_out[d] = moved
                torque = tor_in[d]
                near_out[d] = (torque + COUPLE * (tot[d] - tot[6] * torque)) * fill

    me = row * COLS + col

    level = lax.broadcasted_iota(jnp.int32, (CELL, SLOT), 0).astype(F32) + 0.5
    low_lane = lax.broadcasted_iota(jnp.int32, (24, SLOT), 1) < 64

    gives = [pltpu.make_async_copy(src, out_far.at[k], field_sem.at[4 + k]) for k, src in enumerate((pos_out, near_out, spin))]
    for give in gives[0:2]:
        give.start()
    for table in tables:
        table.wait()

    def bins(d, cell):
        apart = pos_out[d, pl.ds(cell, 1), :] + MID - level
        return jnp.exp(-apart * apart)

    def spread(z, carry):
        planar, lifted, rest = [], [], []
        for h in range(2):
            cell = h * HALF + z
            bx, by, bz = (bins(d, cell) for d in range(3))
            depth[pl.ds(pl.multiple_of(cell * 8, 8), 8), :] = bz
            planar += [bx[a : a + 1, :] * by for a in range(CELL)]
            lift = [state[3 + c, pl.ds(cell, 1), :] * bz for c in range(3)]
            top = [narrow(v) for v in lift]
            lifted += top
            rest += [v - t for v, t in zip(lift, top)]
        ph, pl_ = cut(jnp.concatenate(planar, 0))
        plan_h[z] = ph
        plan_l[z] = pl_
        both = mul_t(jnp.concatenate(lifted + rest, 0).astype(BF16), ph)
        more = mul_t(jnp.concatenate(lifted, 0).astype(BF16), pl_)
        sums = both[0:48] + both[48:96] + more
        block = jnp.where(low_lane, sums[0:24], sums[24:48])
        for c in range(3):
            grid[c, pl.ds(pl.multiple_of(z * 8, 8), 8), :] = block[c * 8 : c * 8 + 8]
        return carry

    lax.fori_loop(0, HALF, spread, 0, unroll=4)

    def along_z(first, v):
        pair = table_left(z_tab[first : first + 2], jnp.concatenate(v[0:2], 1))
        return pair[:, 0:128], pair[:, 128:256], table_left(z_tab[first + 2 : first + 4], v[2])

    for c, v in enumerate(along_z(0, [grid[c] for c in range(3)])):
        out_1[pl.ds(c, DEVICES, stride=8), :] = v

    pl.semaphore_wait(tell.at[2], ROWS - 1)

    def exchange(out, into, k):
        def post(p):
            pltpu.make_async_remote_copy(
                src_ref=out.at[pl.ds(pl.multiple_of(p * 8, 8), 3), :],
                dst_ref=into.at[pl.ds(pl.multiple_of(me * 8, 8), 3), :],
                send_sem=all_send.at[k],
                recv_sem=all_recv.at[k],
                device_id=p,
                device_id_type=LOGICAL,
            ).start()

        def post_bunch(i, carry):
            bunch = me // BUNCH + i
            first = jnp.where(bunch >= DEVICES // BUNCH, bunch - DEVICES // BUNCH, bunch) * BUNCH
            for n in range(BUNCH):
                post(first + n)
            return carry

        lax.fori_loop(1, DEVICES // BUNCH, post_bunch, 0)
        for n in range(1, BUNCH):
            post(me // BUNCH * BUNCH + lax.rem(me + n, BUNCH))
        mine = pl.ds(pl.multiple_of(me * 8, 8), 3)
        keep = pltpu.make_async_copy(out.at[mine, :], into.at[mine, :], self_sem.at[k])
        keep.start()
        keep.wait()
        bulk = out.at[pl.ds(0, 3 * (DEVICES - 1)), :]
        pltpu.make_async_copy(bulk, bulk, all_recv.at[k]).wait()

    exchange(out_1, in_1, 0)

    cos_t, sin_t = twist[0], twist[1]
    planes = jnp.concatenate([in_1[pl.ds(c, DEVICES, stride=8), :] for c in range(3)], 1)
    both = table_left(lf[...], planes)
    turned = []
    for c in range(3):
        re, im = both[0:128, c * 128 : c * 128 + 128], both[128:256, c * 128 : c * 128 + 128]
        turned.append(jnp.concatenate([re * cos_t + im * sin_t, im * cos_t - re * sin_t], 1))
    for c, v in enumerate(table_right(turned, rf)):
        work[c] = v

    special = me < 2
    plain = jnp.where(special, 1.0, 0.0).astype(F32)
    turn = jnp.where(special, 0, 2 * lax.rem(me, 2) - 1).astype(F32)
    kz = jnp.where(me == 1, -64, me // 2).astype(F32)
    kz_top = jnp.where(me == 1, -64, 0).astype(F32)
    kz_low = jnp.where(me == 1, 0, me // 2).astype(F32)

    def signed(v):
        return jnp.where(v < GRID // 2, v, v - GRID)

    def stokes(i, carry):
        rows = pl.ds(pl.multiple_of(i * 16, 16), 16)
        f1 = lax.broadcasted_iota(jnp.int32, (16, 128), 0) + i * 16
        f2 = lax.broadcasted_iota(jnp.int32, (16, 128), 1)
        ix = signed(f1 // 16 + 8 * (f2 // 8))
        iy = signed(f1 % 16 + 16 * (f2 % 8))
        kx, ky = ix.astype(F32), iy.astype(F32)
        kx_top = jnp.where(ix == -64, kx, 0.0)
        ky_top = jnp.where(iy == -64, ky, 0.0)
        kx_low, ky_low = kx - kx_top, ky - ky_top
        square = kx * kx + ky * ky + kz * kz
        damping = (0.25 / GRID**3) * jnp.exp(square * (-((math.pi / GRID) ** 2)))
        inverse = 1.0 / jnp.maximum(square, 1.0)
        w_re, w_im = work[2, rows, 0:128], work[2, rows, 128:256]
        sides = (
            (work[0, rows, 0:128], work[1, rows, 0:128], plain * w_re - turn * w_im),
            (work[0, rows, 128:256], work[1, rows, 128:256], plain * w_im + turn * w_re),
        )
        done = []
        for u, v, w in sides:
            low = (kx_low * u + ky_low * v + kz_low * w) * inverse
            top = (kx_top * u + ky_top * v + kz_top * w) * inverse
            done.append(
                (
                    damping * (u - kx_low * low - kx_top * top),
                    damping * (v - ky_low * low - ky_top * top),
                    damping * (w - kz_low * low - kz_top * top),
                )
            )
        for c in range(2):
            work[c, rows, 0:128] = done[0][c]
            work[c, rows, 128:256] = done[1][c]
        work[2, rows, 0:128] = plain * done[0][2] + turn * done[1][2]
        work[2, rows, 128:256] = plain * done[1][2] - turn * done[0][2]
        return carry

    lax.fori_loop(0, 8, stokes, 0)

    pairs = []
    for both in table_right([work[c] for c in range(3)], rb):
        re, im = both[:, 0:128], both[:, 128:256]
        pairs.append(jnp.concatenate([re * cos_t - im * sin_t, im * cos_t + re * sin_t], 0))
    planes = table_left(lb[...], jnp.concatenate(pairs, 1))
    for c in range(3):
        out_2[pl.ds(c, DEVICES, stride=8), :] = planes[:, c * 128 : c * 128 + 128]

    exchange(out_2, in_2, 1)

    for c, v in enumerate(along_z(4, [in_2[pl.ds(c, DEVICES, stride=8), :] for c in range(3)])):
        grid[c] = v

    def gather(z, carry):
        rows = pl.ds(pl.multiple_of(z * 8, 8), 8)
        block = jnp.concatenate([grid[c, rows, :] for c in range(3)], 0)
        near_half = jnp.where(low_lane, block, 0.0)
        far_half = block - near_half
        both = jnp.concatenate([near_half, far_half], 0)
        top = narrow(both)
        first = mul(jnp.concatenate([top, both - top], 0).astype(BF16), plan_h[z])
        second = mul(top.astype(BF16), plan_l[z])
        sums = first[0:48] + first[48:96] + second
        for h in range(2):
            spot = pl.ds(pl.multiple_of((h * HALF + z) * 8, 8), 8)
            bz = depth[spot, :]
            for c in range(3):
                far[c, spot, :] = sums[h * 24 + c * 8 : h * 24 + c * 8 + 8] * bz
        return carry

    lax.fori_loop(0, HALF, gather, 0)

    for c in range(3):
        total = far[c, pl.ds(0, CELLS, stride=8), :]
        for g in range(1, CELL):
            total = total + far[c, pl.ds(g, CELLS, stride=8), :]
        spin[c] = total * state[6]
    gives[2].start()

    for k in range(2):
        bulk = out_1.at[pl.ds(0, 3 * (DEVICES - 1)), :]
        pltpu.make_async_copy(bulk, bulk, all_send.at[k]).wait()
    for give in gives:
        give.wait()
    for step in range(STEPS):
        for copy in halo(step):
            copy.wait_send()
def shards(positions, torques, counts, neighbour_flags):
    shape = positions.shape
    flat = (3, CELLS, SLOT)
    tables = [jnp.asarray(t) for t in make_tables()]
    there = pl.BlockSpec(memory_space=pl.ANY)
    buffer = pltpu.VMEM((DEVICES * 8, 128), F32)
    out = pl.pallas_call(
        kernel,
        name="spinners",
        out_shape=jax.ShapeDtypeStruct((3,) + flat, F32),
        in_specs=[there] * (4 + len(tables)),
        out_specs=there,
        scratch_shapes=[
            pltpu.VMEM(flat, F32),
            pltpu.VMEM(flat, F32),
            pltpu.VMEM(flat, F32),
            pltpu.VMEM(flat, F32),
            pltpu.SMEM(counts.shape, jnp.int32),
            pltpu.SMEM(neighbour_flags.shape, jnp.int32),
            pltpu.SemaphoreType.DMA((7,)),
            pltpu.VMEM(flat, F32),
            pltpu.VMEM((7, CELLS, SLOT), F32),
            pltpu.VMEM((STEPS - 1, 3, CELLS, SLOT), F32),
            pltpu.VMEM((6, CELLS, SLOT), F32),
            pltpu.VMEM((CELLS * A_PITCH, SLOT), F32),
            pltpu.VMEM((CELLS // GROUP, SLOT, SLOT), BF16),
            pltpu.VMEM((7, CELLS * B_PITCH, SLOT), F32),
            pltpu.VMEM((7, CELLS * L_PITCH, SLOT), F32),
            pltpu.VMEM((CELLS * T_PITCH, SLOT), F32),
            pltpu.VMEM((CELLS * T_PITCH, SLOT), F32),
            pltpu.VMEM((CELLS * T_PITCH, SLOT), F32),
            pltpu.VMEM((2, 7, HALF, SLOT), F32),
            pltpu.VMEM((2, 7, CELLS, SLOT), F32),
            pltpu.VMEM((STEPS - 1, 2, 3, HALF, SLOT), F32),
            pltpu.VMEM((STEPS - 1, 2, 3, CELLS, SLOT), F32),
            pltpu.SemaphoreType.DMA((STEPS, 4)),
            pltpu.SemaphoreType.DMA((STEPS, 4)),
            pltpu.SemaphoreType.REGULAR((3,)),
        ]
        + [pltpu.VMEM(t.shape, t.dtype) for t in tables]
        + [
            pltpu.SemaphoreType.DMA((len(tables),)),
            pltpu.VMEM((3, GRID, 128), F32),
            pltpu.VMEM((HALF, 128, SLOT), BF16),
            pltpu.VMEM((HALF, 128, SLOT), BF16),
            pltpu.VMEM((CELLS * 8, SLOT), F32),
            buffer,
            buffer,
            buffer,
            buffer,
            pltpu.VMEM((3, 128, 256), F32),
            pltpu.VMEM((3, CELLS * 8, SLOT), F32),
            pltpu.SemaphoreType.DMA((2,)),
            pltpu.SemaphoreType.DMA((2,)),
            pltpu.SemaphoreType.DMA((2,)),
        ],
        compiler_params=pltpu.CompilerParams(collective_id=0, has_side_effects=True),
    )(positions.reshape(flat), torques.reshape(flat), counts, neighbour_flags, *tables)
    return (out[0] + MID).reshape(shape), (out[1] + out[2]).reshape(shape)


def solution(mesh):
    in_specs = (
        P(None, "row", "col", None, None),
        P(None, "row", "col", None, None),
        P("row", "col", None),
        P(None, "row", "col", None),
    )
    out_specs = (P(None, "row", "col", None, None), P(None, "row", "col", None, None))
    return jax.shard_map(shards, mesh=mesh, in_specs=in_specs, out_specs=out_specs, check_vma=False)
```

```python
import math

import jax
import jax.numpy as jnp
import numpy as np
from jax import lax
from jax.experimental import pallas as pl
from jax.experimental.pallas import tpu as pltpu
from jax.sharding import PartitionSpec as P

GRID = 128
CELL = 8
SLOT = 128
STEPS = 3
ROWS = 8
COLS = 16
DEVICES = ROWS * COLS
BUNCH = 8
CELLS = 32
HALF = 16
MESH = pl.DeviceIdType.MESH
LOGICAL = pl.DeviceIdType.LOGICAL
F32 = jnp.float32
BF16 = jnp.bfloat16

KAPPA = 2.0 / (CELL * CELL) * math.log2(math.e)
PACE = 0.06 * CELL
DRIFT = 1.0 / SLOT
COUPLE = 0.5 / SLOT
MID = 0.5 * CELL

A_ROWS = 32
GROUP = SLOT // A_ROWS
GROUPS = CELLS // GROUP
B_ROWS = 16
L_ROWS = 16
A_PITCH = A_ROWS + 1
B_PITCH = B_ROWS + 1
L_PITCH = L_ROWS + 1
T_PITCH = 9


def halves(table):
    high = table.astype(np.float32).astype(jnp.bfloat16)
    low = (table - high.astype(np.float64)).astype(np.float32).astype(jnp.bfloat16)
    return high, low


def make_tables():
    n = np.arange(GRID)
    level = np.where(n == 1, 64, n // 2)
    angle = 2.0 * np.pi * (level[:, None] * n[None, :] % GRID) / GRID
    cosine, sine = np.cos(angle), np.sin(angle)
    even = (n % 2 == 0)[:, None]
    whole = (n < 2)[:, None]
    basis_xy = np.where(whole | even, cosine, sine)
    basis_z = np.where(whole | ~even, cosine, sine)
    count = np.where(n < 2, 1.0, 2.0)[:, None]
    back_xy, back_z = (basis_xy * count).T, (basis_z * count).T

    def wave(a, b, period_a, period_b):
        return 2.0 * np.pi * ((a * b[0] % period_a) / period_a + (b[1] % period_b) / period_b)

    r, q = n // 16, n % 16
    turn_l = 2.0 * np.pi * ((r[:, None] * r[None, :] % 8) / 8 + (q[:, None] * q[None, :] % 16) / 16)
    s, t = n // 8, n % 8
    turn_r = 2.0 * np.pi * ((s[:, None] * s[None, :] % 16) / 16 + (t[:, None] * t[None, :] % 8) / 8)
    twist = 2.0 * np.pi * (r[:, None] * s[None, :] + q[:, None] * t[None, :]) / GRID
    cl, sl = np.cos(turn_l), np.sin(turn_l)
    cr, sr = np.cos(turn_r), np.sin(turn_r)
    left = np.concatenate([cl, -sl], 0)
    left_back = np.concatenate([cl, -sl], 1)
    right = np.block([[cr, -sr], [sr, cr]])
    right_back = np.block([[cr, sr], [-sr, cr]])
    along_z = [half for table in (basis_xy, basis_z, back_xy, back_z) for half in halves(table)]
    out = [np.stack(along_z)] + [np.stack(halves(table)) for table in (left, left_back, right, right_back)]
    return out + [np.stack([np.cos(twist), np.sin(twist)]).astype(np.float32)]


def cut(v):
    h = v.astype(BF16)
    return h, (v - h.astype(F32)).astype(BF16)


def mul(a, b):
    return jnp.dot(a, b, preferred_element_type=F32)


def mul_t(a, b):
    return lax.dot_general(a, b, (((1,), (1,)), ((), ())), preferred_element_type=F32)


def table_left(table, v):
    vh, vl = cut(v)
    rows = table.shape[1]
    both = mul(table.reshape(2 * rows, table.shape[2]), vh)
    return both[:rows] + (both[rows:] + mul(table[0], vl))


def table_right(parts, table):
    cuts = [cut(v) for v in parts]
    high = jnp.concatenate([h for h, _ in cuts], 0)
    both = mul(jnp.concatenate([high] + [l for _, l in cuts], 0), table[0])
    rows = high.shape[0]
    total = both[:rows] + (both[rows:] + mul(high, table[1]))
    size = parts[0].shape[0]
    return [total[n * size : (n + 1) * size] for n in range(len(parts))]


def narrow(v):
    return v.astype(BF16).astype(F32)


def split3(v):
    h = narrow(v)
    r = v - h
    m = narrow(r)
    return h, m, r - m


def put(ref, lead, start, stride, val):
    ref[lead, pl.ds(start, val.shape[0], stride=stride), :] = val


def put_receiver(afeat, half, px, py, pz):
    base = half * HALF * A_PITCH

    def row(k, v):
        afeat[pl.ds(base + k, HALF, stride=A_PITCH), :] = v

    size = split3(-KAPPA * (px * px + py * py + pz * pz))
    for d, v in enumerate((px, py, pz)):
        h, m, l = split3(v * (2.0 * KAPPA))
        row(d, h)
        row(8 + d, h)
        row(11 + d, h)
        row((7, 14, 15)[d], l)
        row(16 + d, m)
        row(24 + d, m)
    row(6, size[0])
    row(16 + 6, size[1])


def put_source(bfeat, lfeat, slot, half, place, torque, fill, shift, gate, loads_only=False):
    place = [place[d] + shift[d] if shift[d] != 0.0 else place[d] for d in range(3)]
    x, y, z = place
    if not loads_only:
        base = half * HALF * B_PITCH
        for d in range(3):
            h, m, l = split3(place[d])
            put(bfeat, slot, base + d, B_PITCH, h)
            put(bfeat, slot, base + 8 + d, B_PITCH, m)
            put(bfeat, slot, base + 11 + d, B_PITCH, l)
            put(bfeat, slot, base + (7, 14, 15)[d], B_PITCH, h)
        for k, v in enumerate(split3(-KAPPA * (x * x + y * y + z * z))):
            put(bfeat, slot, base + 3 + k, B_PITCH, v)
    if gate is not None:
        torque = [t * gate for t in torque]
        fill = fill * gate
    tx, ty, tz = torque
    loads = (tx, ty, tz, ty * z - tz * y, tz * x - tx * z, tx * y - ty * x)
    base = half * HALF * L_PITCH
    for q, v in enumerate(loads):
        h = narrow(v)
        put(lfeat, slot, base + q, L_PITCH, h)
        put(lfeat, slot, base + 8 + q, L_PITCH, v - h)
    put(lfeat, slot, base + 6, L_PITCH, fill)


def kernel(
    pos_far, tor_far, cnt_far, flg_far, z_far, lf_far, lb_far, rf_far, rb_far, twist_far, out_far,
    pos_in, tor_in, pos_out, spin, cnt, flg, field_sem, near_out, state, places, gates, afeat, trans, bfeat, lfeat, totals, totals_z, totals_x,
    full_x, full_y, part_x, part_y, send_sem, recv_sem, tell,
    z_tab, lf, lb, rf, rb, twist, table_sem,
    grid, plan_h, plan_l, depth, out_1, in_1, out_2, in_2, work, far, all_send, all_recv, self_sem,
):
    row = lax.axis_index("row")
    col = lax.axis_index("col")
    peers = (
        (lax.rem(row + 1, ROWS), col),
        (lax.rem(row + ROWS - 1, ROWS), col),
        (row, lax.rem(col + 1, COLS)),
        (row, lax.rem(col + COLS - 1, COLS)),
    )
    barrier = pltpu.get_barrier_semaphore()
    for peer in peers:
        pl.semaphore_signal(barrier, inc=1, device_id=peer, device_id_type=MESH)

    fields = [
        pltpu.make_async_copy(src, dst, field_sem.at[k])
        for k, (src, dst) in enumerate(((pos_far, pos_in), (tor_far, tor_in), (cnt_far, cnt), (flg_far, flg)))
    ]
    for field in fields:
        field.start()
    tables = [
        pltpu.make_async_copy(src, dst, table_sem.at[k])
        for k, (src, dst) in enumerate(
            ((z_far, z_tab), (lf_far, lf), (lb_far, lb), (rf_far, rf), (rb_far, rb), (twist_far, twist))
        )
    ]
    for table in tables:
        table.start()

    def inform(k, steps):
        for down, right in steps:
            where = (lax.rem(row + down + ROWS, ROWS), lax.rem(col + right + COLS, COLS))
            pl.semaphore_signal(tell.at[k], inc=1, device_id=where, device_id_type=MESH)

    def learn(step):
        if step == 0:
            inform(0, ((2, 0), (-2, 0), (0, 2), (0, -2)))
        elif step == 1:
            pl.semaphore_wait(tell.at[0], 4)
            inform(1, ((0, 4), (0, -4)))
        else:
            pl.semaphore_wait(tell.at[1], 2)
            inform(2, [(k, 0) for k in range(1, ROWS)])

    lane = lax.broadcasted_iota(jnp.int32, (1, SLOT), 1)

    def spread_scalars(z, carry):
        for h in range(2):
            state[6, pl.ds(h * HALF + z, 1), :] = (lane < cnt[h, 0, z]).astype(F32)
            for f in range(6):
                gates[f, pl.ds(h * HALF + z, 1), :] = jnp.full((1, SLOT), flg[f, h, 0, z], jnp.int32).astype(F32)
        return carry

    for field in fields:
        field.wait()
    lax.fori_loop(0, HALF, spread_scalars, 0)
    fill = state[6]
    for d in range(3):
        state[d] = pos_in[d] - MID
        state[3 + d] = tor_in[d] * fill

    pl.semaphore_wait(barrier, 4)

    def halo(step):
        if step == 0:
            own, into_x, into_y = state, full_x, full_y
        else:
            own, into_x, into_y = places.at[step - 1], part_x.at[step - 1], part_y.at[step - 1]
        moves = (
            (own.at[:, pl.ds(HALF, HALF), :], into_x.at[0], 0),
            (own.at[:, pl.ds(0, HALF), :], into_x.at[1], 1),
            (own, into_y.at[0], 2),
            (own, into_y.at[1], 3),
        )
        copies = []
        for src, dst, k in moves:
            copies.append(
                pltpu.make_async_remote_copy(
                    src_ref=src,
                    dst_ref=dst,
                    send_sem=send_sem.at[step, k],
                    recv_sem=recv_sem.at[step, k],
                    device_id=peers[k],
                    device_id_type=MESH,
                )
            )
        return copies

    one = jnp.ones((CELLS, SLOT), F32)
    zero = jnp.zeros((CELLS, SLOT), F32)
    for k in (19, 20, 21, 23, 27, 28, 29, 30, 31):
        afeat[pl.ds(k, CELLS, stride=A_PITCH), :] = zero
    for k in (3, 4, 5):
        afeat[pl.ds(k, CELLS, stride=A_PITCH), :] = one
    totals_x[pl.ds(0, HALF * T_PITCH), :] = jnp.zeros((HALF * T_PITCH, SLOT), F32)
    for e in range(7):
        put(bfeat, e, 6, B_PITCH, one)
        for k in (7, 14, 15):
            put(lfeat, e, k, L_PITCH, zero)

    owner = lax.broadcasted_iota(jnp.int32, (SLOT, SLOT), 1) // A_ROWS

    def wide(ref, n, cell, faces):
        blocks = [ref[e, pl.ds(cell * (n + 1), n), :] for e in faces]
        return (blocks[0] if len(blocks) == 1 else jnp.concatenate(blocks, 1)).astype(BF16)

    def powers(group, faces):
        block = trans[group]
        ats = [jnp.where(owner == k, block, jnp.zeros_like(block)) for k in range(GROUP)]
        b = []
        for k in range(GROUP):
            part = wide(bfeat, B_ROWS, group * GROUP + k, faces)
            b += [part, part]
        return jnp.dot(jnp.concatenate(ats, 0), jnp.concatenate(b, 0), preferred_element_type=F32)

    def add_up(load, w, side):
        acc = lax.dot_general(load, w, (((1,), (side,)), ((), ())), preferred_element_type=F32)
        return acc[0:8] + acc[8:16]

    def inner_cell(group, k, faces, power):
        cell = group * GROUP + k
        w = jnp.exp2(power[k * SLOT : (k + 1) * SLOT]).astype(BF16)
        totals[pl.ds(cell * T_PITCH, 8), :] = add_up(wide(lfeat, L_ROWS, cell, faces), w, 1)
        upper = (cell // HALF) * HALF + (cell + 1) % HALF
        load = wide(lfeat, L_ROWS, upper, (2,))
        if len(faces) == 2:
            totals_z[pl.ds(upper * T_PITCH, 8), :] = add_up(load, w[:, SLOT:], 0)
        else:
            load = jnp.concatenate([load, wide(lfeat, L_ROWS, cell + HALF, (3,))], 0)
            acc = lax.dot_general(load, w[:, SLOT:], (((1,), (0,)), ((), ())), preferred_element_type=F32)
            totals_z[pl.ds(upper * T_PITCH, 8), :] = acc[0:8, 0:SLOT] + acc[8:16, 0:SLOT]
            totals_x[pl.ds((cell + HALF) * T_PITCH, 8), :] = acc[16:24, SLOT:] + acc[24:32, SLOT:]

    def inner_faces(i, carry):
        sides = ((i, (0, 1, 3)), (i + GROUPS // 2, (0, 1)))
        both = [powers(g, faces) for g, faces in sides]
        for k, n in [(k, n) for k in range(GROUP) for n in range(2)]:
            inner_cell(sides[n][0], k, sides[n][1], both[n])

        return carry

    def turn_receivers(group):
        rows = [afeat[pl.ds((group * GROUP + k) * A_PITCH, A_ROWS), :] for k in range(GROUP)]
        trans[group] = jnp.concatenate(rows, 0).T.astype(BF16)

    def outer_faces(i, carry):
        both = [powers(i + g * (GROUPS // 2), (4, 5, 6)) for g in range(2)]
        for cell, power, k in [((i + g * (GROUPS // 2)) * GROUP + k, both[g], k) for g in range(2) for k in range(GROUP)]:
            w = jnp.exp2(power[k * SLOT : (k + 1) * SLOT]).astype(BF16)
            spot = pl.ds(cell * T_PITCH, 8)
            totals[spot, :] = totals[spot, :] + add_up(wide(lfeat, L_ROWS, cell, (4, 5, 6)), w, 1)
        return carry

    for step in range(STEPS):
        copies = halo(step)
        for copy in copies:
            copy.start()
        here = state if step == 0 else places.at[step - 1]
        for h in range(2):
            part = slice(h * HALF, (h + 1) * HALF)
            other = slice((1 - h) * HALF, (2 - h) * HALF)
            place = [here[d, part, :] for d in range(3)]
            torque = [state[3 + d, part, :] for d in range(3)]
            fill = state[6, part, :]
            put_receiver(afeat, h, *place)
            put_source(bfeat, lfeat, 0, h, place, torque, fill, (0.0, 0.0, 0.0), None)
            for slot, turn, lift, face in ((1, HALF - 1, CELL, 4), (2, 1, -CELL, 5)):
                def turned(v):
                    return pltpu.roll(v, turn, 0)

                put_source(
                    bfeat, lfeat, slot, h, [turned(v) for v in place], [turned(v) for v in torque], turned(fill),
                    (0.0, 0.0, float(lift)), gates[face, part, :], loads_only=slot == 2,
                )
            put_source(
                bfeat, lfeat, 3, h,
                [here[d, other, :] for d in range(3)],
                [state[3 + d, other, :] for d in range(3)],
                state[6, other, :],
                (float(CELL) if h == 0 else -float(CELL), 0.0, 0.0),
                gates[0 if h == 0 else 1, part, :],
                loads_only=h == 1,
            )
        for g in range(GROUPS):
            turn_receivers(g)
        lax.fori_loop(0, GROUPS // 2, inner_faces, 0)
        for copy in copies:
            copy.wait_recv()
        learn(step)
        for h in range(2):
            part = slice(h * HALF, (h + 1) * HALF)
            near_x = full_x if step == 0 else part_x.at[step - 1]
            near_y = full_y if step == 0 else part_y.at[step - 1]
            put_source(
                bfeat, lfeat, 4, h,
                [near_x[h, d] for d in range(3)],
                [full_x[h, 3 + d] for d in range(3)],
                full_x[h, 6],
                (-float(CELL) if h == 0 else float(CELL), 0.0, 0.0),
                gates[1 if h == 0 else 0, part, :],
            )
            for slot, side, lift, face in ((5, 1, CELL, 2), (6, 0, -CELL, 3)):
                put_source(
                    bfeat, lfeat, slot, h,
                    [near_y[side, d, part, :] for d in range(3)],
                    [full_y[side, 3 + d, part, :] for d in range(3)],
                    full_y[side, 6, part, :],
                    (0.0, float(lift), 0.0),
                    gates[face, part, :],
                )
        lax.fori_loop(0, GROUPS // 2, outer_faces, 0)

        tot = []
        for q in range(7):
            rows = pl.ds(q, CELLS, stride=T_PITCH)
            tot.append(totals[rows, :] + totals_z[rows, :] + totals_x[rows, :])
        fill = state[6]
        x, y, z = (here[d] for d in range(3))
        speed = (
            tot[1] * z - tot[2] * y - tot[3],
            tot[2] * x - tot[0] * z - tot[4],
            tot[0] * y - tot[1] * x - tot[5],
        )
        for d in range(3):
            moved = here[d] + PACE * (DRIFT * speed[d] * fill)
            if step < STEPS - 1:
                places[step, d] = moved
            else:
                pos_out[d] = moved
                torque = tor_in[d]
                near_out[d] = (torque + COUPLE * (tot[d] - tot[6] * torque)) * fill

    me = row * COLS + col

    level = lax.broadcasted_iota(jnp.int32, (CELL, SLOT), 0).astype(F32) + 0.5
    low_lane = lax.broadcasted_iota(jnp.int32, (24, SLOT), 1) < 64

    gives = [pltpu.make_async_copy(src, out_far.at[k], field_sem.at[4 + k]) for k, src in enumerate((pos_out, near_out, spin))]
    for give in gives[0:2]:
        give.start()
    for table in tables:
        table.wait()

    def bins(d, cell):
        apart = pos_out[d, pl.ds(cell, 1), :] + MID - level
        return jnp.exp(-apart * apart)

    def spread(z, carry):
        planar, lifted, rest = [], [], []
        for h in range(2):
            cell = h * HALF + z
            bx, by, bz = (bins(d, cell) for d in range(3))
            depth[pl.ds(pl.multiple_of(cell * 8, 8), 8), :] = bz
            planar += [bx[a : a + 1, :] * by for a in range(CELL)]
            lift = [state[3 + c, pl.ds(cell, 1), :] * bz for c in range(3)]
            top = [narrow(v) for v in lift]
            lifted += top
            rest += [v - t for v, t in zip(lift, top)]
        ph, pl_ = cut(jnp.concatenate(planar, 0))
        plan_h[z] = ph
        plan_l[z] = pl_
        both = mul_t(jnp.concatenate(lifted + rest, 0).astype(BF16), ph)
        more = mul_t(jnp.concatenate(lifted, 0).astype(BF16), pl_)
        sums = both[0:48] + both[48:96] + more
        block = jnp.where(low_lane, sums[0:24], sums[24:48])
        for c in range(3):
            grid[c, pl.ds(pl.multiple_of(z * 8, 8), 8), :] = block[c * 8 : c * 8 + 8]
        return carry

    lax.fori_loop(0, HALF, spread, 0, unroll=16)

    def along_z(first, v):
        pair = table_left(z_tab[first : first + 2], jnp.concatenate(v[0:2], 1))
        return pair[:, 0:128], pair[:, 128:256], table_left(z_tab[first + 2 : first + 4], v[2])

    for c, v in enumerate(along_z(0, [grid[c] for c in range(3)])):
        out_1[pl.ds(c, DEVICES, stride=8), :] = v

    pl.semaphore_wait(tell.at[2], ROWS - 1)

    def exchange(out, into, k):
        def post(p):
            pltpu.make_async_remote_copy(
                src_ref=out.at[pl.ds(pl.multiple_of(p * 8, 8), 3), :],
                dst_ref=into.at[pl.ds(pl.multiple_of(me * 8, 8), 3), :],
                send_sem=all_send.at[k],
                recv_sem=all_recv.at[k],
                device_id=p,
                device_id_type=LOGICAL,
            ).start()

        layer, place = me // BUNCH // 4, lax.rem(me // BUNCH, 4)

        def post_bunch(i, carry):
            turn = i // 4
            target = layer + jnp.where(turn == 2, 3, jnp.where(turn == 3, 0, 2 - turn))
            target = jnp.where(target >= 4, target - 4, target)
            first = (target * 4 + (place + i) % 4) * BUNCH
            for n in range(BUNCH):
                post(first + n)
            return carry

        lax.fori_loop(0, 12, post_bunch, 0)
        lax.fori_loop(13, 16, post_bunch, 0)
        for n in range(1, BUNCH):
            post(me // BUNCH * BUNCH + lax.rem(me + n, BUNCH))
        mine = pl.ds(pl.multiple_of(me * 8, 8), 3)
        keep = pltpu.make_async_copy(out.at[mine, :], into.at[mine, :], self_sem.at[k])
        keep.start()
        keep.wait()
        bulk = out.at[pl.ds(0, 3 * (DEVICES - 1)), :]
        pltpu.make_async_copy(bulk, bulk, all_recv.at[k]).wait()

    exchange(out_1, in_1, 0)

    cos_t, sin_t = twist[0], twist[1]
    planes = jnp.concatenate([in_1[pl.ds(c, DEVICES, stride=8), :] for c in range(3)], 1)
    both = table_left(lf[...], planes)
    turned = []
    for c in range(3):
        re, im = both[0:128, c * 128 : c * 128 + 128], both[128:256, c * 128 : c * 128 + 128]
        turned.append(jnp.concatenate([re * cos_t + im * sin_t, im * cos_t - re * sin_t], 1))
    for c, v in enumerate(table_right(turned, rf)):
        work[c] = v

    special = me < 2
    plain = jnp.where(special, 1.0, 0.0).astype(F32)
    turn = jnp.where(special, 0, 2 * lax.rem(me, 2) - 1).astype(F32)
    kz = jnp.where(me == 1, -64, me // 2).astype(F32)
    kz_top = jnp.where(me == 1, -64, 0).astype(F32)
    kz_low = jnp.where(me == 1, 0, me // 2).astype(F32)

    def signed(v):
        return jnp.where(v < GRID // 2, v, v - GRID)

    def stokes(i, carry):
        rows = pl.ds(pl.multiple_of(i * 16, 16), 16)
        f1 = lax.broadcasted_iota(jnp.int32, (16, 128), 0) + i * 16
        f2 = lax.broadcasted_iota(jnp.int32, (16, 128), 1)
        ix = signed(f1 // 16 + 8 * (f2 // 8))
        iy = signed(f1 % 16 + 16 * (f2 % 8))
        kx, ky = ix.astype(F32), iy.astype(F32)
        kx_top = jnp.where(ix == -64, kx, 0.0)
        ky_top = jnp.where(iy == -64, ky, 0.0)
        kx_low, ky_low = kx - kx_top, ky - ky_top
        square = kx * kx + ky * ky + kz * kz
        damping = (0.25 / GRID**3) * jnp.exp(square * (-((math.pi / GRID) ** 2)))
        inverse = 1.0 / jnp.maximum(square, 1.0)
        w_re, w_im = work[2, rows, 0:128], work[2, rows, 128:256]
        sides = (
            (work[0, rows, 0:128], work[1, rows, 0:128], plain * w_re - turn * w_im),
            (work[0, rows, 128:256], work[1, rows, 128:256], plain * w_im + turn * w_re),
        )
        done = []
        for u, v, w in sides:
            low = (kx_low * u + ky_low * v + kz_low * w) * inverse
            top = (kx_top * u + ky_top * v + kz_top * w) * inverse
            done.append(
                (
                    damping * (u - kx_low * low - kx_top * top),
                    damping * (v - ky_low * low - ky_top * top),
                    damping * (w - kz_low * low - kz_top * top),
                )
            )
        for c in range(2):
            work[c, rows, 0:128] = done[0][c]
            work[c, rows, 128:256] = done[1][c]
        work[2, rows, 0:128] = plain * done[0][2] + turn * done[1][2]
        work[2, rows, 128:256] = plain * done[1][2] - turn * done[0][2]
        return carry

    lax.fori_loop(0, 8, stokes, 0)

    pairs = []
    for both in table_right([work[c] for c in range(3)], rb):
        re, im = both[:, 0:128], both[:, 128:256]
        pairs.append(jnp.concatenate([re * cos_t - im * sin_t, im * cos_t + re * sin_t], 0))
    planes = table_left(lb[...], jnp.concatenate(pairs, 1))
    for c in range(3):
        out_2[pl.ds(c, DEVICES, stride=8), :] = planes[:, c * 128 : c * 128 + 128]

    exchange(out_2, in_2, 1)

    for c, v in enumerate(along_z(4, [in_2[pl.ds(c, DEVICES, stride=8), :] for c in range(3)])):
        grid[c] = v

    def gather(z, carry):
        rows = pl.ds(pl.multiple_of(z * 8, 8), 8)
        block = jnp.concatenate([grid[c, rows, :] for c in range(3)], 0)
        near_half = jnp.where(low_lane, block, 0.0)
        far_half = block - near_half
        both = jnp.concatenate([near_half, far_half], 0)
        top = narrow(both)
        first = mul(jnp.concatenate([top, both - top], 0).astype(BF16), plan_h[z])
        second = mul(top.astype(BF16), plan_l[z])
        sums = first[0:48] + first[48:96] + second
        for h in range(2):
            spot = pl.ds(pl.multiple_of((h * HALF + z) * 8, 8), 8)
            bz = depth[spot, :]
            for c in range(3):
                far[c, spot, :] = sums[h * 24 + c * 8 : h * 24 + c * 8 + 8] * bz
        return carry

    lax.fori_loop(0, HALF, gather, 0, unroll=8)

    for c in range(3):
        total = far[c, pl.ds(0, CELLS, stride=8), :]
        for g in range(1, CELL):
            total = total + far[c, pl.ds(g, CELLS, stride=8), :]
        spin[c] = total * state[6]
    gives[2].start()

    for k in range(2):
        bulk = out_1.at[pl.ds(0, 3 * (DEVICES - 1)), :]
        pltpu.make_async_copy(bulk, bulk, all_send.at[k]).wait()
    for give in gives:
        give.wait()
    for step in range(STEPS):
        for copy in halo(step):
            copy.wait_send()
def shards(positions, torques, counts, neighbour_flags):
    shape = positions.shape
    flat = (3, CELLS, SLOT)
    tables = [jnp.asarray(t) for t in make_tables()]
    there = pl.BlockSpec(memory_space=pl.ANY)
    buffer = pltpu.VMEM((DEVICES * 8, 128), F32)
    out = pl.pallas_call(
        kernel,
        name="spinners",
        out_shape=jax.ShapeDtypeStruct((3,) + flat, F32),
        in_specs=[there] * (4 + len(tables)),
        out_specs=there,
        scratch_shapes=[
            pltpu.VMEM(flat, F32),
            pltpu.VMEM(flat, F32),
            pltpu.VMEM(flat, F32),
            pltpu.VMEM(flat, F32),
            pltpu.SMEM(counts.shape, jnp.int32),
            pltpu.SMEM(neighbour_flags.shape, jnp.int32),
            pltpu.SemaphoreType.DMA((7,)),
            pltpu.VMEM(flat, F32),
            pltpu.VMEM((7, CELLS, SLOT), F32),
            pltpu.VMEM((STEPS - 1, 3, CELLS, SLOT), F32),
            pltpu.VMEM((6, CELLS, SLOT), F32),
            pltpu.VMEM((CELLS * A_PITCH, SLOT), F32),
            pltpu.VMEM((CELLS // GROUP, SLOT, SLOT), BF16),
            pltpu.VMEM((7, CELLS * B_PITCH, SLOT), F32),
            pltpu.VMEM((7, CELLS * L_PITCH, SLOT), F32),
            pltpu.VMEM((CELLS * T_PITCH, SLOT), F32),
            pltpu.VMEM((CELLS * T_PITCH, SLOT), F32),
            pltpu.VMEM((CELLS * T_PITCH, SLOT), F32),
            pltpu.VMEM((2, 7, HALF, SLOT), F32),
            pltpu.VMEM((2, 7, CELLS, SLOT), F32),
            pltpu.VMEM((STEPS - 1, 2, 3, HALF, SLOT), F32),
            pltpu.VMEM((STEPS - 1, 2, 3, CELLS, SLOT), F32),
            pltpu.SemaphoreType.DMA((STEPS, 4)),
            pltpu.SemaphoreType.DMA((STEPS, 4)),
            pltpu.SemaphoreType.REGULAR((3,)),
        ]
        + [pltpu.VMEM(t.shape, t.dtype) for t in tables]
        + [
            pltpu.SemaphoreType.DMA((len(tables),)),
            pltpu.VMEM((3, GRID, 128), F32),
            pltpu.VMEM((HALF, 128, SLOT), BF16),
            pltpu.VMEM((HALF, 128, SLOT), BF16),
            pltpu.VMEM((CELLS * 8, SLOT), F32),
            buffer,
            buffer,
            buffer,
            buffer,
            pltpu.VMEM((3, 128, 256), F32),
            pltpu.VMEM((3, CELLS * 8, SLOT), F32),
            pltpu.SemaphoreType.DMA((2,)),
            pltpu.SemaphoreType.DMA((2,)),
            pltpu.SemaphoreType.DMA((2,)),
        ],
        compiler_params=pltpu.CompilerParams(collective_id=0, has_side_effects=True),
    )(positions.reshape(flat), torques.reshape(flat), counts, neighbour_flags, *tables)
    return (out[0] + MID).reshape(shape), (out[1] + out[2]).reshape(shape)


def solution(mesh):
    in_specs = (
        P(None, "row", "col", None, None),
        P(None, "row", "col", None, None),
        P("row", "col", None),
        P(None, "row", "col", None),
    )
    out_specs = (P(None, "row", "col", None, None), P(None, "row", "col", None, None))
    return jax.shard_map(shards, mesh=mesh, in_specs=in_specs, out_specs=out_specs, check_vma=False)
```

```python
import math

import jax
import jax.numpy as jnp
import numpy as np
from jax import lax
from jax.experimental import pallas as pl
from jax.experimental.pallas import tpu as pltpu
from jax.sharding import PartitionSpec as P

GRID = 128
CELL = 8
SLOT = 128
STEPS = 3
ROWS = 8
COLS = 16
DEVICES = ROWS * COLS
BUNCH = 8
CELLS = 32
HALF = 16
MESH = pl.DeviceIdType.MESH
LOGICAL = pl.DeviceIdType.LOGICAL
F32 = jnp.float32
BF16 = jnp.bfloat16

KAPPA = 2.0 / (CELL * CELL) * math.log2(math.e)
PACE = 0.06 * CELL
DRIFT = 1.0 / SLOT
COUPLE = 0.5 / SLOT
MID = 0.5 * CELL

A_ROWS = 32
GROUP = SLOT // A_ROWS
GROUPS = CELLS // GROUP
B_ROWS = 16
L_ROWS = 16
A_PITCH = A_ROWS + 1
B_PITCH = B_ROWS + 1
L_PITCH = L_ROWS + 1
T_PITCH = 9


def halves(table):
    high = table.astype(np.float32).astype(jnp.bfloat16)
    low = (table - high.astype(np.float64)).astype(np.float32).astype(jnp.bfloat16)
    return high, low


def make_tables():
    n = np.arange(GRID)
    level = np.where(n == 1, 64, n // 2)
    angle = 2.0 * np.pi * (level[:, None] * n[None, :] % GRID) / GRID
    cosine, sine = np.cos(angle), np.sin(angle)
    even = (n % 2 == 0)[:, None]
    whole = (n < 2)[:, None]
    basis_xy = np.where(whole | even, cosine, sine)
    basis_z = np.where(whole | ~even, cosine, sine)
    count = np.where(n < 2, 1.0, 2.0)[:, None]
    back_xy, back_z = (basis_xy * count).T, (basis_z * count).T

    def wave(a, b, period_a, period_b):
        return 2.0 * np.pi * ((a * b[0] % period_a) / period_a + (b[1] % period_b) / period_b)

    r, q = n // 16, n % 16
    turn_l = 2.0 * np.pi * ((r[:, None] * r[None, :] % 8) / 8 + (q[:, None] * q[None, :] % 16) / 16)
    s, t = n // 8, n % 8
    turn_r = 2.0 * np.pi * ((s[:, None] * s[None, :] % 16) / 16 + (t[:, None] * t[None, :] % 8) / 8)
    twist = 2.0 * np.pi * (r[:, None] * s[None, :] + q[:, None] * t[None, :]) / GRID
    cl, sl = np.cos(turn_l), np.sin(turn_l)
    cr, sr = np.cos(turn_r), np.sin(turn_r)
    left = np.concatenate([cl, -sl], 0)
    left_back = np.concatenate([cl, -sl], 1)
    right = np.block([[cr, -sr], [sr, cr]])
    right_back = np.block([[cr, sr], [-sr, cr]])
    along_z = [half for table in (basis_xy, basis_z, back_xy, back_z) for half in halves(table)]
    out = [np.stack(along_z)] + [np.stack(halves(table)) for table in (left, left_back, right, right_back)]
    return out + [np.stack([np.cos(twist), np.sin(twist)]).astype(np.float32)]


def cut(v):
    h = v.astype(BF16)
    return h, (v - h.astype(F32)).astype(BF16)


def mul(a, b):
    return jnp.dot(a, b, preferred_element_type=F32)


def mul_t(a, b):
    return lax.dot_general(a, b, (((1,), (1,)), ((), ())), preferred_element_type=F32)


def table_left(table, v):
    vh, vl = cut(v)
    rows = table.shape[1]
    both = mul(table.reshape(2 * rows, table.shape[2]), vh)
    return both[:rows] + (both[rows:] + mul(table[0], vl))


def table_right(parts, table):
    cuts = [cut(v) for v in parts]
    high = jnp.concatenate([h for h, _ in cuts], 0)
    both = mul(jnp.concatenate([high] + [l for _, l in cuts], 0), table[0])
    rows = high.shape[0]
    total = both[:rows] + (both[rows:] + mul(high, table[1]))
    size = parts[0].shape[0]
    return [total[n * size : (n + 1) * size] for n in range(len(parts))]


def narrow(v):
    return v.astype(BF16).astype(F32)


def split3(v):
    h = narrow(v)
    r = v - h
    m = narrow(r)
    return h, m, r - m


def put(ref, lead, start, stride, val):
    ref[lead, pl.ds(start, val.shape[0], stride=stride), :] = val


def put_receiver(afeat, half, px, py, pz):
    base = half * HALF * A_PITCH

    def row(k, v):
        afeat[pl.ds(base + k, HALF, stride=A_PITCH), :] = v

    size = split3(-KAPPA * (px * px + py * py + pz * pz))
    for d, v in enumerate((px, py, pz)):
        h, m, l = split3(v * (2.0 * KAPPA))
        row(d, h)
        row(8 + d, h)
        row(11 + d, h)
        row((7, 14, 15)[d], l)
        row(16 + d, m)
        row(24 + d, m)
    row(6, size[0])
    row(16 + 6, size[1])


def put_source(bfeat, lfeat, slot, half, place, torque, fill, shift, gate, loads_only=False):
    place = [place[d] + shift[d] if shift[d] != 0.0 else place[d] for d in range(3)]
    x, y, z = place
    if not loads_only:
        base = half * HALF * B_PITCH
        for d in range(3):
            h, m, l = split3(place[d])
            put(bfeat, slot, base + d, B_PITCH, h)
            put(bfeat, slot, base + 8 + d, B_PITCH, m)
            put(bfeat, slot, base + 11 + d, B_PITCH, l)
            put(bfeat, slot, base + (7, 14, 15)[d], B_PITCH, h)
        for k, v in enumerate(split3(-KAPPA * (x * x + y * y + z * z))):
            put(bfeat, slot, base + 3 + k, B_PITCH, v)
    if gate is not None:
        torque = [t * gate for t in torque]
        fill = fill * gate
    tx, ty, tz = torque
    loads = (tx, ty, tz, ty * z - tz * y, tz * x - tx * z, tx * y - ty * x)
    base = half * HALF * L_PITCH
    for q, v in enumerate(loads):
        h = narrow(v)
        put(lfeat, slot, base + q, L_PITCH, h)
        put(lfeat, slot, base + 8 + q, L_PITCH, v - h)
    put(lfeat, slot, base + 6, L_PITCH, fill)


def kernel(
    pos_far, tor_far, cnt_far, flg_far, z_far, lf_far, lb_far, rf_far, rb_far, twist_far, out_far,
    pos_in, tor_in, pos_out, spin, cnt, flg, field_sem, near_out, state, places, gates, afeat, trans, bfeat, lfeat, totals, totals_z, totals_x,
    full_x, full_y, part_x, part_y, send_sem, recv_sem, tell,
    z_tab, lf, lb, rf, rb, twist, table_sem,
    grid, plan_h, plan_l, depth, out_1, in_1, out_2, in_2, work, far, all_send, all_recv, self_sem,
):
    row = lax.axis_index("row")
    col = lax.axis_index("col")
    peers = (
        (lax.rem(row + 1, ROWS), col),
        (lax.rem(row + ROWS - 1, ROWS), col),
        (row, lax.rem(col + 1, COLS)),
        (row, lax.rem(col + COLS - 1, COLS)),
    )
    barrier = pltpu.get_barrier_semaphore()
    for peer in peers:
        pl.semaphore_signal(barrier, inc=1, device_id=peer, device_id_type=MESH)

    fields = [
        pltpu.make_async_copy(src, dst, field_sem.at[k])
        for k, (src, dst) in enumerate(((pos_far, pos_in), (tor_far, tor_in), (cnt_far, cnt), (flg_far, flg)))
    ]
    for field in fields:
        field.start()
    tables = [
        pltpu.make_async_copy(src, dst, table_sem.at[k])
        for k, (src, dst) in enumerate(
            ((z_far, z_tab), (lf_far, lf), (lb_far, lb), (rf_far, rf), (rb_far, rb), (twist_far, twist))
        )
    ]
    for table in tables:
        table.start()

    def inform(k, steps):
        for down, right in steps:
            where = (lax.rem(row + down + ROWS, ROWS), lax.rem(col + right + COLS, COLS))
            pl.semaphore_signal(tell.at[k], inc=1, device_id=where, device_id_type=MESH)

    def learn(step):
        if step == 0:
            inform(0, ((2, 0), (-2, 0), (0, 2), (0, -2)))
        elif step == 1:
            pl.semaphore_wait(tell.at[0], 4)
            inform(1, ((0, 4), (0, -4)))
        else:
            pl.semaphore_wait(tell.at[1], 2)
            inform(2, [(k, 0) for k in range(1, ROWS)])

    lane = lax.broadcasted_iota(jnp.int32, (1, SLOT), 1)

    def spread_scalars(z, carry):
        for h in range(2):
            state[6, pl.ds(h * HALF + z, 1), :] = (lane < cnt[h, 0, z]).astype(F32)
            for f in range(6):
                gates[f, pl.ds(h * HALF + z, 1), :] = jnp.full((1, SLOT), flg[f, h, 0, z], jnp.int32).astype(F32)
        return carry

    for field in fields:
        field.wait()
    lax.fori_loop(0, HALF, spread_scalars, 0, unroll=8)
    fill = state[6]
    for d in range(3):
        state[d] = pos_in[d] - MID
        state[3 + d] = tor_in[d] * fill

    pl.semaphore_wait(barrier, 4)

    def halo(step):
        if step == 0:
            own, into_x, into_y = state, full_x, full_y
        else:
            own, into_x, into_y = places.at[step - 1], part_x.at[step - 1], part_y.at[step - 1]
        moves = (
            (own.at[:, pl.ds(HALF, HALF), :], into_x.at[0], 0),
            (own.at[:, pl.ds(0, HALF), :], into_x.at[1], 1),
            (own, into_y.at[0], 2),
            (own, into_y.at[1], 3),
        )
        copies = []
        for src, dst, k in moves:
            copies.append(
                pltpu.make_async_remote_copy(
                    src_ref=src,
                    dst_ref=dst,
                    send_sem=send_sem.at[step, k],
                    recv_sem=recv_sem.at[step, k],
                    device_id=peers[k],
                    device_id_type=MESH,
                )
            )
        return copies

    one = jnp.ones((CELLS, SLOT), F32)
    zero = jnp.zeros((CELLS, SLOT), F32)
    for k in (19, 20, 21, 23, 27, 28, 29, 30, 31):
        afeat[pl.ds(k, CELLS, stride=A_PITCH), :] = zero
    for k in (3, 4, 5):
        afeat[pl.ds(k, CELLS, stride=A_PITCH), :] = one
    totals_x[pl.ds(0, HALF * T_PITCH), :] = jnp.zeros((HALF * T_PITCH, SLOT), F32)
    for e in range(7):
        put(bfeat, e, 6, B_PITCH, one)
        for k in (7, 14, 15):
            put(lfeat, e, k, L_PITCH, zero)

    owner = lax.broadcasted_iota(jnp.int32, (SLOT, SLOT), 1) // A_ROWS

    def wide(ref, n, cell, faces):
        blocks = [ref[e, pl.ds(cell * (n + 1), n), :] for e in faces]
        return (blocks[0] if len(blocks) == 1 else jnp.concatenate(blocks, 1)).astype(BF16)

    def powers(group, faces):
        block = trans[group]
        ats = [jnp.where(owner == k, block, jnp.zeros_like(block)) for k in range(GROUP)]
        b = []
        for k in range(GROUP):
            part = wide(bfeat, B_ROWS, group * GROUP + k, faces)
            b += [part, part]
        return jnp.dot(jnp.concatenate(ats, 0), jnp.concatenate(b, 0), preferred_element_type=F32)

    def add_up(load, w, side):
        acc = lax.dot_general(load, w, (((1,), (side,)), ((), ())), preferred_element_type=F32)
        return acc[0:8] + acc[8:16]

    def inner_cell(group, k, faces, power):
        cell = group * GROUP + k
        w = jnp.exp2(power[k * SLOT : (k + 1) * SLOT]).astype(BF16)
        totals[pl.ds(cell * T_PITCH, 8), :] = add_up(wide(lfeat, L_ROWS, cell, faces), w, 1)
        upper = (cell // HALF) * HALF + (cell + 1) % HALF
        load = wide(lfeat, L_ROWS, upper, (2,))
        if len(faces) == 2:
            totals_z[pl.ds(upper * T_PITCH, 8), :] = add_up(load, w[:, SLOT:], 0)
        else:
            load = jnp.concatenate([load, wide(lfeat, L_ROWS, cell + HALF, (3,))], 0)
            acc = lax.dot_general(load, w[:, SLOT:], (((1,), (0,)), ((), ())), preferred_element_type=F32)
            totals_z[pl.ds(upper * T_PITCH, 8), :] = acc[0:8, 0:SLOT] + acc[8:16, 0:SLOT]
            totals_x[pl.ds((cell + HALF) * T_PITCH, 8), :] = acc[16:24, SLOT:] + acc[24:32, SLOT:]

    def inner_faces(i, carry):
        sides = ((i, (0, 1, 3)), (i + GROUPS // 2, (0, 1)))
        both = [powers(g, faces) for g, faces in sides]
        for k, n in [(k, n) for k in range(GROUP) for n in range(2)]:
            inner_cell(sides[n][0], k, sides[n][1], both[n])

        return carry

    def turn_receivers(group):
        rows = [afeat[pl.ds((group * GROUP + k) * A_PITCH, A_ROWS), :] for k in range(GROUP)]
        trans[group] = jnp.concatenate(rows, 0).T.astype(BF16)

    def outer_faces(i, carry):
        both = [powers(i + g * (GROUPS // 2), (4, 5, 6)) for g in range(2)]
        for cell, power, k in [((i + g * (GROUPS // 2)) * GROUP + k, both[g], k) for g in range(2) for k in range(GROUP)]:
            w = jnp.exp2(power[k * SLOT : (k + 1) * SLOT]).astype(BF16)
            spot = pl.ds(cell * T_PITCH, 8)
            totals[spot, :] = totals[spot, :] + add_up(wide(lfeat, L_ROWS, cell, (4, 5, 6)), w, 1)
        return carry

    for step in range(STEPS):
        copies = halo(step)
        for copy in copies:
            copy.start()
        here = state if step == 0 else places.at[step - 1]
        for h in range(2):
            part = slice(h * HALF, (h + 1) * HALF)
            other = slice((1 - h) * HALF, (2 - h) * HALF)
            place = [here[d, part, :] for d in range(3)]
            torque = [state[3 + d, part, :] for d in range(3)]
            fill = state[6, part, :]
            put_receiver(afeat, h, *place)
            put_source(bfeat, lfeat, 0, h, place, torque, fill, (0.0, 0.0, 0.0), None)
            for slot, turn, lift, face in ((1, HALF - 1, CELL, 4), (2, 1, -CELL, 5)):
                def turned(v):
                    return pltpu.roll(v, turn, 0)

                put_source(
                    bfeat, lfeat, slot, h, [turned(v) for v in place], [turned(v) for v in torque], turned(fill),
                    (0.0, 0.0, float(lift)), gates[face, part, :], loads_only=slot == 2,
                )
            put_source(
                bfeat, lfeat, 3, h,
                [here[d, other, :] for d in range(3)],
                [state[3 + d, other, :] for d in range(3)],
                state[6, other, :],
                (float(CELL) if h == 0 else -float(CELL), 0.0, 0.0),
                gates[0 if h == 0 else 1, part, :],
                loads_only=h == 1,
            )
        for g in range(GROUPS):
            turn_receivers(g)
        lax.fori_loop(0, GROUPS // 2, inner_faces, 0)
        for copy in copies:
            copy.wait_recv()
        learn(step)
        for h in range(2):
            part = slice(h * HALF, (h + 1) * HALF)
            near_x = full_x if step == 0 else part_x.at[step - 1]
            near_y = full_y if step == 0 else part_y.at[step - 1]
            put_source(
                bfeat, lfeat, 4, h,
                [near_x[h, d] for d in range(3)],
                [full_x[h, 3 + d] for d in range(3)],
                full_x[h, 6],
                (-float(CELL) if h == 0 else float(CELL), 0.0, 0.0),
                gates[1 if h == 0 else 0, part, :],
            )
            for slot, side, lift, face in ((5, 1, CELL, 2), (6, 0, -CELL, 3)):
                put_source(
                    bfeat, lfeat, slot, h,
                    [near_y[side, d, part, :] for d in range(3)],
                    [full_y[side, 3 + d, part, :] for d in range(3)],
                    full_y[side, 6, part, :],
                    (0.0, float(lift), 0.0),
                    gates[face, part, :],
                )
        lax.fori_loop(0, GROUPS // 2, outer_faces, 0)

        tot = []
        for q in range(7):
            rows = pl.ds(q, CELLS, stride=T_PITCH)
            tot.append(totals[rows, :] + totals_z[rows, :] + totals_x[rows, :])
        fill = state[6]
        x, y, z = (here[d] for d in range(3))
        speed = (
            tot[1] * z - tot[2] * y - tot[3],
            tot[2] * x - tot[0] * z - tot[4],
            tot[0] * y - tot[1] * x - tot[5],
        )
        for d in range(3):
            moved = here[d] + PACE * (DRIFT * speed[d] * fill)
            if step < STEPS - 1:
                places[step, d] = moved
            else:
                pos_out[d] = moved
                torque = tor_in[d]
                near_out[d] = (torque + COUPLE * (tot[d] - tot[6] * torque)) * fill

    me = row * COLS + col

    level = lax.broadcasted_iota(jnp.int32, (CELL, SLOT), 0).astype(F32) + 0.5
    low_lane = lax.broadcasted_iota(jnp.int32, (24, SLOT), 1) < 64

    gives = [pltpu.make_async_copy(src, out_far.at[k], field_sem.at[4 + k]) for k, src in enumerate((pos_out, near_out, spin))]
    for give in gives[0:2]:
        give.start()
    for table in tables:
        table.wait()

    def bins(d, cell):
        apart = pos_out[d, pl.ds(cell, 1), :] + MID - level
        return jnp.exp(-apart * apart)

    def spread(z, carry):
        planar, lifted, rest = [], [], []
        for h in range(2):
            cell = h * HALF + z
            bx, by, bz = (bins(d, cell) for d in range(3))
            depth[pl.ds(pl.multiple_of(cell * 8, 8), 8), :] = bz
            planar += [bx[a : a + 1, :] * by for a in range(CELL)]
            lift = [state[3 + c, pl.ds(cell, 1), :] * bz for c in range(3)]
            top = [narrow(v) for v in lift]
            lifted += top
            rest += [v - t for v, t in zip(lift, top)]
        ph, pl_ = cut(jnp.concatenate(planar, 0))
        plan_h[z] = ph
        plan_l[z] = pl_
        both = mul_t(jnp.concatenate(lifted + rest, 0).astype(BF16), ph)
        more = mul_t(jnp.concatenate(lifted, 0).astype(BF16), pl_)
        sums = both[0:48] + both[48:96] + more
        block = jnp.where(low_lane, sums[0:24], sums[24:48])
        for c in range(3):
            grid[c, pl.ds(pl.multiple_of(z * 8, 8), 8), :] = block[c * 8 : c * 8 + 8]
        return carry

    lax.fori_loop(0, HALF, spread, 0, unroll=16)

    def along_z(first, v):
        pair = table_left(z_tab[first : first + 2], jnp.concatenate(v[0:2], 1))
        return pair[:, 0:128], pair[:, 128:256], table_left(z_tab[first + 2 : first + 4], v[2])

    for c, v in enumerate(along_z(0, [grid[c] for c in range(3)])):
        out_1[pl.ds(c, DEVICES, stride=8), :] = v

    pl.semaphore_wait(tell.at[2], ROWS - 1)

    def exchange(out, into, k):
        def post(p):
            pltpu.make_async_remote_copy(
                src_ref=out.at[pl.ds(pl.multiple_of(p * 8, 8), 3), :],
                dst_ref=into.at[pl.ds(pl.multiple_of(me * 8, 8), 3), :],
                send_sem=all_send.at[k],
                recv_sem=all_recv.at[k],
                device_id=p,
                device_id_type=LOGICAL,
            ).start()

        layer, place = me // BUNCH // 4, lax.rem(me // BUNCH, 4)

        def post_bunch(i, carry):
            turn = i // 4
            target = layer + jnp.where(turn == 2, 3, jnp.where(turn == 3, 0, 2 - turn))
            target = jnp.where(target >= 4, target - 4, target)
            first = (target * 4 + (place + i) % 4) * BUNCH
            for n in range(BUNCH):
                post(first + n)
            return carry

        lax.fori_loop(0, 12, post_bunch, 0)
        lax.fori_loop(13, 16, post_bunch, 0)
        for n in range(1, BUNCH):
            post(me // BUNCH * BUNCH + lax.rem(me + n, BUNCH))
        mine = pl.ds(pl.multiple_of(me * 8, 8), 3)
        keep = pltpu.make_async_copy(out.at[mine, :], into.at[mine, :], self_sem.at[k])
        keep.start()
        keep.wait()
        bulk = out.at[pl.ds(0, 3 * (DEVICES - 1)), :]
        pltpu.make_async_copy(bulk, bulk, all_recv.at[k]).wait()

    exchange(out_1, in_1, 0)

    cos_t, sin_t = twist[0], twist[1]
    planes = jnp.concatenate([in_1[pl.ds(c, DEVICES, stride=8), :] for c in range(3)], 1)
    both = table_left(lf[...], planes)
    turned = []
    for c in range(3):
        re, im = both[0:128, c * 128 : c * 128 + 128], both[128:256, c * 128 : c * 128 + 128]
        turned.append(jnp.concatenate([re * cos_t + im * sin_t, im * cos_t - re * sin_t], 1))
    for c, v in enumerate(table_right(turned, rf)):
        work[c] = v

    special = me < 2
    plain = jnp.where(special, 1.0, 0.0).astype(F32)
    turn = jnp.where(special, 0, 2 * lax.rem(me, 2) - 1).astype(F32)
    kz = jnp.where(me == 1, -64, me // 2).astype(F32)
    kz_top = jnp.where(me == 1, -64, 0).astype(F32)
    kz_low = jnp.where(me == 1, 0, me // 2).astype(F32)

    def signed(v):
        return jnp.where(v < GRID // 2, v, v - GRID)

    def stokes(i, carry):
        rows = pl.ds(pl.multiple_of(i * 16, 16), 16)
        f1 = lax.broadcasted_iota(jnp.int32, (16, 128), 0) + i * 16
        f2 = lax.broadcasted_iota(jnp.int32, (16, 128), 1)
        ix = signed(f1 // 16 + 8 * (f2 // 8))
        iy = signed(f1 % 16 + 16 * (f2 % 8))
        kx, ky = ix.astype(F32), iy.astype(F32)
        kx_top = jnp.where(ix == -64, kx, 0.0)
        ky_top = jnp.where(iy == -64, ky, 0.0)
        kx_low, ky_low = kx - kx_top, ky - ky_top
        square = kx * kx + ky * ky + kz * kz
        damping = (0.25 / GRID**3) * jnp.exp(square * (-((math.pi / GRID) ** 2)))
        inverse = 1.0 / jnp.maximum(square, 1.0)
        w_re, w_im = work[2, rows, 0:128], work[2, rows, 128:256]
        sides = (
            (work[0, rows, 0:128], work[1, rows, 0:128], plain * w_re - turn * w_im),
            (work[0, rows, 128:256], work[1, rows, 128:256], plain * w_im + turn * w_re),
        )
        done = []
        for u, v, w in sides:
            low = (kx_low * u + ky_low * v + kz_low * w) * inverse
            top = (kx_top * u + ky_top * v + kz_top * w) * inverse
            done.append(
                (
                    damping * (u - kx_low * low - kx_top * top),
                    damping * (v - ky_low * low - ky_top * top),
                    damping * (w - kz_low * low - kz_top * top),
                )
            )
        for c in range(2):
            work[c, rows, 0:128] = done[0][c]
            work[c, rows, 128:256] = done[1][c]
        work[2, rows, 0:128] = plain * done[0][2] + turn * done[1][2]
        work[2, rows, 128:256] = plain * done[1][2] - turn * done[0][2]
        return carry

    lax.fori_loop(0, 8, stokes, 0, unroll=8)

    pairs = []
    for both in table_right([work[c] for c in range(3)], rb):
        re, im = both[:, 0:128], both[:, 128:256]
        pairs.append(jnp.concatenate([re * cos_t - im * sin_t, im * cos_t + re * sin_t], 0))
    planes = table_left(lb[...], jnp.concatenate(pairs, 1))
    for c in range(3):
        out_2[pl.ds(c, DEVICES, stride=8), :] = planes[:, c * 128 : c * 128 + 128]

    exchange(out_2, in_2, 1)

    for c, v in enumerate(along_z(4, [in_2[pl.ds(c, DEVICES, stride=8), :] for c in range(3)])):
        grid[c] = v

    def gather(z, carry):
        rows = pl.ds(pl.multiple_of(z * 8, 8), 8)
        block = jnp.concatenate([grid[c, rows, :] for c in range(3)], 0)
        near_half = jnp.where(low_lane, block, 0.0)
        far_half = block - near_half
        both = jnp.concatenate([near_half, far_half], 0)
        top = narrow(both)
        first = mul(jnp.concatenate([top, both - top], 0).astype(BF16), plan_h[z])
        second = mul(top.astype(BF16), plan_l[z])
        sums = first[0:48] + first[48:96] + second
        for h in range(2):
            spot = pl.ds(pl.multiple_of((h * HALF + z) * 8, 8), 8)
            bz = depth[spot, :]
            for c in range(3):
                far[c, spot, :] = sums[h * 24 + c * 8 : h * 24 + c * 8 + 8] * bz
        return carry

    lax.fori_loop(0, HALF, gather, 0, unroll=16)

    for c in range(3):
        total = far[c, pl.ds(0, CELLS, stride=8), :]
        for g in range(1, CELL):
            total = total + far[c, pl.ds(g, CELLS, stride=8), :]
        spin[c] = total * state[6]
    gives[2].start()

    for k in range(2):
        bulk = out_1.at[pl.ds(0, 3 * (DEVICES - 1)), :]
        pltpu.make_async_copy(bulk, bulk, all_send.at[k]).wait()
    for give in gives:
        give.wait()
    for step in range(STEPS):
        for copy in halo(step):
            copy.wait_send()
def shards(positions, torques, counts, neighbour_flags):
    shape = positions.shape
    flat = (3, CELLS, SLOT)
    tables = [jnp.asarray(t) for t in make_tables()]
    there = pl.BlockSpec(memory_space=pl.ANY)
    buffer = pltpu.VMEM((DEVICES * 8, 128), F32)
    out = pl.pallas_call(
        kernel,
        name="spinners",
        out_shape=jax.ShapeDtypeStruct((3,) + flat, F32),
        in_specs=[there] * (4 + len(tables)),
        out_specs=there,
        scratch_shapes=[
            pltpu.VMEM(flat, F32),
            pltpu.VMEM(flat, F32),
            pltpu.VMEM(flat, F32),
            pltpu.VMEM(flat, F32),
            pltpu.SMEM(counts.shape, jnp.int32),
            pltpu.SMEM(neighbour_flags.shape, jnp.int32),
            pltpu.SemaphoreType.DMA((7,)),
            pltpu.VMEM(flat, F32),
            pltpu.VMEM((7, CELLS, SLOT), F32),
            pltpu.VMEM((STEPS - 1, 3, CELLS, SLOT), F32),
            pltpu.VMEM((6, CELLS, SLOT), F32),
            pltpu.VMEM((CELLS * A_PITCH, SLOT), F32),
            pltpu.VMEM((CELLS // GROUP, SLOT, SLOT), BF16),
            pltpu.VMEM((7, CELLS * B_PITCH, SLOT), F32),
            pltpu.VMEM((7, CELLS * L_PITCH, SLOT), F32),
            pltpu.VMEM((CELLS * T_PITCH, SLOT), F32),
            pltpu.VMEM((CELLS * T_PITCH, SLOT), F32),
            pltpu.VMEM((CELLS * T_PITCH, SLOT), F32),
            pltpu.VMEM((2, 7, HALF, SLOT), F32),
            pltpu.VMEM((2, 7, CELLS, SLOT), F32),
            pltpu.VMEM((STEPS - 1, 2, 3, HALF, SLOT), F32),
            pltpu.VMEM((STEPS - 1, 2, 3, CELLS, SLOT), F32),
            pltpu.SemaphoreType.DMA((STEPS, 4)),
            pltpu.SemaphoreType.DMA((STEPS, 4)),
            pltpu.SemaphoreType.REGULAR((3,)),
        ]
        + [pltpu.VMEM(t.shape, t.dtype) for t in tables]
        + [
            pltpu.SemaphoreType.DMA((len(tables),)),
            pltpu.VMEM((3, GRID, 128), F32),
            pltpu.VMEM((HALF, 128, SLOT), BF16),
            pltpu.VMEM((HALF, 128, SLOT), BF16),
            pltpu.VMEM((CELLS * 8, SLOT), F32),
            buffer,
            buffer,
            buffer,
            buffer,
            pltpu.VMEM((3, 128, 256), F32),
            pltpu.VMEM((3, CELLS * 8, SLOT), F32),
            pltpu.SemaphoreType.DMA((2,)),
            pltpu.SemaphoreType.DMA((2,)),
            pltpu.SemaphoreType.DMA((2,)),
        ],
        compiler_params=pltpu.CompilerParams(collective_id=0, has_side_effects=True),
    )(positions.reshape(flat), torques.reshape(flat), counts, neighbour_flags, *tables)
    return (out[0] + MID).reshape(shape), (out[1] + out[2]).reshape(shape)


def solution(mesh):
    in_specs = (
        P(None, "row", "col", None, None),
        P(None, "row", "col", None, None),
        P("row", "col", None),
        P(None, "row", "col", None),
    )
    out_specs = (P(None, "row", "col", None, None), P(None, "row", "col", None, None))
    return jax.shard_map(shards, mesh=mesh, in_specs=in_specs, out_specs=out_specs, check_vma=False)
```

```python
import math

import jax
import jax.numpy as jnp
import numpy as np
from jax import lax
from jax.experimental import pallas as pl
from jax.experimental.pallas import tpu as pltpu
from jax.sharding import PartitionSpec as P

GRID = 128
CELL = 8
SLOT = 128
STEPS = 3
ROWS = 8
COLS = 16
DEVICES = ROWS * COLS
BUNCH = 8
CELLS = 32
HALF = 16
MESH = pl.DeviceIdType.MESH
LOGICAL = pl.DeviceIdType.LOGICAL
F32 = jnp.float32
BF16 = jnp.bfloat16

KAPPA = 2.0 / (CELL * CELL) * math.log2(math.e)
PACE = 0.06 * CELL
DRIFT = 1.0 / SLOT
COUPLE = 0.5 / SLOT
MID = 0.5 * CELL

A_ROWS = 32
GROUP = SLOT // A_ROWS
GROUPS = CELLS // GROUP
B_ROWS = 16
L_ROWS = 16
A_PITCH = A_ROWS + 1
B_PITCH = B_ROWS + 1
L_PITCH = L_ROWS + 1
T_PITCH = 9


def halves(table):
    high = table.astype(np.float32).astype(jnp.bfloat16)
    low = (table - high.astype(np.float64)).astype(np.float32).astype(jnp.bfloat16)
    return high, low


def make_tables():
    n = np.arange(GRID)
    level = np.where(n == 1, 64, n // 2)
    angle = 2.0 * np.pi * (level[:, None] * n[None, :] % GRID) / GRID
    cosine, sine = np.cos(angle), np.sin(angle)
    even = (n % 2 == 0)[:, None]
    whole = (n < 2)[:, None]
    basis_xy = np.where(whole | even, cosine, sine)
    basis_z = np.where(whole | ~even, cosine, sine)
    count = np.where(n < 2, 1.0, 2.0)[:, None]
    back_xy, back_z = (basis_xy * count).T, (basis_z * count).T

    def wave(a, b, period_a, period_b):
        return 2.0 * np.pi * ((a * b[0] % period_a) / period_a + (b[1] % period_b) / period_b)

    r, q = n // 16, n % 16
    turn_l = 2.0 * np.pi * ((r[:, None] * r[None, :] % 8) / 8 + (q[:, None] * q[None, :] % 16) / 16)
    s, t = n // 8, n % 8
    turn_r = 2.0 * np.pi * ((s[:, None] * s[None, :] % 16) / 16 + (t[:, None] * t[None, :] % 8) / 8)
    twist = 2.0 * np.pi * (r[:, None] * s[None, :] + q[:, None] * t[None, :]) / GRID
    cl, sl = np.cos(turn_l), np.sin(turn_l)
    cr, sr = np.cos(turn_r), np.sin(turn_r)
    left = np.concatenate([cl, -sl], 0)
    left_back = np.concatenate([cl, -sl], 1)
    right = np.block([[cr, -sr], [sr, cr]])
    right_back = np.block([[cr, sr], [-sr, cr]])
    along_z = [half for table in (basis_xy, basis_z, back_xy, back_z) for half in halves(table)]
    out = [np.stack(along_z)] + [np.stack(halves(table)) for table in (left, left_back, right, right_back)]
    return out + [np.stack([np.cos(twist), np.sin(twist)]).astype(np.float32)]


def cut(v):
    h = v.astype(BF16)
    return h, (v - h.astype(F32)).astype(BF16)


def mul(a, b):
    return jnp.dot(a, b, preferred_element_type=F32)


def mul_t(a, b):
    return lax.dot_general(a, b, (((1,), (1,)), ((), ())), preferred_element_type=F32)


def table_left(table, v):
    vh, vl = cut(v)
    rows = table.shape[1]
    both = mul(table.reshape(2 * rows, table.shape[2]), vh)
    return both[:rows] + (both[rows:] + mul(table[0], vl))


def table_right(parts, table):
    cuts = [cut(v) for v in parts]
    high = jnp.concatenate([h for h, _ in cuts], 0)
    both = mul(jnp.concatenate([high] + [l for _, l in cuts], 0), table[0])
    rows = high.shape[0]
    total = both[:rows] + (both[rows:] + mul(high, table[1]))
    size = parts[0].shape[0]
    return [total[n * size : (n + 1) * size] for n in range(len(parts))]


def narrow(v):
    return v.astype(BF16).astype(F32)


def split3(v):
    h = narrow(v)
    r = v - h
    m = narrow(r)
    return h, m, r - m


def put(ref, lead, start, stride, val):
    ref[lead, pl.ds(start, val.shape[0], stride=stride), :] = val


def put_receiver(afeat, half, px, py, pz):
    base = half * HALF * A_PITCH

    def row(k, v):
        afeat[pl.ds(base + k, HALF, stride=A_PITCH), :] = v

    size = split3(-KAPPA * (px * px + py * py + pz * pz))
    for d, v in enumerate((px, py, pz)):
        h, m, l = split3(v * (2.0 * KAPPA))
        row(d, h)
        row(8 + d, h)
        row(11 + d, h)
        row((7, 14, 15)[d], l)
        row(16 + d, m)
        row(24 + d, m)
    row(6, size[0])
    row(16 + 6, size[1])


def put_source(bfeat, lfeat, slot, half, place, torque, fill, shift, gate, loads_only=False):
    place = [place[d] + shift[d] if shift[d] != 0.0 else place[d] for d in range(3)]
    x, y, z = place
    if not loads_only:
        base = half * HALF * B_PITCH
        for d in range(3):
            h, m, l = split3(place[d])
            put(bfeat, slot, base + d, B_PITCH, h)
            put(bfeat, slot, base + 8 + d, B_PITCH, m)
            put(bfeat, slot, base + 11 + d, B_PITCH, l)
            put(bfeat, slot, base + (7, 14, 15)[d], B_PITCH, h)
        for k, v in enumerate(split3(-KAPPA * (x * x + y * y + z * z))):
            put(bfeat, slot, base + 3 + k, B_PITCH, v)
    if gate is not None:
        torque = [t * gate for t in torque]
        fill = fill * gate
    tx, ty, tz = torque
    loads = (tx, ty, tz, ty * z - tz * y, tz * x - tx * z, tx * y - ty * x)
    base = half * HALF * L_PITCH
    for q, v in enumerate(loads):
        h = narrow(v)
        put(lfeat, slot, base + q, L_PITCH, h)
        put(lfeat, slot, base + 8 + q, L_PITCH, v - h)
    put(lfeat, slot, base + 6, L_PITCH, fill)


def kernel(
    pos_far, tor_far, cnt_far, flg_far, z_far, lf_far, lb_far, rf_far, rb_far, twist_far, out_far,
    pos_in, tor_in, pos_out, spin, cnt, flg, field_sem, near_out, state, places, gates, afeat, trans, bfeat, lfeat, totals, totals_z, totals_x,
    full_x, full_y, part_x, part_y, send_sem, recv_sem, tell,
    z_tab, lf, lb, rf, rb, twist, table_sem,
    grid, plan_h, plan_l, depth, out_1, in_1, out_2, in_2, work, far, all_send, all_recv, self_sem,
):
    row = lax.axis_index("row")
    col = lax.axis_index("col")
    peers = (
        (lax.rem(row + 1, ROWS), col),
        (lax.rem(row + ROWS - 1, ROWS), col),
        (row, lax.rem(col + 1, COLS)),
        (row, lax.rem(col + COLS - 1, COLS)),
    )
    barrier = pltpu.get_barrier_semaphore()
    for peer in peers:
        pl.semaphore_signal(barrier, inc=1, device_id=peer, device_id_type=MESH)

    fields = [
        pltpu.make_async_copy(src, dst, field_sem.at[k])
        for k, (src, dst) in enumerate(((pos_far, pos_in), (tor_far, tor_in), (cnt_far, cnt), (flg_far, flg)))
    ]
    for field in fields:
        field.start()
    tables = [
        pltpu.make_async_copy(src, dst, table_sem.at[k])
        for k, (src, dst) in enumerate(
            ((z_far, z_tab), (lf_far, lf), (lb_far, lb), (rf_far, rf), (rb_far, rb), (twist_far, twist))
        )
    ]
    for table in tables:
        table.start()

    def inform(k, steps):
        for down, right in steps:
            where = (lax.rem(row + down + ROWS, ROWS), lax.rem(col + right + COLS, COLS))
            pl.semaphore_signal(tell.at[k], inc=1, device_id=where, device_id_type=MESH)

    def learn(step):
        if step == 0:
            inform(0, ((2, 0), (-2, 0), (0, 2), (0, -2)))
        elif step == 1:
            pl.semaphore_wait(tell.at[0], 4)
            inform(1, ((0, 4), (0, -4)))
        else:
            pl.semaphore_wait(tell.at[1], 2)
            inform(2, [(k, 0) for k in range(1, ROWS)])

    lane = lax.broadcasted_iota(jnp.int32, (1, SLOT), 1)

    def spread_scalars(z, carry):
        for h in range(2):
            state[6, pl.ds(h * HALF + z, 1), :] = (lane < cnt[h, 0, z]).astype(F32)
            for f in range(6):
                gates[f, pl.ds(h * HALF + z, 1), :] = jnp.full((1, SLOT), flg[f, h, 0, z], jnp.int32).astype(F32)
        return carry

    for field in fields:
        field.wait()
    lax.fori_loop(0, HALF, spread_scalars, 0, unroll=8)
    fill = state[6]
    for d in range(3):
        state[d] = pos_in[d] - MID
        state[3 + d] = tor_in[d] * fill

    pl.semaphore_wait(barrier, 4)

    def halo(step):
        if step == 0:
            own, into_x, into_y = state, full_x, full_y
        else:
            own, into_x, into_y = places.at[step - 1], part_x.at[step - 1], part_y.at[step - 1]
        moves = (
            (own.at[:, pl.ds(HALF, HALF), :], into_x.at[0], 0),
            (own.at[:, pl.ds(0, HALF), :], into_x.at[1], 1),
            (own, into_y.at[0], 2),
            (own, into_y.at[1], 3),
        )
        copies = []
        for src, dst, k in moves:
            copies.append(
                pltpu.make_async_remote_copy(
                    src_ref=src,
                    dst_ref=dst,
                    send_sem=send_sem.at[step, k],
                    recv_sem=recv_sem.at[step, k],
                    device_id=peers[k],
                    device_id_type=MESH,
                )
            )
        return copies

    one = jnp.ones((CELLS, SLOT), F32)
    zero = jnp.zeros((CELLS, SLOT), F32)
    for k in (19, 20, 21, 23, 27, 28, 29, 30, 31):
        afeat[pl.ds(k, CELLS, stride=A_PITCH), :] = zero
    for k in (3, 4, 5):
        afeat[pl.ds(k, CELLS, stride=A_PITCH), :] = one
    totals_x[pl.ds(0, HALF * T_PITCH), :] = jnp.zeros((HALF * T_PITCH, SLOT), F32)
    for e in range(7):
        put(bfeat, e, 6, B_PITCH, one)
        for k in (7, 14, 15):
            put(lfeat, e, k, L_PITCH, zero)

    owner = lax.broadcasted_iota(jnp.int32, (SLOT, SLOT), 1) // A_ROWS

    def wide(ref, n, cell, faces):
        blocks = [ref[e, pl.ds(cell * (n + 1), n), :] for e in faces]
        return (blocks[0] if len(blocks) == 1 else jnp.concatenate(blocks, 1)).astype(BF16)

    def powers(group, faces):
        block = trans[group]
        ats = [jnp.where(owner == k, block, jnp.zeros_like(block)) for k in range(GROUP)]
        b = []
        for k in range(GROUP):
            part = wide(bfeat, B_ROWS, group * GROUP + k, faces)
            b += [part, part]
        return jnp.dot(jnp.concatenate(ats, 0), jnp.concatenate(b, 0), preferred_element_type=F32)

    def add_up(load, w, side):
        acc = lax.dot_general(load, w, (((1,), (side,)), ((), ())), preferred_element_type=F32)
        return acc[0:8] + acc[8:16]

    def inner_cell(group, k, faces, power):
        cell = group * GROUP + k
        w = jnp.exp2(power[k * SLOT : (k + 1) * SLOT]).astype(BF16)
        totals[pl.ds(cell * T_PITCH, 8), :] = add_up(wide(lfeat, L_ROWS, cell, faces), w, 1)
        upper = (cell // HALF) * HALF + (cell + 1) % HALF
        load = wide(lfeat, L_ROWS, upper, (2,))
        if len(faces) == 2:
            totals_z[pl.ds(upper * T_PITCH, 8), :] = add_up(load, w[:, SLOT:], 0)
        else:
            load = jnp.concatenate([load, wide(lfeat, L_ROWS, cell + HALF, (3,))], 0)
            acc = lax.dot_general(load, w[:, SLOT:], (((1,), (0,)), ((), ())), preferred_element_type=F32)
            totals_z[pl.ds(upper * T_PITCH, 8), :] = acc[0:8, 0:SLOT] + acc[8:16, 0:SLOT]
            totals_x[pl.ds((cell + HALF) * T_PITCH, 8), :] = acc[16:24, SLOT:] + acc[24:32, SLOT:]

    def inner_faces(i, carry):
        sides = ((i, (0, 1, 3)), (i + GROUPS // 2, (0, 1)))
        both = [powers(g, faces) for g, faces in sides]
        for k, n in [(k, n) for k in range(GROUP) for n in range(2)]:
            inner_cell(sides[n][0], k, sides[n][1], both[n])

        return carry

    def turn_receivers(group):
        rows = [afeat[pl.ds((group * GROUP + k) * A_PITCH, A_ROWS), :] for k in range(GROUP)]
        trans[group] = jnp.concatenate(rows, 0).T.astype(BF16)

    def outer_faces(i, carry):
        both = [powers(i + g * (GROUPS // 2), (4, 5, 6)) for g in range(2)]
        for cell, power, k in [((i + g * (GROUPS // 2)) * GROUP + k, both[g], k) for g in range(2) for k in range(GROUP)]:
            w = jnp.exp2(power[k * SLOT : (k + 1) * SLOT]).astype(BF16)
            spot = pl.ds(cell * T_PITCH, 8)
            totals[spot, :] = totals[spot, :] + add_up(wide(lfeat, L_ROWS, cell, (4, 5, 6)), w, 1)
        return carry

    for step in range(STEPS):
        copies = halo(step)
        for copy in copies:
            copy.start()
        here = state if step == 0 else places.at[step - 1]
        for h in range(2):
            part = slice(h * HALF, (h + 1) * HALF)
            other = slice((1 - h) * HALF, (2 - h) * HALF)
            place = [here[d, part, :] for d in range(3)]
            torque = [state[3 + d, part, :] for d in range(3)]
            fill = state[6, part, :]
            put_receiver(afeat, h, *place)
            put_source(bfeat, lfeat, 0, h, place, torque, fill, (0.0, 0.0, 0.0), None)
            for slot, turn, lift, face in ((1, HALF - 1, CELL, 4), (2, 1, -CELL, 5)):
                def turned(v):
                    return pltpu.roll(v, turn, 0)

                put_source(
                    bfeat, lfeat, slot, h, [turned(v) for v in place], [turned(v) for v in torque], turned(fill),
                    (0.0, 0.0, float(lift)), gates[face, part, :], loads_only=slot == 2,
                )
            put_source(
                bfeat, lfeat, 3, h,
                [here[d, other, :] for d in range(3)],
                [state[3 + d, other, :] for d in range(3)],
                state[6, other, :],
                (float(CELL) if h == 0 else -float(CELL), 0.0, 0.0),
                gates[0 if h == 0 else 1, part, :],
                loads_only=h == 1,
            )
        for g in range(GROUPS):
            turn_receivers(g)
        lax.fori_loop(0, GROUPS // 2, inner_faces, 0)
        for copy in copies:
            copy.wait_recv()
        learn(step)
        for h in range(2):
            part = slice(h * HALF, (h + 1) * HALF)
            near_x = full_x if step == 0 else part_x.at[step - 1]
            near_y = full_y if step == 0 else part_y.at[step - 1]
            put_source(
                bfeat, lfeat, 4, h,
                [near_x[h, d] for d in range(3)],
                [full_x[h, 3 + d] for d in range(3)],
                full_x[h, 6],
                (-float(CELL) if h == 0 else float(CELL), 0.0, 0.0),
                gates[1 if h == 0 else 0, part, :],
            )
            for slot, side, lift, face in ((5, 1, CELL, 2), (6, 0, -CELL, 3)):
                put_source(
                    bfeat, lfeat, slot, h,
                    [near_y[side, d, part, :] for d in range(3)],
                    [full_y[side, 3 + d, part, :] for d in range(3)],
                    full_y[side, 6, part, :],
                    (0.0, float(lift), 0.0),
                    gates[face, part, :],
                )
        lax.fori_loop(0, GROUPS // 2, outer_faces, 0)

        tot = []
        for q in range(7):
            rows = pl.ds(q, CELLS, stride=T_PITCH)
            tot.append(totals[rows, :] + totals_z[rows, :] + totals_x[rows, :])
        fill = state[6]
        x, y, z = (here[d] for d in range(3))
        speed = (
            tot[1] * z - tot[2] * y - tot[3],
            tot[2] * x - tot[0] * z - tot[4],
            tot[0] * y - tot[1] * x - tot[5],
        )
        for d in range(3):
            moved = here[d] + PACE * (DRIFT * speed[d] * fill)
            if step < STEPS - 1:
                places[step, d] = moved
            else:
                pos_out[d] = moved
                torque = tor_in[d]
                near_out[d] = (torque + COUPLE * (tot[d] - tot[6] * torque)) * fill

    me = row * COLS + col

    level = lax.broadcasted_iota(jnp.int32, (CELL, SLOT), 0).astype(F32) + 0.5
    low_lane = lax.broadcasted_iota(jnp.int32, (24, SLOT), 1) < 64

    gives = [pltpu.make_async_copy(src, out_far.at[k], field_sem.at[4 + k]) for k, src in enumerate((pos_out, near_out, spin))]
    for give in gives[0:2]:
        give.start()
    for table in tables:
        table.wait()

    def bins(d, cell):
        apart = pos_out[d, pl.ds(cell, 1), :] + MID - level
        return jnp.exp(-apart * apart)

    def spread(z, carry):
        planar, lifted, rest = [], [], []
        for h in range(2):
            cell = h * HALF + z
            bx, by, bz = (bins(d, cell) for d in range(3))
            depth[pl.ds(pl.multiple_of(cell * 8, 8), 8), :] = bz
            planar += [bx[a : a + 1, :] * by for a in range(CELL)]
            lift = [state[3 + c, pl.ds(cell, 1), :] * bz for c in range(3)]
            top = [narrow(v) for v in lift]
            lifted += top
            rest += [v - t for v, t in zip(lift, top)]
        ph, pl_ = cut(jnp.concatenate(planar, 0))
        plan_h[z] = ph
        plan_l[z] = pl_
        both = mul_t(jnp.concatenate(lifted + rest, 0).astype(BF16), ph)
        more = mul_t(jnp.concatenate(lifted, 0).astype(BF16), pl_)
        sums = both[0:48] + both[48:96] + more
        block = jnp.where(low_lane, sums[0:24], sums[24:48])
        for c in range(3):
            grid[c, pl.ds(pl.multiple_of(z * 8, 8), 8), :] = block[c * 8 : c * 8 + 8]
        return carry

    lax.fori_loop(0, HALF, spread, 0, unroll=16)

    def along_z(first, v):
        pair = table_left(z_tab[first : first + 2], jnp.concatenate(v[0:2], 1))
        return pair[:, 0:128], pair[:, 128:256], table_left(z_tab[first + 2 : first + 4], v[2])

    for c, v in enumerate(along_z(0, [grid[c] for c in range(3)])):
        out_1[pl.ds(c, DEVICES, stride=8), :] = v

    pl.semaphore_wait(tell.at[2], ROWS - 1)

    def exchange(out, into, k):
        def post(p):
            pltpu.make_async_remote_copy(
                src_ref=out.at[pl.ds(pl.multiple_of(p * 8, 8), 3), :],
                dst_ref=into.at[pl.ds(pl.multiple_of(me * 8, 8), 3), :],
                send_sem=all_send.at[k],
                recv_sem=all_recv.at[k],
                device_id=p,
                device_id_type=LOGICAL,
            ).start()

        layer, place = me // BUNCH // 4, lax.rem(me // BUNCH, 4)

        def post_bunch(i, carry):
            turn = i // 4
            target = layer + jnp.where(turn == 2, 3, jnp.where(turn == 3, 0, 2 - turn))
            target = jnp.where(target >= 4, target - 4, target)
            first = (target * 4 + (place + i) % 4) * BUNCH
            for n in range(BUNCH):
                post(first + n)
            return carry

        lax.fori_loop(0, 12, post_bunch, 0, unroll=6)
        lax.fori_loop(13, 16, post_bunch, 0, unroll=3)
        for n in range(1, BUNCH):
            post(me // BUNCH * BUNCH + lax.rem(me + n, BUNCH))
        mine = pl.ds(pl.multiple_of(me * 8, 8), 3)
        keep = pltpu.make_async_copy(out.at[mine, :], into.at[mine, :], self_sem.at[k])
        keep.start()
        keep.wait()
        bulk = out.at[pl.ds(0, 3 * (DEVICES - 1)), :]
        pltpu.make_async_copy(bulk, bulk, all_recv.at[k]).wait()

    exchange(out_1, in_1, 0)

    cos_t, sin_t = twist[0], twist[1]
    planes = jnp.concatenate([in_1[pl.ds(c, DEVICES, stride=8), :] for c in range(3)], 1)
    both = table_left(lf[...], planes)
    turned = []
    for c in range(3):
        re, im = both[0:128, c * 128 : c * 128 + 128], both[128:256, c * 128 : c * 128 + 128]
        turned.append(jnp.concatenate([re * cos_t + im * sin_t, im * cos_t - re * sin_t], 1))
    for c, v in enumerate(table_right(turned, rf)):
        work[c] = v

    special = me < 2
    plain = jnp.where(special, 1.0, 0.0).astype(F32)
    turn = jnp.where(special, 0, 2 * lax.rem(me, 2) - 1).astype(F32)
    kz = jnp.where(me == 1, -64, me // 2).astype(F32)
    kz_top = jnp.where(me == 1, -64, 0).astype(F32)
    kz_low = jnp.where(me == 1, 0, me // 2).astype(F32)

    def signed(v):
        return jnp.where(v < GRID // 2, v, v - GRID)

    def stokes(i, carry):
        rows = pl.ds(pl.multiple_of(i * 16, 16), 16)
        f1 = lax.broadcasted_iota(jnp.int32, (16, 128), 0) + i * 16
        f2 = lax.broadcasted_iota(jnp.int32, (16, 128), 1)
        ix = signed(f1 // 16 + 8 * (f2 // 8))
        iy = signed(f1 % 16 + 16 * (f2 % 8))
        kx, ky = ix.astype(F32), iy.astype(F32)
        kx_top = jnp.where(ix == -64, kx, 0.0)
        ky_top = jnp.where(iy == -64, ky, 0.0)
        kx_low, ky_low = kx - kx_top, ky - ky_top
        square = kx * kx + ky * ky + kz * kz
        damping = (0.25 / GRID**3) * jnp.exp(square * (-((math.pi / GRID) ** 2)))
        inverse = 1.0 / jnp.maximum(square, 1.0)
        w_re, w_im = work[2, rows, 0:128], work[2, rows, 128:256]
        sides = (
            (work[0, rows, 0:128], work[1, rows, 0:128], plain * w_re - turn * w_im),
            (work[0, rows, 128:256], work[1, rows, 128:256], plain * w_im + turn * w_re),
        )
        done = []
        for u, v, w in sides:
            low = (kx_low * u + ky_low * v + kz_low * w) * inverse
            top = (kx_top * u + ky_top * v + kz_top * w) * inverse
            done.append(
                (
                    damping * (u - kx_low * low - kx_top * top),
                    damping * (v - ky_low * low - ky_top * top),
                    damping * (w - kz_low * low - kz_top * top),
                )
            )
        for c in range(2):
            work[c, rows, 0:128] = done[0][c]
            work[c, rows, 128:256] = done[1][c]
        work[2, rows, 0:128] = plain * done[0][2] + turn * done[1][2]
        work[2, rows, 128:256] = plain * done[1][2] - turn * done[0][2]
        return carry

    lax.fori_loop(0, 8, stokes, 0, unroll=8)

    pairs = []
    for both in table_right([work[c] for c in range(3)], rb):
        re, im = both[:, 0:128], both[:, 128:256]
        pairs.append(jnp.concatenate([re * cos_t - im * sin_t, im * cos_t + re * sin_t], 0))
    planes = table_left(lb[...], jnp.concatenate(pairs, 1))
    for c in range(3):
        out_2[pl.ds(c, DEVICES, stride=8), :] = planes[:, c * 128 : c * 128 + 128]

    exchange(out_2, in_2, 1)

    for c, v in enumerate(along_z(4, [in_2[pl.ds(c, DEVICES, stride=8), :] for c in range(3)])):
        grid[c] = v

    def gather(z, carry):
        rows = pl.ds(pl.multiple_of(z * 8, 8), 8)
        block = jnp.concatenate([grid[c, rows, :] for c in range(3)], 0)
        near_half = jnp.where(low_lane, block, 0.0)
        far_half = block - near_half
        both = jnp.concatenate([near_half, far_half], 0)
        top = narrow(both)
        first = mul(jnp.concatenate([top, both - top], 0).astype(BF16), plan_h[z])
        second = mul(top.astype(BF16), plan_l[z])
        sums = first[0:48] + first[48:96] + second
        for h in range(2):
            spot = pl.ds(pl.multiple_of((h * HALF + z) * 8, 8), 8)
            bz = depth[spot, :]
            for c in range(3):
                far[c, spot, :] = sums[h * 24 + c * 8 : h * 24 + c * 8 + 8] * bz
        return carry

    lax.fori_loop(0, HALF, gather, 0, unroll=16)

    for c in range(3):
        total = far[c, pl.ds(0, CELLS, stride=8), :]
        for g in range(1, CELL):
            total = total + far[c, pl.ds(g, CELLS, stride=8), :]
        spin[c] = total * state[6]
    gives[2].start()

    for k in range(2):
        bulk = out_1.at[pl.ds(0, 3 * (DEVICES - 1)), :]
        pltpu.make_async_copy(bulk, bulk, all_send.at[k]).wait()
    for give in gives:
        give.wait()
    for step in range(STEPS):
        for copy in halo(step):
            copy.wait_send()
def shards(positions, torques, counts, neighbour_flags):
    shape = positions.shape
    flat = (3, CELLS, SLOT)
    tables = [jnp.asarray(t) for t in make_tables()]
    there = pl.BlockSpec(memory_space=pl.ANY)
    buffer = pltpu.VMEM((DEVICES * 8, 128), F32)
    out = pl.pallas_call(
        kernel,
        name="spinners",
        out_shape=jax.ShapeDtypeStruct((3,) + flat, F32),
        in_specs=[there] * (4 + len(tables)),
        out_specs=there,
        scratch_shapes=[
            pltpu.VMEM(flat, F32),
            pltpu.VMEM(flat, F32),
            pltpu.VMEM(flat, F32),
            pltpu.VMEM(flat, F32),
            pltpu.SMEM(counts.shape, jnp.int32),
            pltpu.SMEM(neighbour_flags.shape, jnp.int32),
            pltpu.SemaphoreType.DMA((7,)),
            pltpu.VMEM(flat, F32),
            pltpu.VMEM((7, CELLS, SLOT), F32),
            pltpu.VMEM((STEPS - 1, 3, CELLS, SLOT), F32),
            pltpu.VMEM((6, CELLS, SLOT), F32),
            pltpu.VMEM((CELLS * A_PITCH, SLOT), F32),
            pltpu.VMEM((CELLS // GROUP, SLOT, SLOT), BF16),
            pltpu.VMEM((7, CELLS * B_PITCH, SLOT), F32),
            pltpu.VMEM((7, CELLS * L_PITCH, SLOT), F32),
            pltpu.VMEM((CELLS * T_PITCH, SLOT), F32),
            pltpu.VMEM((CELLS * T_PITCH, SLOT), F32),
            pltpu.VMEM((CELLS * T_PITCH, SLOT), F32),
            pltpu.VMEM((2, 7, HALF, SLOT), F32),
            pltpu.VMEM((2, 7, CELLS, SLOT), F32),
            pltpu.VMEM((STEPS - 1, 2, 3, HALF, SLOT), F32),
            pltpu.VMEM((STEPS - 1, 2, 3, CELLS, SLOT), F32),
            pltpu.SemaphoreType.DMA((STEPS, 4)),
            pltpu.SemaphoreType.DMA((STEPS, 4)),
            pltpu.SemaphoreType.REGULAR((3,)),
        ]
        + [pltpu.VMEM(t.shape, t.dtype) for t in tables]
        + [
            pltpu.SemaphoreType.DMA((len(tables),)),
            pltpu.VMEM((3, GRID, 128), F32),
            pltpu.VMEM((HALF, 128, SLOT), BF16),
            pltpu.VMEM((HALF, 128, SLOT), BF16),
            pltpu.VMEM((CELLS * 8, SLOT), F32),
            buffer,
            buffer,
            buffer,
            buffer,
            pltpu.VMEM((3, 128, 256), F32),
            pltpu.VMEM((3, CELLS * 8, SLOT), F32),
            pltpu.SemaphoreType.DMA((2,)),
            pltpu.SemaphoreType.DMA((2,)),
            pltpu.SemaphoreType.DMA((2,)),
        ],
        compiler_params=pltpu.CompilerParams(collective_id=0, has_side_effects=True),
    )(positions.reshape(flat), torques.reshape(flat), counts, neighbour_flags, *tables)
    return (out[0] + MID).reshape(shape), (out[1] + out[2]).reshape(shape)


def solution(mesh):
    in_specs = (
        P(None, "row", "col", None, None),
        P(None, "row", "col", None, None),
        P("row", "col", None),
        P(None, "row", "col", None),
    )
    out_specs = (P(None, "row", "col", None, None), P(None, "row", "col", None, None))
    return jax.shard_map(shards, mesh=mesh, in_specs=in_specs, out_specs=out_specs, check_vma=False)
```
